32 devices in a mesh: dp: 8 (over y, x, core), mp: 4 (over z).
Axes of the slice: x: 2, y: 2, z: 4, core: 2. Of those that a mesh axis runs over, the one named last changes fastest.
Arguments:
- tokens_in: bfloat16 [8192, 2048], P('dp'), may hold values from -6 to 6
- cotangent: bfloat16 [8192, 2048], P('dp'), may hold values from -6 to 6
- segment_ids: int32 [8192], replicated, may hold values from 0 to 1, never falling along the last dimension, each value on 1 to 6144 neighbouring positions
- pad_mask: int32 [8192], replicated, may hold values from 0 to 1, as said below
- qk_proj: float32 [2048, 2, 16, 128], P('dp', None, 'mp'), may hold values from -0.125 to 0.125
- qk_proj_first: float32 [2048, 2, 16, 128], P('dp', None, 'mp'), may hold values from -6 to 6
- qk_proj_second: float32 [2048, 2, 16, 128], P('dp', None, 'mp'), may hold values from 0.08192 to 0.32768
- vg_proj: float32 [2048, 2, 16, 256], P('dp', None, 'mp'), may hold values from -0.125 to 0.125
- vg_proj_first: float32 [2048, 2, 16, 256], P('dp', None, 'mp'), may hold values from -12 to 12
- vg_proj_second: float32 [2048, 2, 16, 256], P('dp', None, 'mp'), may hold values from 0.32768 to 1.31072
- ab_proj: float32 [2048, 2, 16], P('dp', None, 'mp'), may hold values from -0.125 to 0.125
- ab_proj_first: float32 [2048, 2, 16], P('dp', None, 'mp'), may hold values from -16 to 16
- ab_proj_second: float32 [2048, 2, 16], P('dp', None, 'mp'), may hold values from 0.73728 to 2.94912
- out_proj: float32 [16, 256, 2048], P('mp', None, 'dp'), may hold values from -0.125 to 0.125
- out_proj_first: float32 [16, 256, 2048], P('mp', None, 'dp'), may hold values from -32 to 32
- out_proj_second: float32 [16, 256, 2048], P('mp', None, 'dp'), may hold values from 2.048 to 8.192
- gu_proj: float32 [2048, 2, 5632], P('dp', None, 'mp'), may hold values from -0.125 to 0.125
- gu_proj_first: float32 [2048, 2, 5632], P('dp', None, 'mp'), may hold values from -16 to 16
- gu_proj_second: float32 [2048, 2, 5632], P('dp', None, 'mp'), may hold values from 0.73728 to 2.94912
- down_proj: float32 [5632, 2048], P('mp', 'dp'), may hold values from -0.109375 to 0.109375
- down_proj_first: float32 [5632, 2048], P('mp', 'dp'), may hold values from -32 to 32
- down_proj_second: float32 [5632, 2048], P('mp', 'dp'), may hold values from 2.048 to 8.192
- norm_gains: float32 [2, 2048], P(None, 'dp'), may hold values from 0.5 to 1.5
- norm_gains_first: float32 [2, 2048], P(None, 'dp'), may hold values from -40 to 40
- norm_gains_second: float32 [2, 2048], P(None, 'dp'), may hold values from 4.01408 to 16.05632
- qk_conv: float32 [2, 4, 16, 128], P(None, None, 'mp', 'dp'), may hold values from -2.5 to 2.5
- qk_conv_first: float32 [2, 4, 16, 128], P(None, None, 'mp', 'dp'), may hold values from -16 to 16
- qk_conv_second: float32 [2, 4, 16, 128], P(None, None, 'mp', 'dp'), may hold values from 0.73728 to 2.94912
- v_conv: float32 [4, 16, 256], P(None, 'mp', 'dp'), may hold values from -2.5 to 2.5
- v_conv_first: float32 [4, 16, 256], P(None, 'mp', 'dp'), may hold values from -16 to 16
- v_conv_second: float32 [4, 16, 256], P(None, 'mp', 'dp'), may hold values from 0.73728 to 2.94912
- out_gain: float32 [256], P('dp'), may hold values from 0.5 to 1.5
- out_gain_first: float32 [256], P('dp'), may hold values from -64 to 64
- out_gain_second: float32 [256], P('dp'), may hold values from 11.79648 to 47.18592
- decay_params: float32 [2, 16], P(None, 'mp'), may hold values from -9 to 1
- decay_params_first: float32 [2, 16], P(None, 'mp'), may hold values from -16 to 16
- decay_params_second: float32 [2, 16], P(None, 'mp'), may hold values from 0.73728 to 2.94912
Outputs:
- block_out: bfloat16 [8192, 2048], P('dp')
- input_grad: float32 [8192, 2048], P('dp')
- qk_proj_next: float32 [2048, 2, 16, 128], P('dp', None, 'mp')
- qk_proj_first_next: float32 [2048, 2, 16, 128], P('dp', None, 'mp')
- qk_proj_second_next: float32 [2048, 2, 16, 128], P('dp', None, 'mp')
- vg_proj_next: float32 [2048, 2, 16, 256], P('dp', None, 'mp')
- vg_proj_first_next: float32 [2048, 2, 16, 256], P('dp', None, 'mp')
- vg_proj_second_next: float32 [2048, 2, 16, 256], P('dp', None, 'mp')
- ab_proj_next: float32 [2048, 2, 16], P('dp', None, 'mp')
- ab_proj_first_next: float32 [2048, 2, 16], P('dp', None, 'mp')
- ab_proj_second_next: float32 [2048, 2, 16], P('dp', None, 'mp')
- out_proj_next: float32 [16, 256, 2048], P('mp', None, 'dp')
- out_proj_first_next: float32 [16, 256, 2048], P('mp', None, 'dp')
- out_proj_second_next: float32 [16, 256, 2048], P('mp', None, 'dp')
- gu_proj_next: float32 [2048, 2, 5632], P('dp', None, 'mp')
- gu_proj_first_next: float32 [2048, 2, 5632], P('dp', None, 'mp')
- gu_proj_second_next: float32 [2048, 2, 5632], P('dp', None, 'mp')
- down_proj_next: float32 [5632, 2048], P('mp', 'dp')
- down_proj_first_next: float32 [5632, 2048], P('mp', 'dp')
- down_proj_second_next: float32 [5632, 2048], P('mp', 'dp')
- norm_gains_next: float32 [2, 2048], P(None, 'dp')
- norm_gains_first_next: float32 [2, 2048], P(None, 'dp')
- norm_gains_second_next: float32 [2, 2048], P(None, 'dp')
- qk_conv_next: float32 [2, 4, 16, 128], P(None, None, 'mp', 'dp')
- qk_conv_first_next: float32 [2, 4, 16, 128], P(None, None, 'mp', 'dp')
- qk_conv_second_next: float32 [2, 4, 16, 128], P(None, None, 'mp', 'dp')
- v_conv_next: float32 [4, 16, 256], P(None, 'mp', 'dp')
- v_conv_first_next: float32 [4, 16, 256], P(None, 'mp', 'dp')
- v_conv_second_next: float32 [4, 16, 256], P(None, 'mp', 'dp')
- out_gain_next: float32 [256], P('dp')
- out_gain_first_next: float32 [256], P('dp')
- out_gain_second_next: float32 [256], P('dp')
- decay_params_next: float32 [2, 16], P(None, 'mp')
- decay_params_first_next: float32 [2, 16], P(None, 'mp')
- decay_params_second_next: float32 [2, 16], P(None, 'mp')
- qk_proj_copy: bfloat16 [2048, 2, 16, 128], P('dp', None, 'mp')
- vg_proj_copy: bfloat16 [2048, 2, 16, 256], P('dp', None, 'mp')
- ab_proj_copy: bfloat16 [2048, 2, 16], P('dp', None, 'mp')
- out_proj_copy: bfloat16 [16, 256, 2048], P('mp', None, 'dp')
- gu_proj_copy: bfloat16 [2048, 2, 5632], P('dp', None, 'mp')
- down_proj_copy: bfloat16 [5632, 2048], P('mp', 'dp')
The draws below stay inside these ranges and needn't reach their ends.
Inputs may be any that keep to these rules, and one draw needn't show every extreme that they name: `segment_ids`: item numbers never fall along the packed sequence; there are two items, each of 2048 to 6144 tokens. `pad_mask`: the zeros, 1 to 1023 of them, are the sequence's last tokens.
All inputs are finite; a program needn't handle non-finite values.
Results may differ from the reference program's by a relative error of at most 0.028.
The reference program's roundings to bfloat16 on the way count: a program that leaves them out, or rounds other values in their place, can miss the bound.
Values may be sent and summed in bfloat16 or wider, within the bound.
A program may use at most 320 MiB of HBM per device.

```python
import math
import jax
import jax.numpy as jnp
import numpy as np
from jax import lax

D = 2048
H = 16
KEY = 128
VAL = 256
FF = 5632
CONV = 4
BLOCK = 64
TOKENS = 8192
ROW_LEN = 8192


def draw_pad_mask(key, part):
    row_count = TOKENS // ROW_LEN
    padding = jax.random.randint(key, (row_count,), 1, ROW_LEN // 8)
    places = jnp.arange(TOKENS, dtype=jnp.int32)
    row_of = places // ROW_LEN
    within = places % ROW_LEN
    limit = ROW_LEN - jnp.take(padding, row_of)
    return (within < limit).astype(jnp.int32)


def draw_decay_params(key, part):
    first_key, second_key = jax.random.split(jax.random.fold_in(key, 7))
    log_rates = jax.random.uniform(first_key, (H,), jnp.float32, -9.0, -2.5)
    offsets = jax.random.uniform(second_key, (H,), jnp.float32, -1.0, 1.0)
    return jnp.stack([log_rates, offsets])


def levels(own_key, extent, cuts, low, high):
    def one(axis_at, shards_of):
        heights = jax.random.uniform(jax.random.fold_in(jax.random.fold_in(own_key, 6), axis_at), (shards_of,), jnp.float32, low / len(cuts), high / len(cuts))
        return jnp.repeat(jnp.exp(heights), extent[axis_at] // shards_of).reshape((-1,) + (1,) * (len(extent) - axis_at - 1))

    level = one(*cuts[0])
    for cut in cuts[1:]:
        level = level * one(*cut)
    return level


def split_up(amount, total, bound, skew):
    loads = [(1 << 20) // math.isqrt(standing ** skew) + 1 for standing in range(2, amount + 1)]
    rest, holding = total - bound - (amount - 1), [1] * (amount - 1)
    while rest > 0:
        movable = [i for i in range(amount - 1) if holding[i] < bound]
        whole, remaining = sum([loads[i] for i in movable]), rest
        for i in movable:
            extra = min(bound - holding[i], max(1, remaining * loads[i] // whole), rest)
            holding[i] = holding[i] + extra
            rest = rest - extra
    return np.array([bound] + holding)


def uneven(key, count, total, most, skew):
    if count == 2:
        one = jax.random.randint(key, (), max(1, total - most), min(most, total - 1) + 1)
        return jnp.stack([one, total - one])
    tallies = jnp.asarray(split_up(count, total, most, skew), jnp.int32)
    pairs = (count - 1) // 2
    source_of, receiver = tallies[1:1 + 2 * pairs:2], tallies[2:2 + 2 * pairs:2]
    room = jnp.minimum(source_of - 1, most - receiver)
    moved = jax.random.randint(jax.random.fold_in(key, 1), (pairs,), 0, 1 << 20) % (room + 1)
    tallies = tallies.at[1:1 + 2 * pairs:2].set(source_of - moved).at[2:2 + 2 * pairs:2].set(receiver + moved)
    return tallies[jax.random.permutation(jax.random.fold_in(key, 2), count)]


def noise(own_key, extent, scale, most, shards=(), kind=jnp.bfloat16):
    values = jax.random.normal(own_key, extent, jnp.float32) * scale
    if len(shards) > 0:
        values = levels(own_key, extent, shards, -0.22, 0.18) * values
    return jnp.clip(values, min=-most, max=most).astype(kind)


def setup_inputs(seed: int = 0) -> dict:
    streams_of = jax.random.split(jax.random.key(seed), 38)
    return {
        "tokens_in": noise(streams_of[0], (TOKENS, D), 1.0, 6.0, ((0, 8),)),
        "cotangent": noise(streams_of[1], (TOKENS, D), 1.0, 6.0, ((0, 8),)),
        "segment_ids": jnp.searchsorted(jnp.cumsum(uneven(streams_of[2], 2, TOKENS, 3 * TOKENS // 4, 1)), jnp.arange(TOKENS), side="right").astype(jnp.int32),
        "pad_mask": draw_pad_mask(jax.random.fold_in(streams_of[37], 71), 0),
        "qk_proj": noise(streams_of[4], (D, 2, H, KEY), D ** -0.5, 0.125, ((0, 8), (2, 4)), jnp.float32),
        "qk_proj_first": noise(streams_of[5], (D, 2, H, KEY), (0.011 * TOKENS ** 0.5), 6.0, ((0, 8), (2, 4)), jnp.float32),
        "qk_proj_second": jnp.clip(0.08192 + 0.24576 * jax.random.uniform(streams_of[6], (D, 2, H, KEY), jnp.float32) ** levels(streams_of[6], (D, 2, H, KEY), ((0, 8), (2, 4)), -0.2, 0.2), 0.08192, 0.32768),
        "vg_proj": noise(streams_of[7], (D, 2, H, VAL), D ** -0.5, 0.125, ((0, 8), (2, 4)), jnp.float32),
        "vg_proj_first": noise(streams_of[8], (D, 2, H, VAL), (0.022 * TOKENS ** 0.5), 12.0, ((0, 8), (2, 4)), jnp.float32),
        "vg_proj_second": jnp.clip(0.32768 + 0.98304 * jax.random.uniform(streams_of[9], (D, 2, H, VAL), jnp.float32) ** levels(streams_of[9], (D, 2, H, VAL), ((0, 8), (2, 4)), -0.2, 0.2), 0.32768, 1.31072),
        "ab_proj": noise(streams_of[10], (D, 2, H), D ** -0.5, 0.125, ((0, 8), (2, 4)), jnp.float32),
        "ab_proj_first": noise(streams_of[11], (D, 2, H), (0.033 * TOKENS ** 0.5), 16.0, ((0, 8), (2, 4)), jnp.float32),
        "ab_proj_second": jnp.clip(0.73728 + 2.211840033531189 * jax.random.uniform(streams_of[12], (D, 2, H), jnp.float32) ** levels(streams_of[12], (D, 2, H), ((0, 8), (2, 4)), -0.2, 0.2), 0.73728, 2.94912),
        "out_proj": noise(streams_of[13], (H, VAL, D), (H * VAL // 2) ** -0.5, 0.125, ((0, 4), (2, 8)), jnp.float32),
        "out_proj_first": noise(streams_of[14], (H, VAL, D), (0.055 * TOKENS ** 0.5), 32.0, ((0, 4), (2, 8)), jnp.float32),
        "out_proj_second": jnp.clip(2.048 + 6.144 * jax.random.uniform(streams_of[15], (H, VAL, D), jnp.float32) ** levels(streams_of[15], (H, VAL, D), ((0, 4), (2, 8)), -0.2, 0.2), 2.048, 8.192),
        "gu_proj": noise(streams_of[16], (D, 2, FF), D ** -0.5, 0.125, ((0, 8), (2, 4)), jnp.float32),
        "gu_proj_first": noise(streams_of[17], (D, 2, FF), (0.033 * TOKENS ** 0.5), 16.0, ((0, 8), (2, 4)), jnp.float32),
        "gu_proj_second": jnp.clip(0.73728 + 2.211840033531189 * jax.random.uniform(streams_of[18], (D, 2, FF), jnp.float32) ** levels(streams_of[18], (D, 2, FF), ((0, 8), (2, 4)), -0.2, 0.2), 0.73728, 2.94912),
        "down_proj": noise(streams_of[19], (FF, D), (FF // 2) ** -0.5, 0.109375, ((0, 4), (1, 8)), jnp.float32),
        "down_proj_first": noise(streams_of[20], (FF, D), (0.055 * TOKENS ** 0.5), 32.0, ((0, 4), (1, 8)), jnp.float32),
        "down_proj_second": jnp.clip(2.048 + 6.144 * jax.random.uniform(streams_of[21], (FF, D), jnp.float32) ** levels(streams_of[21], (FF, D), ((0, 4), (1, 8)), -0.2, 0.2), 2.048, 8.192),
        "norm_gains": jnp.clip(1.0 + 0.1 * jax.random.normal(streams_of[22], (2, D), jnp.float32), 0.5, 1.5),
        "norm_gains_first": noise(streams_of[23], (2, D), (0.077 * TOKENS ** 0.5), 40.0, ((1, 8),), jnp.float32),
        "norm_gains_second": jnp.clip(4.01408 + 12.04224 * jax.random.uniform(streams_of[24], (2, D), jnp.float32) ** levels(streams_of[24], (2, D), ((1, 8),), -0.2, 0.2), 4.01408, 16.05632),
        "qk_conv": noise(streams_of[25], (2, CONV, H, KEY), 0.5, 2.5, ((2, 4), (3, 8)), jnp.float32),
        "qk_conv_first": noise(streams_of[26], (2, CONV, H, KEY), (0.033 * TOKENS ** 0.5), 16.0, ((2, 4), (3, 8)), jnp.float32),
        "qk_conv_second": jnp.clip(0.73728 + 2.211840033531189 * jax.random.uniform(streams_of[27], (2, CONV, H, KEY), jnp.float32) ** levels(streams_of[27], (2, CONV, H, KEY), ((2, 4), (3, 8)), -0.2, 0.2), 0.73728, 2.94912),
        "v_conv": noise(streams_of[28], (CONV, H, VAL), 0.5, 2.5, ((1, 4), (2, 8)), jnp.float32),
        "v_conv_first": noise(streams_of[29], (CONV, H, VAL), (0.033 * TOKENS ** 0.5), 16.0, ((1, 4), (2, 8)), jnp.float32),
        "v_conv_second": jnp.clip(0.73728 + 2.211840033531189 * jax.random.uniform(streams_of[30], (CONV, H, VAL), jnp.float32) ** levels(streams_of[30], (CONV, H, VAL), ((1, 4), (2, 8)), -0.2, 0.2), 0.73728, 2.94912),
        "out_gain": jnp.clip(1.0 + 0.1 * jax.random.normal(streams_of[31], (VAL,), jnp.float32), 0.5, 1.5),
        "out_gain_first": noise(streams_of[32], (VAL,), (0.13 * TOKENS ** 0.5), 64.0, ((0, 8),), jnp.float32),
        "out_gain_second": jnp.clip(11.79648 + 35.389441 * jax.random.uniform(streams_of[33], (VAL,), jnp.float32) ** levels(streams_of[33], (VAL,), ((0, 8),), -0.2, 0.2), 11.79648, 47.18592),
        "decay_params": draw_decay_params(jax.random.fold_in(streams_of[37], 71), 0),
        "decay_params_first": noise(streams_of[35], (2, H), (0.033 * TOKENS ** 0.5), 16.0, ((1, 4),), jnp.float32),
        "decay_params_second": jnp.clip(0.73728 + 2.211840033531189 * jax.random.uniform(streams_of[36], (2, H), jnp.float32) ** levels(streams_of[36], (2, H), ((1, 4),), -0.2, 0.2), 0.73728, 2.94912),
    }


PRECISION_TOP = lax.Precision.HIGHEST
adam_step = 10.0

@jax.custom_vjp
def low(v):
    return lax.optimization_barrier(v.astype(jnp.bfloat16)).astype(jnp.float32)

@jax.custom_vjp
def low_back(v):
    return v

def low_keep(v):
    return (low(v), None)

def low_pass(kept, grad):
    return (grad,)

def back_keep(v):
    return (v, None)

def back_low(kept, grad):
    return (low(grad),)
low.defvjp(low_keep, low_pass)
low_back.defvjp(back_keep, back_low)

def norm_rows(values, gain):
    return values * lax.rsqrt(lax.optimization_barrier(jnp.mean(values * values, axis=-1, keepdims=True)) + 1e-06) * gain

def resets_of(segment_ids):
    places = jnp.arange(segment_ids.shape[0], dtype=jnp.int32)
    previous = jnp.concatenate([jnp.full((1,), -1, jnp.int32), segment_ids[:-1]])
    flags = (segment_ids != previous) | (places % ROW_LEN == 0)
    return flags.astype(jnp.float32)

def causal_conv(values, taps, resets):
    keep = 1.0 - resets
    count = values.shape[0]
    total = values * taps[CONV - 1]
    valid = jnp.ones_like(keep)
    for lag in range(1, CONV):
        valid = valid * jnp.concatenate([jnp.ones((lag - 1,), jnp.float32), keep[:count - lag + 1]])
        moved = jnp.concatenate([jnp.zeros((lag,) + values.shape[1:], jnp.float32), values[:count - lag]])
        total = total + moved * taps[CONV - 1 - lag] * valid[:, None, None]
    return total

def unit_rows(values):
    return values * lax.rsqrt(lax.optimization_barrier(jnp.sum(values * values, axis=-1, keepdims=True)) + 1e-06)

def token_step(memory_states, inputs):
    query_vector, current_key, current_value, decay_log, beta_strength, reset = inputs
    memory_states = memory_states * ((1.0 - reset) * jnp.exp(decay_log))[:, None, None]
    retrieved_value = jnp.einsum('io,iof->if', current_key, memory_states, precision=PRECISION_TOP)
    memory_states = memory_states + jnp.einsum('au,ag->aug', current_key, beta_strength[:, None] * (current_value - retrieved_value), precision=PRECISION_TOP)
    return (memory_states, jnp.einsum('io,iof->if', query_vector, memory_states, precision=PRECISION_TOP))

def block_steps(memory_states, inputs):
    return lax.scan(token_step, memory_states, inputs)

def recurrence(query_vector, key_rows, values, decay_log, beta_strength, resets):
    count = query_vector.shape[0] // BLOCK

    def split(array):
        return array.reshape((count, BLOCK) + array.shape[1:])
    start = jnp.zeros((H, KEY, VAL), jnp.float32)
    final, outputs = lax.scan(jax.checkpoint(block_steps), start, (split(query_vector), split(key_rows), split(values), split(decay_log), split(beta_strength), split(resets)))
    return outputs.reshape((count * BLOCK,) + outputs.shape[2:])

def block_forward(x_float, qk_proj, vg_proj, ab_proj, out_proj, gu_proj, down_proj, norm_gains, qk_conv, v_conv, out_gain, decay_params, resets, pad):
    normed = low(norm_rows(x_float, norm_gains[0]))
    pre_qk = low_back(low(jnp.einsum('td,dshk->tshk', normed, qk_proj, precision=PRECISION_TOP)))
    both = jnp.einsum('td,dshv->tshv', normed, vg_proj, precision=PRECISION_TOP)
    pre_v = low_back(low(both[:, 0]))
    gate_pre = low_back(both[:, 1])
    mixed_ab = low_back(jnp.einsum('td,dsh->tsh', normed, ab_proj, precision=PRECISION_TOP))
    query_vector = unit_rows(jax.nn.silu(causal_conv(pre_qk[:, 0], qk_conv[0], resets))) * KEY ** (-0.5)
    key_rows = unit_rows(jax.nn.silu(causal_conv(pre_qk[:, 1], qk_conv[1], resets)))
    values = jax.nn.silu(causal_conv(pre_v, v_conv, resets))
    decay_log = -jnp.exp(decay_params[0]) * jax.nn.softplus(mixed_ab[:, 0] + decay_params[1]) * pad[:, None]
    beta_strength = jax.nn.sigmoid(mixed_ab[:, 1]) * pad[:, None]
    read_out = recurrence(query_vector, key_rows, values, decay_log, beta_strength, resets)
    gated = read_out * lax.rsqrt(lax.optimization_barrier(jnp.mean(read_out * read_out, axis=-1, keepdims=True)) + 1e-05) * out_gain * jax.nn.silu(gate_pre) * pad[:, None, None]
    mixer_out = low(gated)
    attn = low_back(jnp.einsum('thv,hvd->td', mixer_out, out_proj, precision=PRECISION_TOP))
    hidden = x_float + attn
    normed_two = low(norm_rows(hidden, norm_gains[1]))
    gate_up = low_back(jnp.einsum('td,dsf->tsf', normed_two, gu_proj, precision=PRECISION_TOP))
    activated = low(jax.nn.silu(gate_up[:, 0]) * gate_up[:, 1])
    down = low_back(jnp.dot(activated, down_proj, precision=PRECISION_TOP))
    return hidden + down

def adamw(weight, grad, first, second, rate, shrink):
    first = 0.9 * first + 0.1 * grad
    second = 0.999 * second + 0.001 * grad * grad
    first_hat = first / (1.0 - 0.9 ** adam_step)
    second_hat = second / (1.0 - 0.999 ** adam_step)
    weight = weight - rate * (first_hat / (jnp.sqrt(second_hat) + 1e-08) + shrink * weight)
    return [weight, first, second]

def reference(tokens_in, cotangent, segment_ids, pad_mask, qk_proj, qk_proj_first, qk_proj_second, vg_proj, vg_proj_first, vg_proj_second, ab_proj, ab_proj_first, ab_proj_second, out_proj, out_proj_first, out_proj_second, gu_proj, gu_proj_first, gu_proj_second, down_proj, down_proj_first, down_proj_second, norm_gains, norm_gains_first, norm_gains_second, qk_conv, qk_conv_first, qk_conv_second, v_conv, v_conv_first, v_conv_second, out_gain, out_gain_first, out_gain_second, decay_params, decay_params_first, decay_params_second):
    resets = resets_of(segment_ids)
    pad = pad_mask.astype(jnp.float32)
    masters = [qk_proj, vg_proj, ab_proj, out_proj, gu_proj, down_proj, norm_gains, qk_conv, v_conv, out_gain, decay_params]
    firsts = [qk_proj_first, vg_proj_first, ab_proj_first, out_proj_first, gu_proj_first, down_proj_first, norm_gains_first, qk_conv_first, v_conv_first, out_gain_first, decay_params_first]
    seconds = [qk_proj_second, vg_proj_second, ab_proj_second, out_proj_second, gu_proj_second, down_proj_second, norm_gains_second, qk_conv_second, v_conv_second, out_gain_second, decay_params_second]
    rounded = [lax.optimization_barrier(weight.astype(jnp.bfloat16)).astype(jnp.float32) for weight in masters]

    def forward(x_float, *weights):
        return block_forward(x_float, *weights, resets, pad)
    output, pull = jax.vjp(forward, tokens_in.astype(jnp.float32), *rounded)
    grads = pull(cotangent.astype(jnp.float32))
    matrix_rate = 2.5 * D ** (-0.5)
    rates = [matrix_rate] * 6 + [0.5, 1.0, 1.0, 0.5, 2.0]
    shrinks = [0.1] * 6 + [0.0] * 5
    updates = []
    for index in range(11):
        updates = updates + adamw(masters[index], grads[index + 1], firsts[index], seconds[index], rates[index], shrinks[index])
    copies = [updates[3 * index].astype(jnp.bfloat16) for index in range(6)]
    return (output.astype(jnp.bfloat16), grads[0], updates[0], updates[1], updates[2], updates[3], updates[4], updates[5], updates[6], updates[7], updates[8], updates[9], updates[10], updates[11], updates[12], updates[13], updates[14], updates[15], updates[16], updates[17], updates[18], updates[19], updates[20], updates[21], updates[22], updates[23], updates[24], updates[25], updates[26], updates[27], updates[28], updates[29], updates[30], updates[31], updates[32], copies[0], copies[1], copies[2], copies[3], copies[4], copies[5])
```

```python
from functools import partial

import jax
import jax.numpy as jnp
from jax import lax
from jax.experimental import pallas as pl
from jax.experimental.pallas import tpu as pltpu
from jax.sharding import PartitionSpec as P

D = 2048
CONV = 4
SPAN = CONV - 1
CH = 128
HALO = 8
f32 = jnp.float32
bf16 = jnp.bfloat16
VLIM = 56 * 2**20

NN = (((1,), (0,)), ((), ()))
NT = (((1,), (1,)), ((), ()))
TN = (((0,), (0,)), ((), ()))

N_INV = 3
N_FWD = 1
N_SCAN = 1
N_BWD = 1


def mm(a, b, dims=NN, passes=1):
    def dot(x, y):
        return lax.dot_general(x, y, dims, preferred_element_type=f32)

    ah, bh = a.astype(bf16), b.astype(bf16)
    out = dot(ah, bh)
    if passes == 3:
        al = (a - ah.astype(f32)).astype(bf16)
        bl = (b - bh.astype(f32)).astype(bf16)
        out = out + (dot(ah, bl) + dot(al, bh))
    return out


def grid_iotas(n):
    return (
        lax.broadcasted_iota(jnp.int32, (n, n), 0),
        lax.broadcasted_iota(jnp.int32, (n, n), 1),
    )


def unit_lower_inverse(lowers, n):
    rows, cols = grid_iotas(n)
    eye = (rows == cols).astype(f32)
    small = lax.shift_right_logical(rows, 3) == lax.shift_right_logical(cols, 3)
    diag = [jnp.where(small, low, 0.0) for low in lowers]
    two = [mm(d, d, NN, N_INV) for d in diag]
    four = [mm(t, t, NN, N_INV) for t in two]
    inv = [eye - d for d in diag]
    inv = [x + mm(x, t, NN, N_INV) for x, t in zip(inv, two)]
    inv = [x + mm(x, f, NN, N_INV) for x, f in zip(inv, four)]
    bits = 3
    while (1 << bits) < n:
        wide = lax.shift_right_logical(rows, bits + 1) == lax.shift_right_logical(cols, bits + 1)
        fine = lax.shift_right_logical(rows, bits) != lax.shift_right_logical(cols, bits)
        off = [jnp.where(wide & fine, low, 0.0) for low in lowers]
        half = [mm(x, o, NN, N_INV) for x, o in zip(inv, off)]
        inv = [x - mm(y, x, NN, N_INV) for x, y in zip(inv, half)]
        bits += 1
    return inv


def sigmoid(x):
    return 1.0 / (1.0 + jnp.exp(-x))


def decay_matrix(aux, rows, h, heads, tri):
    cg = aux[:, 5 + h : 6 + h]
    cg_row = rows[1 + h : 2 + h, :]
    same = (aux[:, 4:5] == rows[0:1, :]) & tri
    return jnp.where(same, jnp.exp(jnp.where(same, cg - cg_row, 0.0)), 0.0)


def conv_of(ext_ref, taps_ref, aux, c0, c1):
    n = aux.shape[0]
    total = ext_ref[HALO : HALO + n, c0:c1] * taps_ref[SPAN : SPAN + 1, c0:c1]
    for lag in range(1, SPAN + 1):
        total = total + ext_ref[HALO - lag : HALO - lag + n, c0:c1] * (
            taps_ref[SPAN - lag : SPAN - lag + 1, c0:c1] * aux[:, lag - 1 : lag]
        )
    return total


def unit_of(act):
    return lax.rsqrt(jnp.sum(act * act, axis=-1, keepdims=True) + 1e-06)


def kernel_a(heads, key, val, pqk, pv, hqk, hv, tqk, tv, aux_ref, rows_ref,
             q_out, k_out, w_out, u_out, p_out, t_out, r_out, rend_out,
             xqk, xv, state):
    c = pl.program_id(0)
    n = pqk.shape[0]
    hk = heads * key

    @pl.when(c == 0)
    def _():
        xqk[0:HALO, :] = hqk[...]
        xv[0:HALO, :] = hv[...]
        r, s = (lax.broadcasted_iota(jnp.int32, (key, key + val), i) for i in (0, 1))
        for h in range(heads):
            state[h] = (r == s).astype(f32)

    xqk[HALO:, :] = pqk[...].astype(f32)
    xv[HALO:, :] = pv[...].astype(f32)
    aux = aux_ref[...]
    rows = rows_ref[0]
    ti, si = grid_iotas(n)
    tri = ti >= si
    lowers, queries, keys = [], [], []
    for h in range(heads):
        uq = conv_of(xqk, tqk, aux, h * key, (h + 1) * key)
        uk = conv_of(xqk, tqk, aux, hk + h * key, hk + (h + 1) * key)
        aq = uq * sigmoid(uq)
        ak = uk * sigmoid(uk)
        q = aq * unit_of(aq) * key ** (-0.5)
        k = ak * unit_of(ak)
        q_out[:, h * key : (h + 1) * key] = q
        k_out[:, h * key : (h + 1) * key] = k
        dec = decay_matrix(aux, rows, h, heads, tri)
        beta = aux[:, 5 + 3 * heads + h : 6 + 3 * heads + h]
        p_out[:, h * n : (h + 1) * n] = mm(q, k, NT, N_FWD) * dec
        lowers.append(jnp.where(ti > si, mm(k, k, NT, N_INV) * dec, 0.0) * beta)
        queries.append(q)
        keys.append(k)
    invs = unit_lower_inverse(lowers, n)
    for h in range(heads):
        k = keys[h]
        beta = aux[:, 5 + 3 * heads + h : 6 + 3 * heads + h]
        fs = aux[:, 5 + heads + h : 6 + heads + h]
        lr = aux[:, 5 + 2 * heads + h : 6 + 2 * heads + h]
        uv = conv_of(xv, tv, aux, h * val, (h + 1) * val)
        v = uv * sigmoid(uv)
        t_out[:, h * n : (h + 1) * n] = invs[h]
        w = mm(invs[h], (beta * fs) * k, NN, N_FWD)
        u = mm(invs[h], beta * v, NN, N_FWD)
        w_out[:, h * key : (h + 1) * key] = w
        u_out[:, h * val : (h + 1) * val] = u
        st = state[h]
        r_out[0, h] = st
        new = jnp.concatenate([jnp.zeros((n, key), f32), u], axis=1) - mm(w, st, NN, N_SCAN)
        st = fs[n - 1 :, :] * st + mm(lr * k, new, TN, N_SCAN)
        state[h] = st
        rend_out[h] = st
    xqk[0:HALO, :] = xqk[n:, :]
    xv[0:HALO, :] = xv[n:, :]


def kernel_b(heads, key, val, mine, gath, r_in, w_in, u_in, p_in, q_in, aux_ref, gate_in, gain_ref,
             y_out, s_out, vn_out, o_out, start):
    c = pl.program_id(0)
    n = w_in.shape[0]

    @pl.when(c == 0)
    def _():
        start[...] = jnp.zeros_like(start)

        @pl.loop(0, mine[0])
        def _(d):
            for h in range(heads):
                start[h] = gath[d, h, :, key:].astype(f32) + mm(gath[d, h, :, :key], start[h], NN, N_FWD)

    aux = aux_ref[...]
    pad = aux[:, 3:4]
    for h in range(heads):
        fs = aux[:, 5 + heads + h : 6 + heads + h]
        st = r_in[0, h, :, key:] + mm(r_in[0, h, :, :key], start[h], NN, N_FWD)
        s_out[0, h] = st
        v0, v1 = h * val, (h + 1) * val
        new = u_in[:, v0:v1] - mm(w_in[:, h * key : (h + 1) * key], st, NN, N_FWD)
        vn_out[:, v0:v1] = new
        o = mm(fs * q_in[:, h * key : (h + 1) * key], st, NN, N_FWD)
        o = o + mm(p_in[:, h * n : (h + 1) * n], new, NN, N_FWD)
        o_out[:, v0:v1] = o
        scale = lax.rsqrt(jnp.mean(o * o, axis=-1, keepdims=True) + 1e-05)
        gate = gate_in[:, v0:v1]
        y = o * scale * gain_ref[0:1, :] * (gate * sigmoid(gate)) * pad
        y_out[:, v0:v1] = y.astype(bf16)


def kernel_c(heads, key, val, dy_in, o_in, gate_in, gain_ref, aux_ref, q_in, k_in, w_in, p_in,
             do_out, dgate_out, dgain_out, z_out, zend_out, carry):
    c = pl.program_id(0)
    n = dy_in.shape[0]

    @pl.when(c == 0)
    def _():
        r, s = (lax.broadcasted_iota(jnp.int32, (key, key + val), i) for i in (0, 1))
        for h in range(heads):
            carry[h] = (r == s).astype(f32)
        dgain_out[...] = jnp.zeros_like(dgain_out)

    aux = aux_ref[...]
    pad = aux[:, 3:4]
    gain = gain_ref[0:1, :]
    for h in range(heads):
        v0, v1 = h * val, (h + 1) * val
        k0, k1 = h * key, (h + 1) * key
        fs = aux[:, 5 + heads + h : 6 + heads + h]
        lr = aux[:, 5 + 2 * heads + h : 6 + 2 * heads + h]
        o = o_in[:, v0:v1]
        gate = gate_in[:, v0:v1]
        dy = dy_in[:, v0:v1] * pad
        scale = lax.rsqrt(jnp.mean(o * o, axis=-1, keepdims=True) + 1e-05)
        sig = sigmoid(gate)
        act = gate * sig
        unit = o * scale
        prod = dy * unit
        dgain_out[0:1, :] += jnp.sum(prod * act, axis=0, keepdims=True)
        dgate_out[:, v0:v1] = (prod * gain * (sig * (1.0 + gate * (1.0 - sig)))).astype(bf16)
        dn = dy * gain * act
        do = scale * (dn - unit * jnp.mean(dn * unit, axis=-1, keepdims=True))
        do_out[:, v0:v1] = do
        zst = carry[h]
        z_out[0, h] = zst
        lead = jnp.zeros((n, key), f32)
        dnew = jnp.concatenate([lead, mm(p_in[:, h * n : (h + 1) * n], do, TN, N_FWD)], axis=1)
        dnew = dnew + mm(lr * k_in[:, k0:k1], zst, NN, N_SCAN)
        own = jnp.concatenate(
            [jnp.zeros((key, key), f32), mm(fs * q_in[:, k0:k1], do, TN, N_FWD)], axis=1
        )
        zst = fs[n - 1 :, :] * zst + own - mm(w_in[:, k0:k1], dnew, TN, N_SCAN)
        carry[h] = zst
        zend_out[h] = zst


def through_act(u, grad):
    sig = sigmoid(u)
    return grad * (sig * (1.0 + u * (1.0 - sig)))


def kernel_d(heads, key, val, count, mine, gath, z_in, do_in, s_in, vn_in, q_in, k_in, w_in, u_in, p_in, t_in,
             aux_ref, rows_ref, pqk, pv, bqk, bv, hqk, hv, tqk, tv,
             dqk_out, dv_out, tailqk, tailv, headqk, headv, dtqk, dtv, dcg_out, dbeta_out,
             xqk, xv, dxqk, dxv, end):
    c = pl.program_id(0)
    steps = pl.num_programs(0)
    n = do_in.shape[0]
    hk = heads * key

    @pl.when(c == 0)
    def _():
        end[...] = jnp.zeros_like(end)

        @pl.loop(0, count - 1 - mine[0])
        def _(i):
            d = count - 1 - i
            for h in range(heads):
                end[h] = gath[d, h, :, key:].astype(f32) + mm(gath[d, h, :, :key], end[h], NN, N_FWD)

        dxqk[...] = jnp.zeros_like(dxqk)
        dxv[...] = jnp.zeros_like(dxv)
        dtqk[...] = jnp.zeros_like(dtqk)
        dtv[...] = jnp.zeros_like(dtv)

    @pl.when(c < steps - 1)
    def _():
        xqk[0:HALO, :] = bqk[...].astype(f32)[bqk.shape[0] - HALO :]
        xv[0:HALO, :] = bv[...].astype(f32)[bv.shape[0] - HALO :]

    @pl.when(c == steps - 1)
    def _():
        xqk[0:HALO, :] = hqk[...]
        xv[0:HALO, :] = hv[...]

    xqk[HALO:, :] = pqk[...].astype(f32)
    xv[HALO:, :] = pv[...].astype(f32)
    aux = aux_ref[...]
    rows = rows_ref[0]
    ti, si = grid_iotas(n)
    tri = ti >= si
    last = (lax.broadcasted_iota(jnp.int32, (n, 1), 0) == n - 1).astype(f32)
    dxqk[n:, :] = dxqk[0:HALO, :]
    dxv[n:, :] = dxv[0:HALO, :]
    dxqk[0:n, :] = jnp.zeros((n, 2 * hk), f32)
    dxv[0:n, :] = jnp.zeros((n, heads * val), f32)

    def conv_back(du, ext, dext, taps, dtaps, c0, c1):
        for lag in range(SPAN + 1):
            part = du if lag == 0 else du * aux[:, lag - 1 : lag]
            dtaps[SPAN - lag : SPAN - lag + 1, c0:c1] += jnp.sum(
                part * ext[HALO - lag : HALO - lag + n, c0:c1], axis=0, keepdims=True
            )
            spot = slice(HALO - lag, HALO - lag + n)
            dext[spot, c0:c1] += part * taps[SPAN - lag : SPAN - lag + 1, c0:c1]

    for h in range(heads):
        v0, v1 = h * val, (h + 1) * val
        k0, k1 = h * key, (h + 1) * key
        fs = aux[:, 5 + heads + h : 6 + heads + h]
        lr = aux[:, 5 + 2 * heads + h : 6 + 2 * heads + h]
        beta = aux[:, 5 + 3 * heads + h : 6 + 3 * heads + h]
        q, k = q_in[:, k0:k1], k_in[:, k0:k1]
        w, u = w_in[:, k0:k1], u_in[:, v0:v1]
        p, inv = p_in[:, h * n : (h + 1) * n], t_in[:, h * n : (h + 1) * n]
        do, new, st = do_in[:, v0:v1], vn_in[:, v0:v1], s_in[0, h]
        dst = z_in[0, h, :, key:] + mm(z_in[0, h, :, :key], end[h], NN, N_BWD)
        dec = decay_matrix(aux, rows, h, heads, tri)
        kk = mm(k, k, NT, N_BWD)
        kl = lr * k
        dnew = mm(p, do, TN, N_BWD) + mm(kl, dst, NN, N_BWD)
        dp = mm(do, new, NT, N_BWD)
        dqf = mm(do, st, NT, N_BWD)
        dkl = mm(new, dst, NT, N_BWD)
        dw = -mm(dnew, st, NT, N_BWD)
        drv = mm(inv, dnew, TN, N_BWD)
        drk = mm(inv, dw, TN, N_BWD)
        dlow = -(mm(drv, u, NT, N_BWD) + mm(drk, w, NT, N_BWD))
        dlow = jnp.where(ti > si, dlow, 0.0) * dec
        dkk = dlow * beta
        hh = dp * dec
        pairs = dkk * kk + dp * p
        dq = fs * dqf + mm(hh, k, NN, N_BWD)
        dk = mm(hh, q, TN, N_BWD) + mm(dkk, k, NN, N_BWD) + mm(dkk, k, TN, N_BWD)
        dk = dk + lr * dkl + (beta * fs) * drk
        uv = conv_of(xv, tv, aux, v0, v1)
        v = uv * sigmoid(uv)
        kd = jnp.sum(k * drk, axis=-1, keepdims=True) * fs
        dbeta = jnp.sum(dlow * kk, axis=-1, keepdims=True) + kd
        dbeta = dbeta + jnp.sum(v * drv, axis=-1, keepdims=True)
        leave = lr * jnp.sum(k * dkl, axis=-1, keepdims=True)
        dcg = jnp.sum(pairs, axis=-1, keepdims=True) + beta * kd - leave
        dcg = dcg + fs * jnp.sum(q * dqf, axis=-1, keepdims=True)
        ones = jnp.ones((n, 8), f32)
        dcg = dcg - mm(pairs, ones, TN, 3)[:, 0:1]
        tail = jnp.sum(leave, axis=0, keepdims=True) + fs[n - 1 :, :] * jnp.sum(
            jnp.sum(st * dst, axis=-1, keepdims=True), axis=0, keepdims=True
        )
        dcg_out[:, h : h + 1] = dcg + last * tail
        dbeta_out[:, h : h + 1] = dbeta
        conv_back(through_act(uv, beta * drv), xv, dxv, tv, dtv, v0, v1)
        for off, grad, size in ((0, dq, key ** (-0.5)), (hk, dk, 1.0)):
            uu = conv_of(xqk, tqk, aux, off + k0, off + k1)
            act = uu * sigmoid(uu)
            rs = unit_of(act)
            da = (rs * size) * (grad - act * (rs * rs) * jnp.sum(act * grad, axis=-1, keepdims=True))
            conv_back(through_act(uu, da), xqk, dxqk, tqk, dtqk, off + k0, off + k1)
    dqk_out[...] = dxqk[HALO:, :].astype(bf16)
    dv_out[...] = dxv[HALO:, :].astype(bf16)

    @pl.when(c == 0)
    def _():
        tailqk[...] = dxqk[n:, :]
        tailv[...] = dxv[n:, :]

    headqk[...] = dxqk[0:HALO, :]
    headv[...] = dxv[0:HALO, :]


def params(**kw):
    return pltpu.CompilerParams(vmem_limit_bytes=VLIM, dimension_semantics=("arbitrary",), **kw)


def sds(shape, dtype=f32):
    return jax.ShapeDtypeStruct(shape, dtype)


class Mixer:
    def __init__(self, tokens, heads, key, val):
        self.sizes = (heads, key, val)
        self.tokens, self.n, self.steps = tokens, CH, tokens // CH

    def rows(self, width, back=False):
        m = self.steps - 1
        return pl.BlockSpec((self.n, width), (lambda c: (m - c, 0)) if back else (lambda c: (c, 0)))

    def lead(self, shape, back=False):
        m, rest = self.steps - 1, (0,) * len(shape)
        return pl.BlockSpec((1,) + shape, (lambda c: (m - c,) + rest) if back else (lambda c: (c,) + rest))

    def whole(self, shape):
        rest = (0,) * len(shape)
        return pl.BlockSpec(shape, lambda c: rest)

    def forward_local(self, pqk, pv, hqk, hv, tqk, tv, aux, rows):
        heads, key, val = self.sizes
        t, n, s = self.tokens, self.n, self.steps
        hk, hv_ = heads * key, heads * val
        wide = key + val
        return pl.pallas_call(
            partial(kernel_a, heads, key, val),
            grid=(s,),
            in_specs=[self.rows(2 * hk), self.rows(hv_), self.whole(hqk.shape), self.whole(hv.shape),
                      self.whole(tqk.shape), self.whole(tv.shape), self.rows(aux.shape[1]), self.lead(rows.shape[1:])],
            out_specs=[self.rows(hk), self.rows(hk), self.rows(hk), self.rows(hv_), self.rows(heads * n), self.rows(heads * n),
                       self.lead((heads, key, wide)), self.whole((heads, key, wide))],
            out_shape=[sds((t, hk)), sds((t, hk)), sds((t, hk)), sds((t, hv_)), sds((t, heads * n)), sds((t, heads * n)),
                       sds((s, heads, key, wide)), sds((heads, key, wide))],
            scratch_shapes=[pltpu.VMEM((HALO + n, 2 * hk), f32), pltpu.VMEM((HALO + n, hv_), f32),
                            pltpu.VMEM((heads, key, wide), f32)],
            compiler_params=params(),
            name="mixer_local",
        )(pqk, pv, hqk, hv, tqk, tv, aux, rows)

    def output(self, mine, gath, r, w, u, p, q, aux, gate, gain):
        heads, key, val = self.sizes
        t, n, s = self.tokens, self.n, self.steps
        hk, hv_ = heads * key, heads * val
        return pl.pallas_call(
            partial(kernel_b, heads, key, val),
            grid=(s,),
            in_specs=[pl.BlockSpec(memory_space=pltpu.SMEM), self.whole(gath.shape), self.lead((heads, key, key + val)),
                      self.rows(hk), self.rows(hv_), self.rows(heads * n), self.rows(hk), self.rows(aux.shape[1]),
                      self.rows(hv_), self.whole(gain.shape)],
            out_specs=[self.rows(hv_), self.lead((heads, key, val)), self.rows(hv_), self.rows(hv_)],
            out_shape=[sds((t, hv_), bf16), sds((s, heads, key, val)), sds((t, hv_)), sds((t, hv_))],
            scratch_shapes=[pltpu.VMEM((heads, key, val), f32)],
            compiler_params=params(),
            name="mixer_output",
        )(mine, gath, r, w, u, p, q, aux, gate, gain)

    def backward_local(self, dy, o, gate, gain, aux, q, k, w, p):
        heads, key, val = self.sizes
        t, n, s = self.tokens, self.n, self.steps
        hk, hv_ = heads * key, heads * val
        wide = key + val
        back = partial(self.rows, back=True)
        return pl.pallas_call(
            partial(kernel_c, heads, key, val),
            grid=(s,),
            in_specs=[back(hv_), back(hv_), back(hv_), self.whole(gain.shape), back(aux.shape[1]),
                      back(hk), back(hk), back(hk), back(heads * n)],
            out_specs=[back(hv_), back(hv_), self.whole((8, val)), self.lead((heads, key, wide), True),
                       self.whole((heads, key, wide))],
            out_shape=[sds((t, hv_)), sds((t, hv_), bf16), sds((8, val)), sds((s, heads, key, wide)),
                       sds((heads, key, wide))],
            scratch_shapes=[pltpu.VMEM((heads, key, wide), f32)],
            compiler_params=params(),
            name="mixer_back_local",
        )(dy, o, gate, gain, aux, q, k, w, p)

    def backward(self, mine, gath, z, do, st, vn, q, k, w, u, p, inv, aux, rows, pqk, pv, hqk, hv, tqk, tv):
        heads, key, val = self.sizes
        t, n, s = self.tokens, self.n, self.steps
        hk, hv_ = heads * key, heads * val
        back = partial(self.rows, back=True)
        ratio = n // 16
        m = s - 1

        def before(width):
            return pl.BlockSpec((16, width), lambda c: (jnp.maximum((m - c) * ratio - 1, 0), 0))

        return pl.pallas_call(
            partial(kernel_d, heads, key, val, gath.shape[0]),
            grid=(s,),
            in_specs=[pl.BlockSpec(memory_space=pltpu.SMEM), self.whole(gath.shape), self.lead((heads, key, key + val), True),
                      back(hv_), self.lead((heads, key, val), True), back(hv_), back(hk), back(hk), back(hk), back(hv_),
                      back(heads * n), back(heads * n), back(aux.shape[1]), self.lead(rows.shape[1:], True),
                      back(2 * hk), back(hv_), before(2 * hk), before(hv_), self.whole(hqk.shape), self.whole(hv.shape),
                      self.whole(tqk.shape), self.whole(tv.shape)],
            out_specs=[back(2 * hk), back(hv_), self.whole((HALO, 2 * hk)), self.whole((HALO, hv_)),
                       self.whole((HALO, 2 * hk)), self.whole((HALO, hv_)), self.whole((CONV, 2 * hk)), self.whole((CONV, hv_)),
                       back(heads), back(heads)],
            out_shape=[sds((t, 2 * hk), bf16), sds((t, hv_), bf16), sds((HALO, 2 * hk)), sds((HALO, hv_)),
                       sds((HALO, 2 * hk)), sds((HALO, hv_)), sds((CONV, 2 * hk)), sds((CONV, hv_)),
                       sds((t, heads)), sds((t, heads))],
            scratch_shapes=[pltpu.VMEM((HALO + n, 2 * hk), f32), pltpu.VMEM((HALO + n, hv_), f32),
                            pltpu.VMEM((HALO + n, 2 * hk), f32), pltpu.VMEM((HALO + n, hv_), f32),
                            pltpu.VMEM((heads, key, val), f32)],
            compiler_params=params(),
            name="mixer_back",
        )(mine, gath, z, do, st, vn, q, k, w, u, p, inv, aux, rows, pqk, pv, pqk, pv, hqk, hv, tqk, tv)


def gates_of(mixed_ab, decay, pad):
    g = -jnp.exp(decay[0]) * jax.nn.softplus(mixed_ab[:, 0] + decay[1]) * pad[:, None]
    b = jax.nn.sigmoid(mixed_ab[:, 1]) * pad[:, None]
    return (g, b)


def in_chunks(values, upper):
    tri = jnp.tril(jnp.ones((CH, CH), f32))
    tri = tri.T if upper else tri
    parts = values.reshape(-1, CH, values.shape[1])
    return jnp.einsum("ts,csh->cth", tri, parts, precision=lax.Precision.HIGHEST).reshape(values.shape)


def token_tables(g, b, pad, lag_valid, resets):
    t, heads = g.shape
    sums = in_chunks(jnp.concatenate([g, resets[:, None]], axis=1), False)
    cg, count = sums[:, :heads], sums[:, heads:]
    ends = sums.reshape(-1, CH, heads + 1)[:, -1:]
    ends = jnp.broadcast_to(ends, (ends.shape[0], CH, heads + 1)).reshape(t, heads + 1)
    fs = jnp.where(count == 0, jnp.exp(cg), 0.0)
    to_end = count == ends[:, heads:]
    lr = jnp.where(to_end, jnp.exp(jnp.where(to_end, ends[:, :heads] - cg, 0.0)), 0.0)
    aux = jnp.concatenate([lag_valid[1:].T, pad[:, None], count, cg, fs, lr, b], axis=1)
    rows = jnp.concatenate([count, cg], axis=1).reshape(-1, CH, heads + 1).transpose(0, 2, 1)
    return (aux, rows)


def from_behind(value, axis, by):
    length = lax.axis_size(axis)
    pairs = [(i, i + by) for i in range(length) if 0 <= i + by < length]
    return lax.ppermute(value, axis, pairs)


def norm_rows(values, gain):
    return values * lax.rsqrt(jnp.mean(values * values, axis=-1, keepdims=True) + 1e-06) * gain


def norm_back(values, gain, grad_out):
    scale = lax.rsqrt(jnp.mean(values * values, axis=-1, keepdims=True) + 1e-06)
    scaled_grad = grad_out * gain
    grad_in = scale * scaled_grad - values * scale**3 * jnp.mean(
        scaled_grad * values, axis=-1, keepdims=True
    )
    return (grad_in, jnp.sum(grad_out * values * scale, axis=0))


def dot(a, b, dims=NN, out=f32):
    return lax.dot_general(a, b, dims, preferred_element_type=out)


adam_step = 10.0


def adamw(weight, grad, first, second, rate, shrink):
    first = 0.9 * first + 0.1 * grad
    second = 0.999 * second + 0.001 * grad * grad
    first_hat = first / (1.0 - 0.9**adam_step)
    second_hat = second / (1.0 - 0.999**adam_step)
    weight = weight - rate * (first_hat / (jnp.sqrt(second_hat) + 1e-08) + shrink * weight)
    return [weight, first, second]


def on_device(tokens_in, cotangent, segment_ids, pad_mask, *state):
    masters, firsts, seconds = state[0::3], state[1::3], state[2::3]
    (qk_proj, vg_proj, ab_proj, out_proj, gu_proj, down_proj,
     norm_gains, qk_conv, v_conv, out_gain, decay_params) = masters
    tokens = tokens_in.shape[0]
    dp = lax.axis_size("dp")
    mine = lax.axis_index("dp")
    start = mine * tokens
    rows = qk_proj.shape[0]
    heads, key, val = qk_proj.shape[2], qk_proj.shape[3], vg_proj.shape[3]
    units = gu_proj.shape[2]
    hk, hv = heads * key, heads * val
    mixer = Mixer(tokens, heads, key, val)

    def low(x):
        return x.astype(bf16)

    small = [norm_gains, qk_conv, v_conv, out_gain]
    flat = jnp.concatenate([low(x).reshape(-1) for x in small])
    small_cols = pl.cdiv(flat.shape[0], rows)
    room = 128 - 2 * heads - small_cols
    flat = jnp.pad(flat, (0, rows * small_cols - flat.shape[0])).reshape(rows, small_cols)
    extra = jnp.concatenate(
        [low(ab_proj).reshape(rows, 2 * heads), flat, jnp.zeros((rows, room), bf16)], axis=1
    )
    vg_low = low(vg_proj)
    shard_one = jnp.concatenate(
        [low(qk_proj).reshape(rows, 2 * hk), vg_low[:, 0].reshape(rows, hv), extra], axis=1
    )
    shard_two = jnp.concatenate(
        [vg_low[:, 1].reshape(rows, hv), low(out_proj).reshape(hv, rows).T], axis=1
    )
    shard_gu = low(gu_proj).reshape(rows, 2 * units)
    shard_down = low(down_proj).T

    def gather(x):
        return lax.all_gather(x, "dp", axis=0, tiled=True)

    full_one = gather(shard_one)
    full_two = gather(shard_two)
    full_gu = gather(shard_gu)
    full_down = gather(shard_down)

    cut = 2 * hk + hv
    flats = full_one[:, cut + 2 * heads : cut + 2 * heads + small_cols].reshape(dp, rows * small_cols)
    parts, at = [], 0
    for x in small:
        size = x.size
        parts.append(flats[:, at : at + size].reshape((dp,) + x.shape).astype(f32))
        at += size
    gains = jnp.moveaxis(parts[0], 0, 1).reshape(2, -1)
    taps_qk = jnp.moveaxis(parts[1], 0, 3).reshape(2, CONV, hk)
    taps_qk = jnp.moveaxis(taps_qk, 0, 1).reshape(CONV, 2 * hk)
    taps_v = jnp.moveaxis(parts[2], 0, 2).reshape(CONV, hv)
    gain = jnp.broadcast_to(parts[3].reshape(1, val), (8, val))
    decay_low = lax.optimization_barrier(low(decay_params)).astype(f32)

    padded_ids = jnp.concatenate([jnp.full((4,), -1, jnp.int32), segment_ids])
    here_ids = lax.dynamic_slice_in_dim(padded_ids, start + 1, tokens + SPAN)
    prior_ids = lax.dynamic_slice_in_dim(padded_ids, start, tokens + SPAN)
    positions = start - SPAN + jnp.arange(tokens + SPAN, dtype=jnp.int32)
    resets_ext = ((here_ids != prior_ids) | (positions == 0)).astype(f32)
    resets_here = resets_ext[SPAN:]
    keep_ext = 1.0 - resets_ext
    valid_rows = [jnp.ones((tokens,), f32)]
    for lag in range(1, SPAN + 1):
        valid_rows.append(valid_rows[-1] * keep_ext[SPAN - lag + 1 : SPAN - lag + 1 + tokens])
    lag_valid = jnp.stack(valid_rows)
    pad = lax.dynamic_slice_in_dim(pad_mask, start, tokens).astype(f32)

    x_rim = from_behind(tokens_in[tokens - HALO :], "dp", 1)
    x = tokens_in.astype(f32)
    normed = low(norm_rows(x, gains[0]))
    normed_rim = low(norm_rows(x_rim.astype(f32), gains[0]))
    pre_qk = dot(normed, full_one[:, : 2 * hk], out=bf16)
    pre_v = dot(normed, full_one[:, 2 * hk : cut], out=bf16)
    mixed = dot(normed, full_one[:, cut:])[:, : 2 * heads].reshape(tokens, 2, heads)
    rim = low(dot(normed_rim, full_one[:, :cut])).astype(f32)
    gate_pre = dot(normed, full_two[:, :hv])
    (g, b), pull_gates = jax.vjp(lambda ab, dec: gates_of(ab, dec, pad), mixed, decay_low)
    aux, rowform = token_tables(g, b, pad, lag_valid, resets_here)

    rim_qk, rim_v = rim[:, : 2 * hk], rim[:, 2 * hk :]
    q, k, w, u, p, inv, r, r_end = mixer.forward_local(
        pre_qk, pre_v, rim_qk, rim_v, taps_qk, taps_v, aux, rowform
    )
    spot = mine.astype(jnp.int32).reshape(1)
    maps = lax.all_gather(low(r_end), "dp")
    y, st, vn, o = mixer.output(spot, maps, r, w, u, p, q, aux, gate_pre, gain)

    out_t = full_two[:, hv:]
    attn = lax.psum(dot(y, out_t, NT, bf16), "mp").astype(f32)
    hidden = x + attn
    normed_two = low(norm_rows(hidden, gains[1]))
    gate_up = dot(normed_two, full_gu)
    gate_two, up_two = gate_up[:, :units], gate_up[:, units:]
    sig = jax.nn.sigmoid(gate_two)
    act = low(gate_two * sig * up_two)
    down = lax.psum(dot(act, full_down, NT, bf16), "mp").astype(f32)
    block_out = low(hidden + down)
    grad_act = dot(cotangent, full_down)
    grad_up = grad_act * gate_two * sig
    grad_gate = grad_act * up_two * sig * (1.0 + gate_two * (1.0 - sig))
    grad_gu_in = low(jnp.concatenate([grad_gate, grad_up], axis=1))
    grad_two = lax.psum(dot(grad_gu_in, full_gu, NT, bf16), "mp").astype(f32)
    grad_down = dot(cotangent, act, TN, bf16)
    grad_gu = dot(normed_two, grad_gu_in, TN, bf16)

    grad_hidden_norm, grad_gain_two = norm_back(hidden, gains[1], grad_two)
    grad_hidden = cotangent.astype(f32) + grad_hidden_norm
    dattn = low(grad_hidden)
    dy = dot(dattn, out_t)
    grad_out = dot(dattn, y, TN, bf16)
    do, dgate, dgain, z, z_end = mixer.backward_local(dy, o, gate_pre, gain, aux, q, k, w, p)
    back_maps = lax.all_gather(low(z_end), "dp")
    (dqk, dv, tail_qk, tail_v, head_qk, head_v, dtaps_qk, dtaps_v, dcg, dbeta) = mixer.backward(
        spot, back_maps, z, do, st, vn, q, k, w, u, p, inv, aux, rowform,
        pre_qk, pre_v, rim_qk, rim_v, taps_qk, taps_v
    )
    heads_back = from_behind(jnp.concatenate([head_qk, head_v], axis=1), "dp", -1)
    dqk = lax.dynamic_update_slice(dqk, low(tail_qk + heads_back[:, : 2 * hk]), (tokens - HALO, 0))
    dv = lax.dynamic_update_slice(dv, low(tail_v + heads_back[:, 2 * hk :]), (tokens - HALO, 0))
    dmixed, ddecay = pull_gates((in_chunks(dcg, True), dbeta))
    dab = jnp.pad(low(dmixed.reshape(tokens, 2 * heads)), ((0, 0), (0, 128 - 2 * heads)))
    dpre = jnp.concatenate([dqk, dv, dab], axis=1)
    normed_part = dot(dpre, full_one, NT) + dot(dgate, full_two[:, :hv], NT)
    grad_normed = lax.psum(low(normed_part), "mp").astype(f32)
    grad_x, grad_gain_one = norm_back(x, gains[0], grad_normed)
    input_grad = grad_hidden + grad_x

    grad_one = dot(normed, dpre, TN, bf16)
    grad_gate_w = dot(normed, dgate, TN, bf16)
    grad_small = [
        jnp.stack([grad_gain_one, grad_gain_two]).reshape(2, dp, -1),
        dtaps_qk.reshape(CONV, 2, heads, dp, -1).transpose(1, 0, 2, 3, 4),
        dtaps_v.reshape(CONV, heads, dp, -1),
        dgain[0].reshape(dp, -1),
    ]
    grad_flat = jnp.concatenate(
        [jnp.moveaxis(gs, -2, 0).reshape(dp, -1) for gs in grad_small], axis=1
    )
    grad_flat = jnp.pad(grad_flat, ((0, 0), (0, rows * small_cols - grad_flat.shape[1])))
    grad_flat = low(grad_flat).reshape(dp * rows, small_cols)
    grad_one = lax.dynamic_update_slice(grad_one, grad_flat, (0, cut + 2 * heads))

    def scatter(value):
        return lax.psum_scatter(value, "dp", scatter_dimension=0, tiled=True).astype(f32)

    red_gu = scatter(grad_gu)
    red_down = scatter(grad_down)
    red_two = scatter(jnp.concatenate([grad_gate_w, grad_out], axis=1))
    red_one = scatter(grad_one)
    red_flat = red_one[:, cut + 2 * heads : cut + 2 * heads + small_cols].reshape(-1)
    red_small, at = [], 0
    for s in small:
        red_small.append(red_flat[at : at + s.size].reshape(s.shape))
        at += s.size
    red_small[3] = lax.psum(red_small[3], "mp")
    grads = [
        red_one[:, : 2 * hk].reshape(qk_proj.shape),
        jnp.stack([red_one[:, 2 * hk : cut].reshape(rows, heads, val),
                   red_two[:, :hv].reshape(rows, heads, val)], axis=1),
        red_one[:, cut : cut + 2 * heads].reshape(ab_proj.shape),
        red_two[:, hv:].T.reshape(out_proj.shape),
        red_gu.reshape(gu_proj.shape),
        red_down.T,
    ] + red_small + [lax.psum(ddecay, "dp")]
    matrix_rate = 2.5 * D ** (-0.5)
    rates = [matrix_rate] * 6 + [0.5, 1.0, 1.0, 0.5, 2.0]
    shrinks = [0.1] * 6 + [0.0] * 5
    updates = []
    for i in range(11):
        updates += adamw(masters[i], grads[i], firsts[i], seconds[i], rates[i], shrinks[i])
    copies = [low(updates[3 * i]) for i in range(6)]
    return (block_out, input_grad, *updates, *copies)


def solution(mesh):
    weights = [
        P("dp", None, "mp", None),
        P("dp", None, "mp", None),
        P("dp", None, "mp"),
        P("mp", None, "dp"),
        P("dp", None, "mp"),
        P("mp", "dp"),
        P(None, "dp"),
        P(None, None, "mp", "dp"),
        P(None, "mp", "dp"),
        P("dp"),
        P(None, "mp"),
    ]
    thrice = tuple(w for w in weights for _ in range(3))
    rowwise = P("dp", None)
    return jax.shard_map(
        on_device,
        mesh=mesh,
        in_specs=(rowwise, rowwise, P(), P()) + thrice,
        out_specs=(rowwise, rowwise) + thrice + tuple(weights[:6]),
        check_vma=False,
    )
```

```python
from functools import partial

import jax
import jax.numpy as jnp
from jax import lax
from jax.experimental import pallas as pl
from jax.experimental.layout import Layout, with_layout_constraint
from jax.experimental.pallas import tpu as pltpu
from jax.sharding import PartitionSpec as P

D = 2048
CONV = 4
SPAN = CONV - 1
CH = 128
HALO = 8
f32 = jnp.float32
bf16 = jnp.bfloat16
VLIM = 56 * 2**20

NN = (((1,), (0,)), ((), ()))
NT = (((1,), (1,)), ((), ()))
TN = (((0,), (0,)), ((), ()))

N_INV = 3
N_FWD = 1
N_SCAN = 1
N_BWD = 1


def mm(a, b, dims=NN, passes=1):
    def dot(x, y):
        return lax.dot_general(x, y, dims, preferred_element_type=f32)

    ah, bh = a.astype(bf16), b.astype(bf16)
    out = dot(ah, bh)
    if passes == 3:
        al = (a - ah.astype(f32)).astype(bf16)
        bl = (b - bh.astype(f32)).astype(bf16)
        out = out + (dot(ah, bl) + dot(al, bh))
    return out


def grid_iotas(n):
    return (
        lax.broadcasted_iota(jnp.int32, (n, n), 0),
        lax.broadcasted_iota(jnp.int32, (n, n), 1),
    )


def unit_lower_inverse(lowers, n):
    rows, cols = grid_iotas(n)
    eye = (rows == cols).astype(f32)
    small = lax.shift_right_logical(rows, 3) == lax.shift_right_logical(cols, 3)
    diag = [jnp.where(small, low, 0.0) for low in lowers]
    two = [mm(d, d, NN, N_INV) for d in diag]
    four = [mm(t, t, NN, N_INV) for t in two]
    inv = [eye - d for d in diag]
    inv = [x + mm(x, t, NN, N_INV) for x, t in zip(inv, two)]
    inv = [x + mm(x, f, NN, N_INV) for x, f in zip(inv, four)]
    bits = 3
    while (1 << bits) < n:
        wide = lax.shift_right_logical(rows, bits + 1) == lax.shift_right_logical(cols, bits + 1)
        fine = lax.shift_right_logical(rows, bits) != lax.shift_right_logical(cols, bits)
        off = [jnp.where(wide & fine, low, 0.0) for low in lowers]
        half = [mm(x, o, NN, N_INV) for x, o in zip(inv, off)]
        inv = [x - mm(y, x, NN, N_INV) for x, y in zip(inv, half)]
        bits += 1
    return inv


def sigmoid(x):
    return 1.0 / (1.0 + jnp.exp(-x))


def decay_matrix(aux, rows, h, heads, tri):
    cg = aux[:, 5 + h : 6 + h]
    cg_row = rows[1 + h : 2 + h, :]
    same = (aux[:, 4:5] == rows[0:1, :]) & tri
    return jnp.where(same, jnp.exp(jnp.where(same, cg - cg_row, 0.0)), 0.0)


def conv_of(ext_ref, taps_ref, aux, c0, c1):
    n = aux.shape[0]
    total = ext_ref[HALO : HALO + n, c0:c1] * taps_ref[SPAN : SPAN + 1, c0:c1]
    for lag in range(1, SPAN + 1):
        total = total + ext_ref[HALO - lag : HALO - lag + n, c0:c1] * (
            taps_ref[SPAN - lag : SPAN - lag + 1, c0:c1] * aux[:, lag - 1 : lag]
        )
    return total


def unit_of(act):
    return lax.rsqrt(jnp.sum(act * act, axis=-1, keepdims=True) + 1e-06)


def kernel_a(heads, key, val, pqk, pv, hqk, hv, tqk, tv, aux_ref, rows_ref,
             q_out, k_out, w_out, u_out, p_out, t_out, r_out, rend_out,
             xqk, xv, state):
    c = pl.program_id(0)
    n = pqk.shape[0]
    hk = heads * key

    @pl.when(c == 0)
    def _():
        xqk[0:HALO, :] = hqk[...]
        xv[0:HALO, :] = hv[...]
        r, s = (lax.broadcasted_iota(jnp.int32, (key, key + val), i) for i in (0, 1))
        for h in range(heads):
            state[h] = (r == s).astype(f32)

    xqk[HALO:, :] = pqk[...].astype(f32)
    xv[HALO:, :] = pv[...].astype(f32)
    aux = aux_ref[...]
    rows = rows_ref[0]
    ti, si = grid_iotas(n)
    tri = ti >= si
    lowers, queries, keys = [], [], []
    for h in range(heads):
        uq = conv_of(xqk, tqk, aux, h * key, (h + 1) * key)
        uk = conv_of(xqk, tqk, aux, hk + h * key, hk + (h + 1) * key)
        aq = uq * sigmoid(uq)
        ak = uk * sigmoid(uk)
        q = aq * unit_of(aq) * key ** (-0.5)
        k = ak * unit_of(ak)
        q_out[:, h * key : (h + 1) * key] = q
        k_out[:, h * key : (h + 1) * key] = k
        dec = decay_matrix(aux, rows, h, heads, tri)
        beta = aux[:, 5 + 3 * heads + h : 6 + 3 * heads + h]
        p_out[:, h * n : (h + 1) * n] = mm(q, k, NT, N_FWD) * dec
        lowers.append(jnp.where(ti > si, mm(k, k, NT, N_INV) * dec, 0.0) * beta)
        queries.append(q)
        keys.append(k)
    invs = unit_lower_inverse(lowers, n)
    for h in range(heads):
        k = keys[h]
        beta = aux[:, 5 + 3 * heads + h : 6 + 3 * heads + h]
        fs = aux[:, 5 + heads + h : 6 + heads + h]
        lr = aux[:, 5 + 2 * heads + h : 6 + 2 * heads + h]
        uv = conv_of(xv, tv, aux, h * val, (h + 1) * val)
        v = uv * sigmoid(uv)
        t_out[:, h * n : (h + 1) * n] = invs[h]
        w = mm(invs[h], (beta * fs) * k, NN, N_FWD)
        u = mm(invs[h], beta * v, NN, N_FWD)
        w_out[:, h * key : (h + 1) * key] = w
        u_out[:, h * val : (h + 1) * val] = u
        st = state[h]
        r_out[0, h] = st
        new = jnp.concatenate([jnp.zeros((n, key), f32), u], axis=1) - mm(w, st, NN, N_SCAN)
        st = fs[n - 1 :, :] * st + mm(lr * k, new, TN, N_SCAN)
        state[h] = st
        rend_out[h] = st
    xqk[0:HALO, :] = xqk[n:, :]
    xv[0:HALO, :] = xv[n:, :]


def kernel_b(heads, key, val, mine, gath, r_in, w_in, u_in, p_in, q_in, aux_ref, gate_in, gain_ref,
             y_out, s_out, vn_out, o_out, start):
    c = pl.program_id(0)
    n = w_in.shape[0]

    @pl.when(c == 0)
    def _():
        start[...] = jnp.zeros_like(start)

        @pl.loop(0, mine[0])
        def _(d):
            for h in range(heads):
                start[h] = gath[d, h, :, key:].astype(f32) + mm(gath[d, h, :, :key], start[h], NN, N_FWD)

    aux = aux_ref[...]
    pad = aux[:, 3:4]
    for h in range(heads):
        fs = aux[:, 5 + heads + h : 6 + heads + h]
        st = r_in[0, h, :, key:] + mm(r_in[0, h, :, :key], start[h], NN, N_FWD)
        s_out[0, h] = st
        v0, v1 = h * val, (h + 1) * val
        new = u_in[:, v0:v1] - mm(w_in[:, h * key : (h + 1) * key], st, NN, N_FWD)
        vn_out[:, v0:v1] = new
        o = mm(fs * q_in[:, h * key : (h + 1) * key], st, NN, N_FWD)
        o = o + mm(p_in[:, h * n : (h + 1) * n], new, NN, N_FWD)
        o_out[:, v0:v1] = o
        scale = lax.rsqrt(jnp.mean(o * o, axis=-1, keepdims=True) + 1e-05)
        gate = gate_in[:, v0:v1]
        y = o * scale * gain_ref[0:1, :] * (gate * sigmoid(gate)) * pad
        y_out[:, v0:v1] = y.astype(bf16)


def kernel_c(heads, key, val, dy_in, o_in, gate_in, gain_ref, aux_ref, q_in, k_in, w_in, p_in,
             do_out, dgate_out, dgain_out, z_out, zend_out, carry):
    c = pl.program_id(0)
    n = dy_in.shape[0]

    @pl.when(c == 0)
    def _():
        r, s = (lax.broadcasted_iota(jnp.int32, (key, key + val), i) for i in (0, 1))
        for h in range(heads):
            carry[h] = (r == s).astype(f32)
        dgain_out[...] = jnp.zeros_like(dgain_out)

    aux = aux_ref[...]
    pad = aux[:, 3:4]
    gain = gain_ref[0:1, :]
    for h in range(heads):
        v0, v1 = h * val, (h + 1) * val
        k0, k1 = h * key, (h + 1) * key
        fs = aux[:, 5 + heads + h : 6 + heads + h]
        lr = aux[:, 5 + 2 * heads + h : 6 + 2 * heads + h]
        o = o_in[:, v0:v1]
        gate = gate_in[:, v0:v1]
        dy = dy_in[:, v0:v1] * pad
        scale = lax.rsqrt(jnp.mean(o * o, axis=-1, keepdims=True) + 1e-05)
        sig = sigmoid(gate)
        act = gate * sig
        unit = o * scale
        prod = dy * unit
        dgain_out[0:1, :] += jnp.sum(prod * act, axis=0, keepdims=True)
        dgate_out[:, v0:v1] = (prod * gain * (sig * (1.0 + gate * (1.0 - sig)))).astype(bf16)
        dn = dy * gain * act
        do = scale * (dn - unit * jnp.mean(dn * unit, axis=-1, keepdims=True))
        do_out[:, v0:v1] = do
        zst = carry[h]
        z_out[0, h] = zst
        lead = jnp.zeros((n, key), f32)
        dnew = jnp.concatenate([lead, mm(p_in[:, h * n : (h + 1) * n], do, TN, N_FWD)], axis=1)
        dnew = dnew + mm(lr * k_in[:, k0:k1], zst, NN, N_SCAN)
        own = jnp.concatenate(
            [jnp.zeros((key, key), f32), mm(fs * q_in[:, k0:k1], do, TN, N_FWD)], axis=1
        )
        zst = fs[n - 1 :, :] * zst + own - mm(w_in[:, k0:k1], dnew, TN, N_SCAN)
        carry[h] = zst
        zend_out[h] = zst


def through_act(u, grad):
    sig = sigmoid(u)
    return grad * (sig * (1.0 + u * (1.0 - sig)))


def kernel_d(heads, key, val, count, mine, gath, z_in, do_in, s_in, vn_in, q_in, k_in, w_in, u_in, p_in, t_in,
             aux_ref, rows_ref, pqk, pv, bqk, bv, hqk, hv, tqk, tv,
             dqk_out, dv_out, tailqk, tailv, headqk, headv, dtqk, dtv, dcg_out, dbeta_out,
             xqk, xv, dxqk, dxv, end):
    c = pl.program_id(0)
    steps = pl.num_programs(0)
    n = do_in.shape[0]
    hk = heads * key

    @pl.when(c == 0)
    def _():
        end[...] = jnp.zeros_like(end)

        @pl.loop(0, count - 1 - mine[0])
        def _(i):
            d = count - 1 - i
            for h in range(heads):
                end[h] = gath[d, h, :, key:].astype(f32) + mm(gath[d, h, :, :key], end[h], NN, N_FWD)

        dxqk[...] = jnp.zeros_like(dxqk)
        dxv[...] = jnp.zeros_like(dxv)
        dtqk[...] = jnp.zeros_like(dtqk)
        dtv[...] = jnp.zeros_like(dtv)

    @pl.when(c < steps - 1)
    def _():
        xqk[0:HALO, :] = bqk[...].astype(f32)[bqk.shape[0] - HALO :]
        xv[0:HALO, :] = bv[...].astype(f32)[bv.shape[0] - HALO :]

    @pl.when(c == steps - 1)
    def _():
        xqk[0:HALO, :] = hqk[...]
        xv[0:HALO, :] = hv[...]

    xqk[HALO:, :] = pqk[...].astype(f32)
    xv[HALO:, :] = pv[...].astype(f32)
    aux = aux_ref[...]
    rows = rows_ref[0]
    ti, si = grid_iotas(n)
    tri = ti >= si
    last = (lax.broadcasted_iota(jnp.int32, (n, 1), 0) == n - 1).astype(f32)
    dxqk[n:, :] = dxqk[0:HALO, :]
    dxv[n:, :] = dxv[0:HALO, :]
    dxqk[0:n, :] = jnp.zeros((n, 2 * hk), f32)
    dxv[0:n, :] = jnp.zeros((n, heads * val), f32)

    def conv_back(du, ext, dext, taps, dtaps, c0, c1):
        for lag in range(SPAN + 1):
            part = du if lag == 0 else du * aux[:, lag - 1 : lag]
            dtaps[SPAN - lag : SPAN - lag + 1, c0:c1] += jnp.sum(
                part * ext[HALO - lag : HALO - lag + n, c0:c1], axis=0, keepdims=True
            )
            spot = slice(HALO - lag, HALO - lag + n)
            dext[spot, c0:c1] += part * taps[SPAN - lag : SPAN - lag + 1, c0:c1]

    for h in range(heads):
        v0, v1 = h * val, (h + 1) * val
        k0, k1 = h * key, (h + 1) * key
        fs = aux[:, 5 + heads + h : 6 + heads + h]
        lr = aux[:, 5 + 2 * heads + h : 6 + 2 * heads + h]
        beta = aux[:, 5 + 3 * heads + h : 6 + 3 * heads + h]
        q, k = q_in[:, k0:k1], k_in[:, k0:k1]
        w, u = w_in[:, k0:k1], u_in[:, v0:v1]
        p, inv = p_in[:, h * n : (h + 1) * n], t_in[:, h * n : (h + 1) * n]
        do, new, st = do_in[:, v0:v1], vn_in[:, v0:v1], s_in[0, h]
        dst = z_in[0, h, :, key:] + mm(z_in[0, h, :, :key], end[h], NN, N_BWD)
        dec = decay_matrix(aux, rows, h, heads, tri)
        kk = mm(k, k, NT, N_BWD)
        kl = lr * k
        dnew = mm(p, do, TN, N_BWD) + mm(kl, dst, NN, N_BWD)
        dp = mm(do, new, NT, N_BWD)
        dqf = mm(do, st, NT, N_BWD)
        dkl = mm(new, dst, NT, N_BWD)
        dw = -mm(dnew, st, NT, N_BWD)
        drv = mm(inv, dnew, TN, N_BWD)
        drk = mm(inv, dw, TN, N_BWD)
        dlow = -(mm(drv, u, NT, N_BWD) + mm(drk, w, NT, N_BWD))
        dlow = jnp.where(ti > si, dlow, 0.0) * dec
        dkk = dlow * beta
        hh = dp * dec
        pairs = dkk * kk + dp * p
        dq = fs * dqf + mm(hh, k, NN, N_BWD)
        dk = mm(hh, q, TN, N_BWD) + mm(dkk, k, NN, N_BWD) + mm(dkk, k, TN, N_BWD)
        dk = dk + lr * dkl + (beta * fs) * drk
        uv = conv_of(xv, tv, aux, v0, v1)
        v = uv * sigmoid(uv)
        kd = jnp.sum(k * drk, axis=-1, keepdims=True) * fs
        dbeta = jnp.sum(dlow * kk, axis=-1, keepdims=True) + kd
        dbeta = dbeta + jnp.sum(v * drv, axis=-1, keepdims=True)
        leave = lr * jnp.sum(k * dkl, axis=-1, keepdims=True)
        dcg = jnp.sum(pairs, axis=-1, keepdims=True) + beta * kd - leave
        dcg = dcg + fs * jnp.sum(q * dqf, axis=-1, keepdims=True)
        ones = jnp.ones((n, 8), f32)
        dcg = dcg - mm(pairs, ones, TN, 3)[:, 0:1]
        tail = jnp.sum(leave, axis=0, keepdims=True) + fs[n - 1 :, :] * jnp.sum(
            jnp.sum(st * dst, axis=-1, keepdims=True), axis=0, keepdims=True
        )
        dcg_out[:, h : h + 1] = dcg + last * tail
        dbeta_out[:, h : h + 1] = dbeta
        conv_back(through_act(uv, beta * drv), xv, dxv, tv, dtv, v0, v1)
        for off, grad, size in ((0, dq, key ** (-0.5)), (hk, dk, 1.0)):
            uu = conv_of(xqk, tqk, aux, off + k0, off + k1)
            act = uu * sigmoid(uu)
            rs = unit_of(act)
            da = (rs * size) * (grad - act * (rs * rs) * jnp.sum(act * grad, axis=-1, keepdims=True))
            conv_back(through_act(uu, da), xqk, dxqk, tqk, dtqk, off + k0, off + k1)
    dqk_out[...] = dxqk[HALO:, :].astype(bf16)
    dv_out[...] = dxv[HALO:, :].astype(bf16)

    @pl.when(c == 0)
    def _():
        tailqk[...] = dxqk[n:, :]
        tailv[...] = dxv[n:, :]

    headqk[...] = dxqk[0:HALO, :]
    headv[...] = dxv[0:HALO, :]


def cost(microseconds):
    return pl.CostEstimate(flops=0, bytes_accessed=int(microseconds * 3.3e6), transcendentals=0)


def params(**kw):
    return pltpu.CompilerParams(vmem_limit_bytes=VLIM, dimension_semantics=("arbitrary",), **kw)


def sds(shape, dtype=f32):
    return jax.ShapeDtypeStruct(shape, dtype)


class Mixer:
    def __init__(self, tokens, heads, key, val):
        self.sizes = (heads, key, val)
        self.tokens, self.n, self.steps = tokens, CH, tokens // CH

    def rows(self, width, back=False):
        m = self.steps - 1
        return pl.BlockSpec((self.n, width), (lambda c: (m - c, 0)) if back else (lambda c: (c, 0)))

    def lead(self, shape, back=False):
        m, rest = self.steps - 1, (0,) * len(shape)
        return pl.BlockSpec((1,) + shape, (lambda c: (m - c,) + rest) if back else (lambda c: (c,) + rest))

    def whole(self, shape):
        rest = (0,) * len(shape)
        return pl.BlockSpec(shape, lambda c: rest)

    def forward_local(self, pqk, pv, hqk, hv, tqk, tv, aux, rows):
        heads, key, val = self.sizes
        t, n, s = self.tokens, self.n, self.steps
        hk, hv_ = heads * key, heads * val
        wide = key + val
        return pl.pallas_call(
            partial(kernel_a, heads, key, val),
            grid=(s,),
            in_specs=[self.rows(2 * hk), self.rows(hv_), self.whole(hqk.shape), self.whole(hv.shape),
                      self.whole(tqk.shape), self.whole(tv.shape), self.rows(aux.shape[1]), self.lead(rows.shape[1:])],
            out_specs=[self.rows(hk), self.rows(hk), self.rows(hk), self.rows(hv_), self.rows(heads * n), self.rows(heads * n),
                       self.lead((heads, key, wide)), self.whole((heads, key, wide))],
            out_shape=[sds((t, hk)), sds((t, hk)), sds((t, hk)), sds((t, hv_)), sds((t, heads * n)), sds((t, heads * n)),
                       sds((s, heads, key, wide)), sds((heads, key, wide))],
            scratch_shapes=[pltpu.VMEM((HALO + n, 2 * hk), f32), pltpu.VMEM((HALO + n, hv_), f32),
                            pltpu.VMEM((heads, key, wide), f32)],
            compiler_params=params(),
            cost_estimate=cost(39),
            name="mixer_local",
        )(pqk, pv, hqk, hv, tqk, tv, aux, rows)

    def output(self, mine, gath, r, w, u, p, q, aux, gate, gain):
        heads, key, val = self.sizes
        t, n, s = self.tokens, self.n, self.steps
        hk, hv_ = heads * key, heads * val
        return pl.pallas_call(
            partial(kernel_b, heads, key, val),
            grid=(s,),
            in_specs=[pl.BlockSpec(memory_space=pltpu.SMEM), self.whole(gath.shape), self.lead((heads, key, key + val)),
                      self.rows(hk), self.rows(hv_), self.rows(heads * n), self.rows(hk), self.rows(aux.shape[1]),
                      self.rows(hv_), self.whole(gain.shape)],
            out_specs=[self.rows(hv_), self.lead((heads, key, val)), self.rows(hv_), self.rows(hv_)],
            out_shape=[sds((t, hv_), bf16), sds((s, heads, key, val)), sds((t, hv_)), sds((t, hv_))],
            scratch_shapes=[pltpu.VMEM((heads, key, val), f32)],
            compiler_params=params(),
            cost_estimate=cost(18),
            name="mixer_output",
        )(mine, gath, r, w, u, p, q, aux, gate, gain)

    def backward_local(self, dy, o, gate, gain, aux, q, k, w, p):
        heads, key, val = self.sizes
        t, n, s = self.tokens, self.n, self.steps
        hk, hv_ = heads * key, heads * val
        wide = key + val
        back = partial(self.rows, back=True)
        return pl.pallas_call(
            partial(kernel_c, heads, key, val),
            grid=(s,),
            in_specs=[back(hv_), back(hv_), back(hv_), self.whole(gain.shape), back(aux.shape[1]),
                      back(hk), back(hk), back(hk), back(heads * n)],
            out_specs=[back(hv_), back(hv_), self.whole((8, val)), self.lead((heads, key, wide), True),
                       self.whole((heads, key, wide))],
            out_shape=[sds((t, hv_)), sds((t, hv_), bf16), sds((8, val)), sds((s, heads, key, wide)),
                       sds((heads, key, wide))],
            scratch_shapes=[pltpu.VMEM((heads, key, wide), f32)],
            compiler_params=params(),
            cost_estimate=cost(17),
            name="mixer_back_local",
        )(dy, o, gate, gain, aux, q, k, w, p)

    def backward(self, mine, gath, z, do, st, vn, q, k, w, u, p, inv, aux, rows, pqk, pv, hqk, hv, tqk, tv):
        heads, key, val = self.sizes
        t, n, s = self.tokens, self.n, self.steps
        hk, hv_ = heads * key, heads * val
        back = partial(self.rows, back=True)
        ratio = n // 16
        m = s - 1

        def before(width):
            return pl.BlockSpec((16, width), lambda c: (jnp.maximum((m - c) * ratio - 1, 0), 0))

        return pl.pallas_call(
            partial(kernel_d, heads, key, val, gath.shape[0]),
            grid=(s,),
            in_specs=[pl.BlockSpec(memory_space=pltpu.SMEM), self.whole(gath.shape), self.lead((heads, key, key + val), True),
                      back(hv_), self.lead((heads, key, val), True), back(hv_), back(hk), back(hk), back(hk), back(hv_),
                      back(heads * n), back(heads * n), back(aux.shape[1]), self.lead(rows.shape[1:], True),
                      back(2 * hk), back(hv_), before(2 * hk), before(hv_), self.whole(hqk.shape), self.whole(hv.shape),
                      self.whole(tqk.shape), self.whole(tv.shape)],
            out_specs=[back(2 * hk), back(hv_), self.whole((HALO, 2 * hk)), self.whole((HALO, hv_)),
                       self.whole((HALO, 2 * hk)), self.whole((HALO, hv_)), self.whole((CONV, 2 * hk)), self.whole((CONV, hv_)),
                       back(heads), back(heads)],
            out_shape=[sds((t, 2 * hk), bf16), sds((t, hv_), bf16), sds((HALO, 2 * hk)), sds((HALO, hv_)),
                       sds((HALO, 2 * hk)), sds((HALO, hv_)), sds((CONV, 2 * hk)), sds((CONV, hv_)),
                       sds((t, heads)), sds((t, heads))],
            scratch_shapes=[pltpu.VMEM((HALO + n, 2 * hk), f32), pltpu.VMEM((HALO + n, hv_), f32),
                            pltpu.VMEM((HALO + n, 2 * hk), f32), pltpu.VMEM((HALO + n, hv_), f32),
                            pltpu.VMEM((heads, key, val), f32)],
            compiler_params=params(),
            cost_estimate=cost(50),
            name="mixer_back",
        )(mine, gath, z, do, st, vn, q, k, w, u, p, inv, aux, rows, pqk, pv, pqk, pv, hqk, hv, tqk, tv)


def gates_of(mixed_ab, decay, pad):
    g = -jnp.exp(decay[0]) * jax.nn.softplus(mixed_ab[:, 0] + decay[1]) * pad[:, None]
    b = jax.nn.sigmoid(mixed_ab[:, 1]) * pad[:, None]
    return (g, b)


def in_chunks(values, upper):
    tri = jnp.tril(jnp.ones((CH, CH), f32))
    tri = tri.T if upper else tri
    parts = values.reshape(-1, CH, values.shape[1])
    return jnp.einsum("ts,csh->cth", tri, parts, precision=lax.Precision.HIGHEST).reshape(values.shape)


def token_tables(g, b, pad, lag_valid, resets):
    t, heads = g.shape
    sums = in_chunks(jnp.concatenate([g, resets[:, None]], axis=1), False)
    cg, count = sums[:, :heads], sums[:, heads:]
    ends = sums.reshape(-1, CH, heads + 1)[:, -1:]
    ends = jnp.broadcast_to(ends, (ends.shape[0], CH, heads + 1)).reshape(t, heads + 1)
    fs = jnp.where(count == 0, jnp.exp(cg), 0.0)
    to_end = count == ends[:, heads:]
    lr = jnp.where(to_end, jnp.exp(jnp.where(to_end, ends[:, :heads] - cg, 0.0)), 0.0)
    aux = jnp.concatenate([lag_valid[1:].T, pad[:, None], count, cg, fs, lr, b], axis=1)
    rows = jnp.concatenate([count, cg], axis=1).reshape(-1, CH, heads + 1).transpose(0, 2, 1)
    return (aux, rows)


class Line:
    def __init__(self, n, pieces, part, red, fin, sems):
        self.n, self.pieces, self.part, self.red, self.fin = n, pieces, part, red, fin
        self.rs_send, self.rs_recv, self.bc_send, self.bc_recv = sems
        self.half_rows = part.shape[0] // 2
        self.rows = self.half_rows // pieces
        self.rank = lax.axis_index("mp")

    def pos(self, half):
        return self.rank if half == 0 else self.n - 1 - self.rank

    def fwd(self, half):
        return {"mp": self.rank + 1 if half == 0 else self.rank - 1}

    def bwd(self, half):
        return {"mp": self.rank - 1 if half == 0 else self.rank + 1}

    def spot(self, half, j):
        return pl.multiple_of(half * self.half_rows + j * self.rows, self.rows)

    def first(self, half, j):
        return pltpu.make_async_remote_copy(
            self.part.at[pl.ds(self.spot(half, j), self.rows), :], self.red.at[half, j],
            self.rs_send.at[half, j], self.rs_recv.at[half, j], device_id=self.fwd(half))

    def onward(self, half, j):
        return pltpu.make_async_remote_copy(
            self.red.at[half, j], self.red.at[half, j],
            self.rs_send.at[half, j], self.rs_recv.at[half, j], device_id=self.fwd(half))

    def back(self, half, j):
        return pltpu.make_async_remote_copy(
            self.fin.at[half, j], self.fin.at[half, j],
            self.bc_send.at[half, j], self.bc_recv.at[half, j], device_id=self.bwd(half))

    def greet(self, dp_others=()):
        barrier = pltpu.get_barrier_semaphore()
        more = len(dp_others)
        for other in dp_others:
            pl.semaphore_signal(barrier, inc=1, device_id={"dp": other})

        @pl.when(self.rank > 0)
        def _():
            pl.semaphore_signal(barrier, inc=1, device_id={"mp": self.rank - 1})

        @pl.when(self.rank < self.n - 1)
        def _():
            pl.semaphore_signal(barrier, inc=1, device_id={"mp": self.rank + 1})

        @pl.when((self.rank > 0) & (self.rank < self.n - 1))
        def _():
            pl.semaphore_wait(barrier, 2 + more)

        @pl.when((self.rank == 0) | (self.rank == self.n - 1))
        def _():
            pl.semaphore_wait(barrier, 1 + more)

    def run(self, finish):
        n, m = self.n, self.pieces

        @pl.loop(0, m + 2 * (n - 1))
        def _(step):
            for half in (0, 1):
                pos = self.pos(half)
                j = step - pos

                @pl.when((j >= 0) & (j < m))
                def _(half=half, pos=pos, j=j):
                    @pl.when(pos == 0)
                    def _():
                        self.first(half, j).start()

                    @pl.when(pos > 0)
                    def _():
                        self.onward(half, j).wait_recv()

                    @pl.when((pos > 0) & (pos < n - 1))
                    def _():
                        own = self.part[pl.ds(self.spot(half, j), self.rows), :]
                        self.red[half, j] = (self.red[half, j].astype(f32) + own.astype(f32)).astype(bf16)
                        self.onward(half, j).start()

                    @pl.when(pos == n - 1)
                    def _():
                        own = self.part[pl.ds(self.spot(half, j), self.rows), :]
                        self.fin[half, j] = (self.red[half, j].astype(f32) + own.astype(f32)).astype(bf16)
                        self.back(half, j).start()
                        finish(self, half, j)

            for half in (0, 1):
                pos = self.pos(half)
                j = step - (n - 1) - (n - 1 - pos)

                @pl.when((j >= 0) & (j < m) & (pos < n - 1))
                def _(half=half, pos=pos, j=j):
                    self.back(half, j).wait_recv()

                    @pl.when(pos > 0)
                    def _():
                        self.back(half, j).start()

                    finish(self, half, j)

        @pl.loop(0, m)
        def _(j):
            for half in (0, 1):
                pos = self.pos(half)

                @pl.when(pos < n - 1)
                def _(half=half):
                    self.onward(half, j).wait_send()

                @pl.when(pos > 0)
                def _(half=half):
                    self.back(half, j).wait_send()


SUB = 16


def sub_rows(line, half, j, body):
    @pl.loop(0, line.rows // SUB)
    def _(i):
        inner = pl.ds(pl.multiple_of(i * SUB, SUB), SUB)
        outer = pl.ds(pl.multiple_of(line.spot(half, j) + i * SUB, SUB), SUB)
        body(line.fin[half, j, inner, :].astype(f32), outer)


def norm_scale(values):
    return lax.rsqrt(jnp.mean(values * values, axis=-1, keepdims=True) + 1e-06)


def kernel_hidden(n, pieces, part, x_in, gain, hidden, normed, red, fin, rs_send, rs_recv, bc_send, bc_recv, sums):
    line = Line(n, pieces, part, red, fin, (rs_send, rs_recv, bc_send, bc_recv))
    line.greet()

    def finish(line, half, j):
        def body(total, at):
            h = x_in[at, :].astype(f32) + total
            hidden[at, :] = h
            normed[at, :] = (h * norm_scale(h) * gain[0:1, :]).astype(bf16)

        sub_rows(line, half, j, body)

    line.run(finish)


def norm_back_rows(u, gain, grad, sums, at):
    scale = norm_scale(u)
    unit = u * scale
    sums[pl.ds(at.start // SUB, 1), :] = jnp.sum(grad * unit, axis=0, keepdims=True)
    scaled = grad * gain
    return scale * (scaled - unit * jnp.mean(scaled * unit, axis=-1, keepdims=True))


def kernel_dhidden(n, pieces, part, hidden, cot, gain, dhidden, dattn, dgain, red, fin, rs_send, rs_recv, bc_send, bc_recv, sums):
    line = Line(n, pieces, part, red, fin, (rs_send, rs_recv, bc_send, bc_recv))
    line.greet()

    def finish(line, half, j):
        def body(total, at):
            dh = cot[at, :].astype(f32) + norm_back_rows(hidden[at, :], gain[0:1, :], total, sums, at)
            dhidden[at, :] = dh
            dattn[at, :] = dh.astype(bf16)

        sub_rows(line, half, j, body)

    line.run(finish)
    dgain[0:1, :] = jnp.sum(sums[...], axis=0, keepdims=True)


def kernel_dinput(n, pieces, dp, part, x_in, dhidden, gain, dgain_two, dinput, dgains, red, fin, rs_send, rs_recv,
                  bc_send, bc_recv, sums, src, dst, g_send, g_recv):
    line = Line(n, pieces, part, red, fin, (rs_send, rs_recv, bc_send, bc_recv))
    me = lax.axis_index("dp")
    others = [lax.rem(me + i, dp) for i in range(dp)]
    line.greet(others[1:])

    def finish(line, half, j):
        def body(total, at):
            dx = norm_back_rows(x_in[at, :].astype(f32), gain[0:1, :], total, sums, at)
            dinput[at, :] = dhidden[at, :] + dx

        sub_rows(line, half, j, body)

    line.run(finish)
    cols = src.shape[2]
    one = jnp.sum(sums[...], axis=0, keepdims=True)
    for p in range(dp):
        src[p, 0:1, :] = one[:, p * cols : (p + 1) * cols]
        src[p, 1:2, :] = dgain_two[0:1, p * cols : (p + 1) * cols]

    def swap(i):
        return pltpu.make_async_remote_copy(
            src.at[others[i]], dst.at[me], g_send.at[i], g_recv.at[i], device_id={"dp": others[i]})

    for i in range(1, dp):
        swap(i).start()
    dst[me] = src[me]
    for i in range(1, dp):
        swap(i).wait()
    total = dst[0]
    for p in range(1, dp):
        total = total + dst[p]
    dgains[...] = total


PIECES = 16


def line_call(kernel, cid, name, n, part, ins, outs, extra=()):
    tokens, width = part.shape
    pieces = PIECES
    rows = tokens // 2 // pieces
    vmem = pl.BlockSpec(memory_space=pltpu.VMEM)
    return pl.pallas_call(
        partial(kernel, n, pieces),
        in_specs=[vmem] * (1 + len(ins)),
        out_specs=[vmem] * len(outs),
        out_shape=outs,
        scratch_shapes=[pltpu.VMEM((2, pieces, rows, width), bf16)] * 2
        + [pltpu.SemaphoreType.DMA((2, pieces))] * 4
        + [pltpu.VMEM((tokens // SUB, width), f32)]
        + list(extra),
        compiler_params=pltpu.CompilerParams(
            collective_id=cid, has_side_effects=True, vmem_limit_bytes=VLIM),
        cost_estimate=cost(120),
        name=name,
    )(part, *ins)


def from_behind(value, axis, by):
    length = lax.axis_size(axis)
    pairs = [(i, i + by) for i in range(length) if 0 <= i + by < length]
    return lax.ppermute(value, axis, pairs)


def norm_rows(values, gain):
    return values * lax.rsqrt(jnp.mean(values * values, axis=-1, keepdims=True) + 1e-06) * gain


class HalvingSum:
    def __init__(self, value, axis):
        self.value, self.axis = value, axis
        self.n, self.rank = lax.axis_size(axis), lax.axis_index(axis)
        bits = [1 << i for i in range(self.n.bit_length() - 1)]
        self.todo = [(self.halve, b) for b in bits] + [(self.double, b) for b in reversed(bits)]

    def swap(self, value, bit):
        return lax.ppermute(value, self.axis, [(i, i ^ bit) for i in range(self.n)])

    def halve(self, bit):
        half = self.value.shape[0] // 2
        up = (self.rank & bit) // bit
        kept = lax.dynamic_slice_in_dim(self.value, up * half, half)
        got = self.swap(lax.dynamic_slice_in_dim(self.value, (1 - up) * half, half), bit)
        self.value = (kept.astype(f32) + got.astype(f32)).astype(bf16)

    def double(self, bit):
        up = (self.rank & bit) != 0
        got = self.swap(self.value, bit)
        self.value = jnp.concatenate([jnp.where(up, got, self.value), jnp.where(up, self.value, got)])

    def step(self):
        if self.todo:
            act, bit = self.todo.pop(0)
            act(bit)

    def tie(self, *others):
        self.value, *others = lax.optimization_barrier((self.value, *others))
        return others


def partial_kernel_dinput(dp):
    def kernel(n, pieces, *refs):
        kernel_dinput(n, pieces, dp, *refs)

    return kernel


def dot(a, b, dims=NN, out=f32):
    return lax.dot_general(a, b, dims, preferred_element_type=out)


adam_step = 10.0


def rowwise(value):
    return with_layout_constraint(value, Layout(major_to_minor=tuple(range(value.ndim))))


def adamw(weight, grad, first, second, rate, shrink):
    grad = grad.astype(f32)
    first = 0.9 * first + 0.1 * grad
    second = 0.999 * second + 0.001 * grad * grad
    first_hat = first / (1.0 - 0.9**adam_step)
    second_hat = second / (1.0 - 0.999**adam_step)
    weight = weight - rate * (first_hat / (jnp.sqrt(second_hat) + 1e-08) + shrink * weight)
    return [weight, first, second]


def on_device(tokens_in, cotangent, segment_ids, pad_mask, *state):
    masters, firsts, seconds = state[0::3], state[1::3], state[2::3]
    (qk_proj, vg_proj, ab_proj, out_proj, gu_proj, down_proj,
     norm_gains, qk_conv, v_conv, out_gain, decay_params) = masters
    tokens = tokens_in.shape[0]
    dp = lax.axis_size("dp")
    mine = lax.axis_index("dp")
    start = mine * tokens
    rows = qk_proj.shape[0]
    heads, key, val = qk_proj.shape[2], qk_proj.shape[3], vg_proj.shape[3]
    units = gu_proj.shape[2]
    hk, hv = heads * key, heads * val
    mixer = Mixer(tokens, heads, key, val)

    def low(x):
        return x.astype(bf16)

    small = [norm_gains, qk_conv, v_conv, out_gain]
    flat = jnp.concatenate([low(x).reshape(-1) for x in small])
    small_cols = pl.cdiv(flat.shape[0], rows)
    room = 128 - 2 * heads - small_cols
    flat = jnp.pad(flat, (0, rows * small_cols - flat.shape[0])).reshape(rows, small_cols)
    extra = jnp.concatenate(
        [low(ab_proj).reshape(rows, 2 * heads), flat, jnp.zeros((rows, room), bf16)], axis=1
    )
    vg_low = low(vg_proj)
    shard_one = jnp.concatenate(
        [low(qk_proj).reshape(rows, 2 * hk), vg_low[:, 0].reshape(rows, hv), extra], axis=1
    )
    shard_two = jnp.concatenate(
        [vg_low[:, 1].reshape(rows, hv), low(out_proj).reshape(hv, rows).T], axis=1
    )
    shard_gu = low(gu_proj).reshape(rows, 2 * units)
    shard_down = low(down_proj).T

    def gather(x):
        return lax.all_gather(x, "dp", axis=0, tiled=True)

    def scatter(value):
        return lax.psum_scatter(value, "dp", scatter_dimension=0, tiled=True)

    full_one = gather(shard_one)
    full_two = gather(shard_two)

    cut = 2 * hk + hv
    flats = full_one[:, cut + 2 * heads : cut + 2 * heads + small_cols].reshape(dp, rows * small_cols)
    parts, at = [], 0
    for x in small:
        size = x.size
        parts.append(flats[:, at : at + size].reshape((dp,) + x.shape).astype(f32))
        at += size
    gains = jnp.moveaxis(parts[0], 0, 1).reshape(2, -1)
    taps_qk = jnp.moveaxis(parts[1], 0, 3).reshape(2, CONV, hk)
    taps_qk = jnp.moveaxis(taps_qk, 0, 1).reshape(CONV, 2 * hk)
    taps_v = jnp.moveaxis(parts[2], 0, 2).reshape(CONV, hv)
    gain = jnp.broadcast_to(parts[3].reshape(1, val), (8, val))
    decay_low = lax.optimization_barrier(low(decay_params)).astype(f32)

    padded_ids = jnp.concatenate([jnp.full((4,), -1, jnp.int32), segment_ids])
    here_ids = lax.dynamic_slice_in_dim(padded_ids, start + 1, tokens + SPAN)
    prior_ids = lax.dynamic_slice_in_dim(padded_ids, start, tokens + SPAN)
    positions = start - SPAN + jnp.arange(tokens + SPAN, dtype=jnp.int32)
    resets_ext = ((here_ids != prior_ids) | (positions == 0)).astype(f32)
    resets_here = resets_ext[SPAN:]
    keep_ext = 1.0 - resets_ext
    valid_rows = [jnp.ones((tokens,), f32)]
    for lag in range(1, SPAN + 1):
        valid_rows.append(valid_rows[-1] * keep_ext[SPAN - lag + 1 : SPAN - lag + 1 + tokens])
    lag_valid = jnp.stack(valid_rows)
    pad = lax.dynamic_slice_in_dim(pad_mask, start, tokens).astype(f32)

    x_rim = from_behind(tokens_in[tokens - HALO :], "dp", 1)
    x = tokens_in.astype(f32)
    normed = low(norm_rows(x, gains[0]))
    normed_rim = low(norm_rows(x_rim.astype(f32), gains[0]))
    pre_qk = dot(normed, full_one[:, : 2 * hk], out=bf16)
    pre_v = dot(normed, full_one[:, 2 * hk : cut], out=bf16)
    mixed = dot(normed, full_one[:, cut:])[:, : 2 * heads].reshape(tokens, 2, heads)
    rim = low(dot(normed_rim, full_one[:, :cut])).astype(f32)
    (g, b), pull_gates = jax.vjp(lambda ab, dec: gates_of(ab, dec, pad), mixed, decay_low)
    aux, rowform = token_tables(g, b, pad, lag_valid, resets_here)

    rim_qk, rim_v = rim[:, : 2 * hk], rim[:, 2 * hk :]
    q, k, w, u, p, inv, r, r_end = mixer.forward_local(
        pre_qk, pre_v, rim_qk, rim_v, taps_qk, taps_v, aux, rowform
    )
    spot = mine.astype(jnp.int32).reshape(1)
    r_end, full_two = lax.optimization_barrier((low(r_end), full_two))
    gate_pre = dot(normed, full_two[:, :hv])
    maps = lax.all_gather(r_end, "dp")
    maps, shard_gu, shard_down = lax.optimization_barrier((maps, shard_gu, shard_down))
    full_gu = gather(shard_gu)
    full_down = gather(shard_down)
    y, st, vn, o = mixer.output(spot, maps, r, w, u, p, q, aux, gate_pre, gain)

    out_t = full_two[:, hv:]
    mp = lax.axis_size("mp")
    gain_one, gain_two = (jnp.broadcast_to(gains[i : i + 1], (8, gains.shape[1])) for i in (0, 1))
    like = sds(tokens_in.shape)
    like_low = sds(tokens_in.shape, bf16)
    hidden, normed_two = line_call(
        kernel_hidden, 0, "sum_hidden", mp, dot(y, out_t, NT, bf16), [tokens_in, gain_two], [like, like_low]
    )
    gate_up = dot(normed_two, full_gu)
    gate_two, up_two = gate_up[:, :units], gate_up[:, units:]
    sig = jax.nn.sigmoid(gate_two)
    act = low(gate_two * sig * up_two)
    down_sum = HalvingSum(dot(act, full_down, NT, bf16), "mp")
    down_sum.step()
    grad_act = dot(cotangent, full_down)
    grad_up = grad_act * gate_two * sig
    grad_gate = grad_act * up_two * sig * (1.0 + gate_two * (1.0 - sig))
    grad_gu_in = low(jnp.concatenate([grad_gate, grad_up], axis=1))
    part_two = dot(grad_gu_in, full_gu, NT, bf16)
    grad_down = dot(cotangent, act, TN, bf16)
    grad_gu = dot(normed_two, grad_gu_in, TN, bf16)
    grad_ffn = jnp.concatenate([grad_gu, grad_down], axis=1)
    part_two, grad_ffn = down_sum.tie(part_two, grad_ffn)
    red_ffn = scatter(grad_ffn)
    grad_hidden, dattn, dgain_two = line_call(
        kernel_dhidden, 1, "sum_dhidden", mp, part_two, [hidden, cotangent, gain_two],
        [like, like_low, sds(gain_two.shape)]
    )
    (dattn,) = down_sum.tie(dattn)
    down_sum.step()
    dy = dot(dattn, out_t)
    grad_out = dot(dattn, y, TN, bf16)
    do, dgate, dgain, z, z_end = mixer.backward_local(dy, o, gate_pre, gain, aux, q, k, w, p)
    z_end, red_ffn = lax.optimization_barrier((low(z_end), red_ffn))
    back_maps = lax.all_gather(z_end, "dp")
    grad_gate_w = dot(normed, dgate, TN, bf16)
    grad_two = jnp.concatenate([grad_gate_w, grad_out], axis=1)
    dgain = lax.psum(dgain[0], "mp")
    back_maps, grad_two, dgain = down_sum.tie(back_maps, grad_two, dgain)
    down_sum.step()
    red_two = scatter(grad_two)
    (dqk, dv, tail_qk, tail_v, head_qk, head_v, dtaps_qk, dtaps_v, dcg, dbeta) = mixer.backward(
        spot, back_maps, z, do, st, vn, q, k, w, u, p, inv, aux, rowform,
        pre_qk, pre_v, rim_qk, rim_v, taps_qk, taps_v
    )
    dqk, dv, head_qk, head_v = down_sum.tie(dqk, dv, head_qk, head_v)
    down_sum.step()
    heads_back = from_behind(jnp.concatenate([head_qk, head_v], axis=1), "dp", -1)
    dqk = lax.dynamic_update_slice(dqk, low(tail_qk + heads_back[:, : 2 * hk]), (tokens - HALO, 0))
    dv = lax.dynamic_update_slice(dv, low(tail_v + heads_back[:, 2 * hk :]), (tokens - HALO, 0))
    dmixed, ddecay = pull_gates((in_chunks(dcg, True), dbeta))
    dab = jnp.pad(low(dmixed.reshape(tokens, 2 * heads)), ((0, 0), (0, 128 - 2 * heads)))
    dpre = jnp.concatenate([dqk, dv, dab], axis=1)
    grad_one = dot(normed, dpre, TN, bf16)
    grad_small = [
        dtaps_qk.reshape(CONV, 2, heads, dp, -1).transpose(1, 0, 2, 3, 4),
        dtaps_v.reshape(CONV, heads, dp, -1),
        dgain.reshape(dp, -1),
    ]
    grad_flat = jnp.concatenate(
        [jnp.moveaxis(gs, -2, 0).reshape(dp, -1) for gs in grad_small], axis=1
    )
    high = low(ddecay).astype(f32)
    pair = jnp.stack([high, ddecay - high]).reshape(1, 1, -1)
    slots = jnp.where(jnp.arange(dp)[None, :, None] == mine, pair, 0.0)
    slots = jnp.broadcast_to(slots, (dp,) + slots.shape[1:]).reshape(dp, -1)
    used = grad_flat.shape[1]
    grad_flat = jnp.concatenate([grad_flat, slots], axis=1)
    grad_flat = jnp.pad(grad_flat, ((0, 0), (0, rows * small_cols - grad_flat.shape[1])))
    grad_flat = low(grad_flat).reshape(dp * rows, small_cols)
    grad_one = lax.dynamic_update_slice(grad_one, grad_flat, (0, cut + 2 * heads))
    grad_one, dpre = lax.optimization_barrier((grad_one, dpre))
    red_one = scatter(grad_one)
    normed_part = low(dot(dpre, full_one, NT) + dot(dgate, full_two[:, :hv], NT))
    while down_sum.todo:
        down_sum.step()
    (normed_part,) = down_sum.tie(normed_part)
    block_out = low(hidden + down_sum.value.astype(f32))
    input_grad, dgains = line_call(
        partial_kernel_dinput(dp), 2, "sum_dinput", mp, normed_part, [tokens_in, grad_hidden, gain_one, dgain_two],
        [like, sds((8, rows))],
        [pltpu.VMEM((dp, 8, rows), f32)] * 2 + [pltpu.SemaphoreType.DMA((dp,))] * 2,
    )
    red_flat = red_one[:, cut + 2 * heads : cut + 2 * heads + small_cols].astype(f32).reshape(-1)
    red_small, at = [dgains[:2]], 0
    for s in small[1:]:
        red_small.append(red_flat[at : at + s.size].reshape(s.shape))
        at += s.size
    slots = red_flat[used : used + slots.shape[1]].reshape((dp, 2) + ddecay.shape)
    grads = [
        red_one[:, : 2 * hk].reshape(qk_proj.shape),
        jnp.stack([red_one[:, 2 * hk : cut].reshape(rows, heads, val),
                   red_two[:, :hv].reshape(rows, heads, val)], axis=1),
        red_one[:, cut : cut + 2 * heads].reshape(ab_proj.shape),
        rowwise(red_two[:, hv:].T).reshape(out_proj.shape),
        red_ffn[:, : 2 * units].reshape(gu_proj.shape),
        rowwise(red_ffn[:, 2 * units :].T),
    ] + red_small + [jnp.sum(slots, axis=(0, 1))]
    matrix_rate = 2.5 * D ** (-0.5)
    rates = [matrix_rate] * 6 + [0.5, 1.0, 1.0, 0.5, 2.0]
    shrinks = [0.1] * 6 + [0.0] * 5
    updates = []
    for i in range(11):
        updates += adamw(masters[i], grads[i], firsts[i], seconds[i], rates[i], shrinks[i])
    copies = [low(updates[3 * i]) for i in range(6)]
    return (block_out, input_grad, *updates, *copies)


def solution(mesh):
    weights = [
        P("dp", None, "mp", None),
        P("dp", None, "mp", None),
        P("dp", None, "mp"),
        P("mp", None, "dp"),
        P("dp", None, "mp"),
        P("mp", "dp"),
        P(None, "dp"),
        P(None, None, "mp", "dp"),
        P(None, "mp", "dp"),
        P("dp"),
        P(None, "mp"),
    ]
    thrice = tuple(w for w in weights for _ in range(3))
    rowwise = P("dp", None)
    return jax.shard_map(
        on_device,
        mesh=mesh,
        in_specs=(rowwise, rowwise, P(), P()) + thrice,
        out_specs=(rowwise, rowwise) + thrice + tuple(weights[:6]),
        check_vma=False,
    )
```

```python
from functools import partial

import jax
import jax.numpy as jnp
from jax import lax
from jax.experimental import pallas as pl
from jax.experimental.layout import Layout, with_layout_constraint
from jax.experimental.pallas import tpu as pltpu
from jax.sharding import PartitionSpec as P

D = 2048
CONV = 4
SPAN = CONV - 1
CH = 128
HALO = 8
f32 = jnp.float32
bf16 = jnp.bfloat16
VLIM = 56 * 2**20

NN = (((1,), (0,)), ((), ()))
NT = (((1,), (1,)), ((), ()))
TN = (((0,), (0,)), ((), ()))

N_INV = 3
N_FWD = 1
N_SCAN = 1
N_BWD = 1


def mm(a, b, dims=NN, passes=1):
    def dot(x, y):
        return lax.dot_general(x, y, dims, preferred_element_type=f32)

    ah, bh = a.astype(bf16), b.astype(bf16)
    out = dot(ah, bh)
    if passes == 3:
        al = (a - ah.astype(f32)).astype(bf16)
        bl = (b - bh.astype(f32)).astype(bf16)
        out = out + (dot(ah, bl) + dot(al, bh))
    return out


def grid_iotas(n):
    return (
        lax.broadcasted_iota(jnp.int32, (n, n), 0),
        lax.broadcasted_iota(jnp.int32, (n, n), 1),
    )


def unit_lower_inverse(lowers, n):
    rows, cols = grid_iotas(n)
    eye = (rows == cols).astype(f32)
    small = lax.shift_right_logical(rows, 3) == lax.shift_right_logical(cols, 3)
    diag = [jnp.where(small, low, 0.0) for low in lowers]
    two = [mm(d, d, NN, N_INV) for d in diag]
    four = [mm(t, t, NN, N_INV) for t in two]
    inv = [eye - d for d in diag]
    inv = [x + mm(x, t, NN, N_INV) for x, t in zip(inv, two)]
    inv = [x + mm(x, f, NN, N_INV) for x, f in zip(inv, four)]
    bits = 3
    while (1 << bits) < n:
        wide = lax.shift_right_logical(rows, bits + 1) == lax.shift_right_logical(cols, bits + 1)
        fine = lax.shift_right_logical(rows, bits) != lax.shift_right_logical(cols, bits)
        off = [jnp.where(wide & fine, low, 0.0) for low in lowers]
        half = [mm(x, o, NN, N_INV) for x, o in zip(inv, off)]
        inv = [x - mm(y, x, NN, N_INV) for x, y in zip(inv, half)]
        bits += 1
    return inv


def sigmoid(x):
    return 1.0 / (1.0 + jnp.exp(-x))


def decay_matrix(aux, rows, h, heads, tri):
    cg = aux[:, 5 + h : 6 + h]
    cg_row = rows[1 + h : 2 + h, :]
    same = (aux[:, 4:5] == rows[0:1, :]) & tri
    return jnp.where(same, jnp.exp(jnp.where(same, cg - cg_row, 0.0)), 0.0)


def conv_of(ext_ref, taps_ref, aux, c0, c1):
    n = aux.shape[0]
    total = ext_ref[HALO : HALO + n, c0:c1] * taps_ref[SPAN : SPAN + 1, c0:c1]
    for lag in range(1, SPAN + 1):
        total = total + ext_ref[HALO - lag : HALO - lag + n, c0:c1] * (
            taps_ref[SPAN - lag : SPAN - lag + 1, c0:c1] * aux[:, lag - 1 : lag]
        )
    return total


def unit_of(act):
    return lax.rsqrt(jnp.sum(act * act, axis=-1, keepdims=True) + 1e-06)


def kernel_a(heads, key, val, pqk, pv, hqk, hv, tqk, tv, aux_ref, rows_ref,
             q_out, k_out, w_out, u_out, p_out, t_out, r_out, rend_out,
             xqk, xv, state):
    c = pl.program_id(0)
    n = pqk.shape[0]
    hk = heads * key

    @pl.when(c == 0)
    def _():
        xqk[0:HALO, :] = hqk[...]
        xv[0:HALO, :] = hv[...]
        r, s = (lax.broadcasted_iota(jnp.int32, (key, key + val), i) for i in (0, 1))
        for h in range(heads):
            state[h] = (r == s).astype(f32)

    xqk[HALO:, :] = pqk[...].astype(f32)
    xv[HALO:, :] = pv[...].astype(f32)
    aux = aux_ref[...]
    rows = rows_ref[0]
    ti, si = grid_iotas(n)
    tri = ti >= si
    lowers, queries, keys = [], [], []
    for h in range(heads):
        uq = conv_of(xqk, tqk, aux, h * key, (h + 1) * key)
        uk = conv_of(xqk, tqk, aux, hk + h * key, hk + (h + 1) * key)
        aq = uq * sigmoid(uq)
        ak = uk * sigmoid(uk)
        q = aq * unit_of(aq) * key ** (-0.5)
        k = ak * unit_of(ak)
        q_out[:, h * key : (h + 1) * key] = q
        k_out[:, h * key : (h + 1) * key] = k
        dec = decay_matrix(aux, rows, h, heads, tri)
        beta = aux[:, 5 + 3 * heads + h : 6 + 3 * heads + h]
        p_out[:, h * n : (h + 1) * n] = mm(q, k, NT, N_FWD) * dec
        lowers.append(jnp.where(ti > si, mm(k, k, NT, N_INV) * dec, 0.0) * beta)
        queries.append(q)
        keys.append(k)
    invs = unit_lower_inverse(lowers, n)
    for h in range(heads):
        k = keys[h]
        beta = aux[:, 5 + 3 * heads + h : 6 + 3 * heads + h]
        fs = aux[:, 5 + heads + h : 6 + heads + h]
        lr = aux[:, 5 + 2 * heads + h : 6 + 2 * heads + h]
        uv = conv_of(xv, tv, aux, h * val, (h + 1) * val)
        v = uv * sigmoid(uv)
        t_out[:, h * n : (h + 1) * n] = invs[h]
        w = mm(invs[h], (beta * fs) * k, NN, N_FWD)
        u = mm(invs[h], beta * v, NN, N_FWD)
        w_out[:, h * key : (h + 1) * key] = w
        u_out[:, h * val : (h + 1) * val] = u
        st = state[h]
        r_out[0, h] = st
        new = jnp.concatenate([jnp.zeros((n, key), f32), u], axis=1) - mm(w, st, NN, N_SCAN)
        st = fs[n - 1 :, :] * st + mm(lr * k, new, TN, N_SCAN)
        state[h] = st
        rend_out[h] = st
    xqk[0:HALO, :] = xqk[n:, :]
    xv[0:HALO, :] = xv[n:, :]


def kernel_b(heads, key, val, mine, gath, r_in, w_in, u_in, p_in, q_in, aux_ref, gate_in, gain_ref,
             y_out, s_out, vn_out, o_out, start):
    c = pl.program_id(0)
    n = w_in.shape[0]

    @pl.when(c == 0)
    def _():
        start[...] = jnp.zeros_like(start)

        @pl.loop(0, mine[0])
        def _(d):
            for h in range(heads):
                start[h] = gath[d, h, :, key:].astype(f32) + mm(gath[d, h, :, :key], start[h], NN, N_FWD)

    aux = aux_ref[...]
    pad = aux[:, 3:4]
    for h in range(heads):
        fs = aux[:, 5 + heads + h : 6 + heads + h]
        st = r_in[0, h, :, key:] + mm(r_in[0, h, :, :key], start[h], NN, N_FWD)
        s_out[0, h] = st
        v0, v1 = h * val, (h + 1) * val
        new = u_in[:, v0:v1] - mm(w_in[:, h * key : (h + 1) * key], st, NN, N_FWD)
        vn_out[:, v0:v1] = new
        o = mm(fs * q_in[:, h * key : (h + 1) * key], st, NN, N_FWD)
        o = o + mm(p_in[:, h * n : (h + 1) * n], new, NN, N_FWD)
        o_out[:, v0:v1] = o
        scale = lax.rsqrt(jnp.mean(o * o, axis=-1, keepdims=True) + 1e-05)
        gate = gate_in[:, v0:v1]
        y = o * scale * gain_ref[0:1, :] * (gate * sigmoid(gate)) * pad
        y_out[:, v0:v1] = y.astype(bf16)


def kernel_c(heads, key, val, dy_in, o_in, gate_in, gain_ref, aux_ref, q_in, k_in, w_in, p_in,
             do_out, dgate_out, dgain_out, z_out, zend_out, carry):
    c = pl.program_id(0)
    n = dy_in.shape[0]

    @pl.when(c == 0)
    def _():
        r, s = (lax.broadcasted_iota(jnp.int32, (key, key + val), i) for i in (0, 1))
        for h in range(heads):
            carry[h] = (r == s).astype(f32)
        dgain_out[...] = jnp.zeros_like(dgain_out)

    aux = aux_ref[...]
    pad = aux[:, 3:4]
    gain = gain_ref[0:1, :]
    for h in range(heads):
        v0, v1 = h * val, (h + 1) * val
        k0, k1 = h * key, (h + 1) * key
        fs = aux[:, 5 + heads + h : 6 + heads + h]
        lr = aux[:, 5 + 2 * heads + h : 6 + 2 * heads + h]
        o = o_in[:, v0:v1]
        gate = gate_in[:, v0:v1]
        dy = dy_in[:, v0:v1] * pad
        scale = lax.rsqrt(jnp.mean(o * o, axis=-1, keepdims=True) + 1e-05)
        sig = sigmoid(gate)
        act = gate * sig
        unit = o * scale
        prod = dy * unit
        dgain_out[0:1, :] += jnp.sum(prod * act, axis=0, keepdims=True)
        dgate_out[:, v0:v1] = (prod * gain * (sig * (1.0 + gate * (1.0 - sig)))).astype(bf16)
        dn = dy * gain * act
        do = scale * (dn - unit * jnp.mean(dn * unit, axis=-1, keepdims=True))
        do_out[:, v0:v1] = do
        zst = carry[h]
        z_out[0, h] = zst
        lead = jnp.zeros((n, key), f32)
        dnew = jnp.concatenate([lead, mm(p_in[:, h * n : (h + 1) * n], do, TN, N_FWD)], axis=1)
        dnew = dnew + mm(lr * k_in[:, k0:k1], zst, NN, N_SCAN)
        own = jnp.concatenate(
            [jnp.zeros((key, key), f32), mm(fs * q_in[:, k0:k1], do, TN, N_FWD)], axis=1
        )
        zst = fs[n - 1 :, :] * zst + own - mm(w_in[:, k0:k1], dnew, TN, N_SCAN)
        carry[h] = zst
        zend_out[h] = zst


def through_act(u, grad):
    sig = sigmoid(u)
    return grad * (sig * (1.0 + u * (1.0 - sig)))


def kernel_d(heads, key, val, count, mine, gath, z_in, do_in, s_in, vn_in, q_in, k_in, w_in, u_in, p_in, t_in,
             aux_ref, rows_ref, pqk, pv, bqk, bv, hqk, hv, tqk, tv,
             dqk_out, dv_out, tailqk, tailv, headqk, headv, dtqk, dtv, dcg_out, dbeta_out,
             xqk, xv, dxqk, dxv, end):
    c = pl.program_id(0)
    steps = pl.num_programs(0)
    n = do_in.shape[0]
    hk = heads * key

    @pl.when(c == 0)
    def _():
        end[...] = jnp.zeros_like(end)

        @pl.loop(0, count - 1 - mine[0])
        def _(i):
            d = count - 1 - i
            for h in range(heads):
                end[h] = gath[d, h, :, key:].astype(f32) + mm(gath[d, h, :, :key], end[h], NN, N_FWD)

        dxqk[...] = jnp.zeros_like(dxqk)
        dxv[...] = jnp.zeros_like(dxv)
        dtqk[...] = jnp.zeros_like(dtqk)
        dtv[...] = jnp.zeros_like(dtv)

    @pl.when(c < steps - 1)
    def _():
        xqk[0:HALO, :] = bqk[...].astype(f32)[bqk.shape[0] - HALO :]
        xv[0:HALO, :] = bv[...].astype(f32)[bv.shape[0] - HALO :]

    @pl.when(c == steps - 1)
    def _():
        xqk[0:HALO, :] = hqk[...]
        xv[0:HALO, :] = hv[...]

    xqk[HALO:, :] = pqk[...].astype(f32)
    xv[HALO:, :] = pv[...].astype(f32)
    aux = aux_ref[...]
    rows = rows_ref[0]
    ti, si = grid_iotas(n)
    tri = ti >= si
    last = (lax.broadcasted_iota(jnp.int32, (n, 1), 0) == n - 1).astype(f32)
    dxqk[n:, :] = dxqk[0:HALO, :]
    dxv[n:, :] = dxv[0:HALO, :]
    dxqk[0:n, :] = jnp.zeros((n, 2 * hk), f32)
    dxv[0:n, :] = jnp.zeros((n, heads * val), f32)

    def conv_back(du, ext, dext, taps, dtaps, c0, c1):
        for lag in range(SPAN + 1):
            part = du if lag == 0 else du * aux[:, lag - 1 : lag]
            dtaps[SPAN - lag : SPAN - lag + 1, c0:c1] += jnp.sum(
                part * ext[HALO - lag : HALO - lag + n, c0:c1], axis=0, keepdims=True
            )
            spot = slice(HALO - lag, HALO - lag + n)
            dext[spot, c0:c1] += part * taps[SPAN - lag : SPAN - lag + 1, c0:c1]

    for h in range(heads):
        v0, v1 = h * val, (h + 1) * val
        k0, k1 = h * key, (h + 1) * key
        fs = aux[:, 5 + heads + h : 6 + heads + h]
        lr = aux[:, 5 + 2 * heads + h : 6 + 2 * heads + h]
        beta = aux[:, 5 + 3 * heads + h : 6 + 3 * heads + h]
        q, k = q_in[:, k0:k1], k_in[:, k0:k1]
        w, u = w_in[:, k0:k1], u_in[:, v0:v1]
        p, inv = p_in[:, h * n : (h + 1) * n], t_in[:, h * n : (h + 1) * n]
        do, new, st = do_in[:, v0:v1], vn_in[:, v0:v1], s_in[0, h]
        dst = z_in[0, h, :, key:] + mm(z_in[0, h, :, :key], end[h], NN, N_BWD)
        dec = decay_matrix(aux, rows, h, heads, tri)
        kk = mm(k, k, NT, N_BWD)
        kl = lr * k
        dnew = mm(p, do, TN, N_BWD) + mm(kl, dst, NN, N_BWD)
        dp = mm(do, new, NT, N_BWD)
        dqf = mm(do, st, NT, N_BWD)
        dkl = mm(new, dst, NT, N_BWD)
        dw = -mm(dnew, st, NT, N_BWD)
        drv = mm(inv, dnew, TN, N_BWD)
        drk = mm(inv, dw, TN, N_BWD)
        dlow = -(mm(drv, u, NT, N_BWD) + mm(drk, w, NT, N_BWD))
        dlow = jnp.where(ti > si, dlow, 0.0) * dec
        dkk = dlow * beta
        hh = dp * dec
        pairs = dkk * kk + dp * p
        dq = fs * dqf + mm(hh, k, NN, N_BWD)
        dk = mm(hh, q, TN, N_BWD) + mm(dkk, k, NN, N_BWD) + mm(dkk, k, TN, N_BWD)
        dk = dk + lr * dkl + (beta * fs) * drk
        uv = conv_of(xv, tv, aux, v0, v1)
        v = uv * sigmoid(uv)
        kd = jnp.sum(k * drk, axis=-1, keepdims=True) * fs
        dbeta = jnp.sum(dlow * kk, axis=-1, keepdims=True) + kd
        dbeta = dbeta + jnp.sum(v * drv, axis=-1, keepdims=True)
        leave = lr * jnp.sum(k * dkl, axis=-1, keepdims=True)
        dcg = jnp.sum(pairs, axis=-1, keepdims=True) + beta * kd - leave
        dcg = dcg + fs * jnp.sum(q * dqf, axis=-1, keepdims=True)
        ones = jnp.ones((n, 8), f32)
        dcg = dcg - mm(pairs, ones, TN, 3)[:, 0:1]
        tail = jnp.sum(leave, axis=0, keepdims=True) + fs[n - 1 :, :] * jnp.sum(
            jnp.sum(st * dst, axis=-1, keepdims=True), axis=0, keepdims=True
        )
        dcg_out[:, h : h + 1] = dcg + last * tail
        dbeta_out[:, h : h + 1] = dbeta
        conv_back(through_act(uv, beta * drv), xv, dxv, tv, dtv, v0, v1)
        for off, grad, size in ((0, dq, key ** (-0.5)), (hk, dk, 1.0)):
            uu = conv_of(xqk, tqk, aux, off + k0, off + k1)
            act = uu * sigmoid(uu)
            rs = unit_of(act)
            da = (rs * size) * (grad - act * (rs * rs) * jnp.sum(act * grad, axis=-1, keepdims=True))
            conv_back(through_act(uu, da), xqk, dxqk, tqk, dtqk, off + k0, off + k1)
    dqk_out[...] = dxqk[HALO:, :].astype(bf16)
    dv_out[...] = dxv[HALO:, :].astype(bf16)

    @pl.when(c == 0)
    def _():
        tailqk[...] = dxqk[n:, :]
        tailv[...] = dxv[n:, :]

    headqk[...] = dxqk[0:HALO, :]
    headv[...] = dxv[0:HALO, :]


def cost(microseconds):
    return pl.CostEstimate(
        flops=int(microseconds * 1e9), bytes_accessed=int(microseconds * 3.3e6), transcendentals=0)


def params(**kw):
    return pltpu.CompilerParams(vmem_limit_bytes=VLIM, dimension_semantics=("arbitrary",), **kw)


def sds(shape, dtype=f32):
    return jax.ShapeDtypeStruct(shape, dtype)


class Mixer:
    def __init__(self, tokens, heads, key, val):
        self.sizes = (heads, key, val)
        self.tokens, self.n, self.steps = tokens, CH, tokens // CH

    def rows(self, width, back=False):
        m = self.steps - 1
        return pl.BlockSpec((self.n, width), (lambda c: (m - c, 0)) if back else (lambda c: (c, 0)))

    def lead(self, shape, back=False):
        m, rest = self.steps - 1, (0,) * len(shape)
        return pl.BlockSpec((1,) + shape, (lambda c: (m - c,) + rest) if back else (lambda c: (c,) + rest))

    def whole(self, shape):
        rest = (0,) * len(shape)
        return pl.BlockSpec(shape, lambda c: rest)

    def forward_local(self, pqk, pv, hqk, hv, tqk, tv, aux, rows):
        heads, key, val = self.sizes
        t, n, s = self.tokens, self.n, self.steps
        hk, hv_ = heads * key, heads * val
        wide = key + val
        return pl.pallas_call(
            partial(kernel_a, heads, key, val),
            grid=(s,),
            in_specs=[self.rows(2 * hk), self.rows(hv_), self.whole(hqk.shape), self.whole(hv.shape),
                      self.whole(tqk.shape), self.whole(tv.shape), self.rows(aux.shape[1]), self.lead(rows.shape[1:])],
            out_specs=[self.rows(hk), self.rows(hk), self.rows(hk), self.rows(hv_), self.rows(heads * n), self.rows(heads * n),
                       self.lead((heads, key, wide)), self.whole((heads, key, wide))],
            out_shape=[sds((t, hk)), sds((t, hk)), sds((t, hk)), sds((t, hv_)), sds((t, heads * n)), sds((t, heads * n)),
                       sds((s, heads, key, wide)), sds((heads, key, wide))],
            scratch_shapes=[pltpu.VMEM((HALO + n, 2 * hk), f32), pltpu.VMEM((HALO + n, hv_), f32),
                            pltpu.VMEM((heads, key, wide), f32)],
            compiler_params=params(),
            cost_estimate=cost(39),
            name="mixer_local",
        )(pqk, pv, hqk, hv, tqk, tv, aux, rows)

    def output(self, mine, gath, r, w, u, p, q, aux, gate, gain):
        heads, key, val = self.sizes
        t, n, s = self.tokens, self.n, self.steps
        hk, hv_ = heads * key, heads * val
        return pl.pallas_call(
            partial(kernel_b, heads, key, val),
            grid=(s,),
            in_specs=[pl.BlockSpec(memory_space=pltpu.SMEM), self.whole(gath.shape), self.lead((heads, key, key + val)),
                      self.rows(hk), self.rows(hv_), self.rows(heads * n), self.rows(hk), self.rows(aux.shape[1]),
                      self.rows(hv_), self.whole(gain.shape)],
            out_specs=[self.rows(hv_), self.lead((heads, key, val)), self.rows(hv_), self.rows(hv_)],
            out_shape=[sds((t, hv_), bf16), sds((s, heads, key, val)), sds((t, hv_)), sds((t, hv_))],
            scratch_shapes=[pltpu.VMEM((heads, key, val), f32)],
            compiler_params=params(),
            cost_estimate=cost(18),
            name="mixer_output",
        )(mine, gath, r, w, u, p, q, aux, gate, gain)

    def backward_local(self, dy, o, gate, gain, aux, q, k, w, p):
        heads, key, val = self.sizes
        t, n, s = self.tokens, self.n, self.steps
        hk, hv_ = heads * key, heads * val
        wide = key + val
        back = partial(self.rows, back=True)
        return pl.pallas_call(
            partial(kernel_c, heads, key, val),
            grid=(s,),
            in_specs=[back(hv_), back(hv_), back(hv_), self.whole(gain.shape), back(aux.shape[1]),
                      back(hk), back(hk), back(hk), back(heads * n)],
            out_specs=[back(hv_), back(hv_), self.whole((8, val)), self.lead((heads, key, wide), True),
                       self.whole((heads, key, wide))],
            out_shape=[sds((t, hv_)), sds((t, hv_), bf16), sds((8, val)), sds((s, heads, key, wide)),
                       sds((heads, key, wide))],
            scratch_shapes=[pltpu.VMEM((heads, key, wide), f32)],
            compiler_params=params(),
            cost_estimate=cost(17),
            name="mixer_back_local",
        )(dy, o, gate, gain, aux, q, k, w, p)

    def backward(self, mine, gath, z, do, st, vn, q, k, w, u, p, inv, aux, rows, pqk, pv, hqk, hv, tqk, tv):
        heads, key, val = self.sizes
        t, n, s = self.tokens, self.n, self.steps
        hk, hv_ = heads * key, heads * val
        back = partial(self.rows, back=True)
        ratio = n // 16
        m = s - 1

        def before(width):
            return pl.BlockSpec((16, width), lambda c: (jnp.maximum((m - c) * ratio - 1, 0), 0))

        return pl.pallas_call(
            partial(kernel_d, heads, key, val, gath.shape[0]),
            grid=(s,),
            in_specs=[pl.BlockSpec(memory_space=pltpu.SMEM), self.whole(gath.shape), self.lead((heads, key, key + val), True),
                      back(hv_), self.lead((heads, key, val), True), back(hv_), back(hk), back(hk), back(hk), back(hv_),
                      back(heads * n), back(heads * n), back(aux.shape[1]), self.lead(rows.shape[1:], True),
                      back(2 * hk), back(hv_), before(2 * hk), before(hv_), self.whole(hqk.shape), self.whole(hv.shape),
                      self.whole(tqk.shape), self.whole(tv.shape)],
            out_specs=[back(2 * hk), back(hv_), self.whole((HALO, 2 * hk)), self.whole((HALO, hv_)),
                       self.whole((HALO, 2 * hk)), self.whole((HALO, hv_)), self.whole((CONV, 2 * hk)), self.whole((CONV, hv_)),
                       back(heads), back(heads)],
            out_shape=[sds((t, 2 * hk), bf16), sds((t, hv_), bf16), sds((HALO, 2 * hk)), sds((HALO, hv_)),
                       sds((HALO, 2 * hk)), sds((HALO, hv_)), sds((CONV, 2 * hk)), sds((CONV, hv_)),
                       sds((t, heads)), sds((t, heads))],
            scratch_shapes=[pltpu.VMEM((HALO + n, 2 * hk), f32), pltpu.VMEM((HALO + n, hv_), f32),
                            pltpu.VMEM((HALO + n, 2 * hk), f32), pltpu.VMEM((HALO + n, hv_), f32),
                            pltpu.VMEM((heads, key, val), f32)],
            compiler_params=params(),
            cost_estimate=cost(50),
            name="mixer_back",
        )(mine, gath, z, do, st, vn, q, k, w, u, p, inv, aux, rows, pqk, pv, pqk, pv, hqk, hv, tqk, tv)


def gates_of(mixed_ab, decay, pad):
    g = -jnp.exp(decay[0]) * jax.nn.softplus(mixed_ab[:, 0] + decay[1]) * pad[:, None]
    b = jax.nn.sigmoid(mixed_ab[:, 1]) * pad[:, None]
    return (g, b)


def in_chunks(values, upper):
    tri = jnp.tril(jnp.ones((CH, CH), f32))
    tri = tri.T if upper else tri
    parts = values.reshape(-1, CH, values.shape[1])
    return jnp.einsum("ts,csh->cth", tri, parts, precision=lax.Precision.HIGHEST).reshape(values.shape)


def token_tables(g, b, pad, lag_valid, resets):
    t, heads = g.shape
    sums = in_chunks(jnp.concatenate([g, resets[:, None]], axis=1), False)
    cg, count = sums[:, :heads], sums[:, heads:]
    ends = sums.reshape(-1, CH, heads + 1)[:, -1:]
    ends = jnp.broadcast_to(ends, (ends.shape[0], CH, heads + 1)).reshape(t, heads + 1)
    fs = jnp.where(count == 0, jnp.exp(cg), 0.0)
    to_end = count == ends[:, heads:]
    lr = jnp.where(to_end, jnp.exp(jnp.where(to_end, ends[:, :heads] - cg, 0.0)), 0.0)
    aux = jnp.concatenate([lag_valid[1:].T, pad[:, None], count, cg, fs, lr, b], axis=1)
    rows = jnp.concatenate([count, cg], axis=1).reshape(-1, CH, heads + 1).transpose(0, 2, 1)
    return (aux, rows)


ROWS = 16
HOP = 3
BAND = 128


class Line:
    def __init__(self, n, part, red, fin, sems, gap=0):
        self.n, self.part, self.red, self.fin, self.gap = n, part, red, fin, gap
        self.rs_send, self.rs_recv, self.bc_send, self.bc_recv = sems
        self.batch = part.shape[0] // 2
        self.pieces = self.batch // ROWS
        self.per = self.pieces // 2
        self.rank = lax.axis_index("mp")

    def pos(self, side):
        return self.rank if side == 0 else self.n - 1 - self.rank

    def fwd(self, side):
        return {"mp": self.rank + 1 if side == 0 else self.rank - 1}

    def bwd(self, side):
        return {"mp": self.rank - 1 if side == 0 else self.rank + 1}

    def rows(self, side, j):
        row = lax.div(j, self.per) * self.batch + side * (self.batch // 2) + lax.rem(j, self.per) * ROWS
        return pl.ds(pl.multiple_of(row, ROWS), ROWS)

    def turn(self, step, delay):
        raw = step - delay
        late = raw >= self.per + self.gap
        live = ((raw >= 0) & (raw < self.per)) | (late & (raw < self.pieces + self.gap))
        return jnp.where(late, raw - self.gap, raw), live

    def first(self, side, j):
        return pltpu.make_async_remote_copy(
            self.part.at[self.rows(side, j), :], self.red.at[side, j],
            self.rs_send.at[side, j], self.rs_recv.at[side, j], device_id=self.fwd(side))

    def onward(self, side, j):
        return pltpu.make_async_remote_copy(
            self.red.at[side, j], self.red.at[side, j],
            self.rs_send.at[side, j], self.rs_recv.at[side, j], device_id=self.fwd(side))

    def back(self, side, j):
        at = self.rows(side, j)
        return pltpu.make_async_remote_copy(
            self.fin.at[at, :], self.fin.at[at, :],
            self.bc_send.at[side, j], self.bc_recv.at[side, j], device_id=self.bwd(side))

    def greet(self, dp_others=(), mp_others=()):
        barrier = pltpu.get_barrier_semaphore()
        more = len(dp_others) + len(mp_others)
        for other in dp_others:
            pl.semaphore_signal(barrier, inc=1, device_id={"dp": other})
        for other in mp_others:
            pl.semaphore_signal(barrier, inc=1, device_id={"mp": other})
        if mp_others:
            pl.semaphore_wait(barrier, more)
            return

        @pl.when(self.rank > 0)
        def _():
            pl.semaphore_signal(barrier, inc=1, device_id={"mp": self.rank - 1})

        @pl.when(self.rank < self.n - 1)
        def _():
            pl.semaphore_signal(barrier, inc=1, device_id={"mp": self.rank + 1})

        @pl.when((self.rank > 0) & (self.rank < self.n - 1))
        def _():
            pl.semaphore_wait(barrier, 2 + more)

        @pl.when((self.rank == 0) | (self.rank == self.n - 1))
        def _():
            pl.semaphore_wait(barrier, 1 + more)

    def total(self, side, j):
        own = self.part[self.rows(side, j), :]
        return (self.red[side, j].astype(f32) + own.astype(f32)).astype(bf16)

    def run(self, finish, beside=None, least=0):
        n = self.n

        def done(side, j):
            at = self.rows(side, j)
            finish(self.fin[at, :].astype(f32), at)

        @pl.loop(0, max(self.pieces + self.gap + 2 * HOP * (n - 1), least))
        def _(step):
            for side in (0, 1):
                pos = self.pos(side)
                j, live = self.turn(step, HOP * pos)

                @pl.when(live)
                def _(side=side, pos=pos, j=j):
                    @pl.when(pos == 0)
                    def _():
                        self.first(side, j).start()

                    @pl.when(pos > 0)
                    def _():
                        self.onward(side, j).wait_recv()

                    @pl.when((pos > 0) & (pos < n - 1))
                    def _():
                        self.red[side, j] = self.total(side, j)
                        self.onward(side, j).start()

                    @pl.when(pos == n - 1)
                    def _():
                        self.fin[self.rows(side, j), :] = self.total(side, j)
                        self.back(side, j).start()
                        done(side, j)

            for side in (0, 1):
                pos = self.pos(side)
                j, live = self.turn(step, HOP * (n - 1) + HOP * (n - 1 - pos))

                @pl.when(live & (pos < n - 1))
                def _(side=side, pos=pos, j=j):
                    self.back(side, j).wait_recv()

                    @pl.when(pos > 0)
                    def _():
                        self.back(side, j).start()

                    done(side, j)

            if beside is not None:
                beside(step)

        @pl.loop(0, self.pieces)
        def _(j):
            for side in (0, 1):
                pos = self.pos(side)

                @pl.when(pos < n - 1)
                def _(side=side):
                    self.onward(side, j).wait_send()

                @pl.when(pos > 0)
                def _(side=side):
                    self.back(side, j).wait_send()


def norm_scale(values):
    return lax.rsqrt(jnp.mean(values * values, axis=-1, keepdims=True) + 1e-06)


def norm_back_rows(u, gain, grad, sums=None, at=None):
    scale = norm_scale(u)
    unit = u * scale
    if sums is not None:
        sums[pl.ds(lax.div(at.start, ROWS), 1), :] = jnp.sum(grad * unit, axis=0, keepdims=True)
    scaled = grad * gain
    return scale * (scaled - unit * jnp.mean(scaled * unit, axis=-1, keepdims=True))


class FeedForward:
    def __init__(self, refs, begin, batch, arrive=None):
        self.arrive = arrive or self.wait_loads
        (self.normed, self.cot, self.gu_hbm, self.down_hbm, self.act_hbm, self.dgu_hbm, self.down_out, self.part_two,
         self.act, self.dgu, self.down_part, self.gu, self.down, self.sems) = refs
        self.begin, self.batch = begin, batch
        self.count = self.act.shape[0]
        self.bands = self.down.shape[1] // BAND
        self.units = self.bands + self.gu.shape[0] // (2 * BAND)
        self.end = begin + self.units

    def loads(self):
        return [pltpu.make_async_copy(self.gu_hbm, self.gu, self.sems.at[0]),
                pltpu.make_async_copy(self.down_hbm, self.down, self.sems.at[1])]

    def stores(self):
        at = pl.ds(self.batch * self.count, self.count)
        return [pltpu.make_async_copy(self.act, self.act_hbm.at[at, :], self.sems.at[2]),
                pltpu.make_async_copy(self.dgu, self.dgu_hbm.at[at, :], self.sems.at[3]),
                pltpu.make_async_copy(self.down_part, self.down_out.at[at, :], self.sems.at[4])]

    def start(self):
        for load in self.loads():
            load.start()

    def wait_loads(self):
        for load in self.loads():
            load.wait()

    def finish(self):
        for store in self.stores():
            store.start()
        for store in self.stores():
            store.wait()

    def step(self, step):
        at = step - self.begin
        mine = pl.ds(self.batch * self.count, self.count)

        @pl.when(at == 0)
        def _():
            self.arrive()

        @pl.when((at >= 0) & (at < self.bands))
        def _():
            two = pl.ds(pl.multiple_of(at * 2 * BAND, 2 * BAND), 2 * BAND)
            one = pl.ds(pl.multiple_of(at * BAND, BAND), BAND)
            gate_up = lax.dot_general(self.normed[...], self.gu[:, two], NN, preferred_element_type=f32)
            grad = lax.dot_general(self.cot[...], self.down[:, one], NN, preferred_element_type=f32)
            gate, up = gate_up[:, :BAND], gate_up[:, BAND:]
            sig = sigmoid(gate)
            swish = gate * sig
            self.act[:, one] = (swish * up).astype(bf16)
            dgate = grad * up * sig * (1.0 + gate * (1.0 - sig))
            self.dgu[:, two] = jnp.concatenate([dgate, grad * swish], axis=1).astype(bf16)

        @pl.when((at >= self.bands) & (at < self.units))
        def _():
            out = pl.ds(pl.multiple_of((at - self.bands) * 2 * BAND, 2 * BAND), 2 * BAND)
            self.part_two[mine, out] = lax.dot_general(
                self.dgu[...], self.gu[out, :], NT, preferred_element_type=f32).astype(bf16)
            self.down_part[:, out] = lax.dot_general(
                self.act[...], self.down[out, :], NT, preferred_element_type=f32).astype(bf16)


class Gather:
    KINDS = ("own1", "own2", "own0", "one0", "one2", "two0", "two1", "both0a", "both0b")

    def __init__(self, refs):
        self.shards, self.full, self.send, self.recv, self.local = refs[:2], refs[2:4], *refs[4:]
        self.me = lax.axis_index("dp")
        self.count = self.shards[0].shape[0]

    def flip(self, device, bit):
        size = 1 << bit
        return device + size - 2 * size * lax.rem(lax.div(device, size), 2)

    def plan(self, kind, sender):
        one, two = self.flip(sender, 1), self.flip(sender, 2)
        both = self.flip(one, 2)
        return {"own1": (1, sender, 2), "own2": (2, sender, 2), "own0": (0, sender, 2),
                "one0": (0, one, 2), "one2": (2, one, 0), "two0": (0, two, 2), "two1": (1, two, 1),
                "both0a": (0, both, 0), "both0b": (0, both, 1)}[kind]

    def copy(self, kind, array, sending):
        k = self.KINDS.index(kind)
        bit = self.plan(kind, self.me)[0]
        other = self.flip(self.me, bit)
        _, owner, half = self.plan(kind, self.me if sending else other)
        size = self.count if half == 2 else self.count // 2
        start = owner * self.count + (size if half == 1 else 0)
        spot = self.full[array].at[pl.ds(pl.multiple_of(start, size), size), :]
        source = self.shards[array] if sending and kind.startswith("own") else spot
        return pltpu.make_async_remote_copy(
            source, spot, self.send.at[k, array], self.recv.at[k, array], device_id={"dp": other})

    def own(self, array):
        spot = pl.ds(pl.multiple_of(self.me * self.count, self.count), self.count)
        return pltpu.make_async_copy(self.shards[array], self.full[array].at[spot, :], self.local.at[array])

    def partners(self):
        return [self.flip(self.me, bit) for bit in (0, 1, 2)]

    def go(self, *kinds):
        for kind in kinds:
            for array in (0, 1):
                self.copy(kind, array, True).start()

    def come(self, *kinds):
        for kind in kinds:
            for array in (0, 1):
                self.copy(kind, array, False).wait_recv()

    def start(self):
        for array in (0, 1):
            self.own(array).start()
        self.go("own1", "own2", "own0")

    def turn(self):
        self.come("own1", "own2")
        self.go("one2", "two1", "one0", "two0")

    def cross(self):
        self.come("one2", "two1")
        self.go("both0a", "both0b")

    def end(self):
        self.come("own0", "one0", "two0", "both0a", "both0b")
        for array in (0, 1):
            self.own(array).wait()

    def sent(self):
        for kind in self.KINDS:
            for array in (0, 1):
                self.copy(kind, array, True).wait_send()


def kernel_hidden(n, part, x_in, gain, attn, normed, red, fin, rs_send, rs_recv, bc_send, bc_recv, sem):
    line = Line(n, part, red, fin, (rs_send, rs_recv, bc_send, bc_recv))
    line.greet()

    def finish(total, at):
        h = x_in[at, :].astype(f32) + total
        normed[at, :] = (h * norm_scale(h) * gain[0:1, :]).astype(bf16)

    line.run(finish)
    keep = pltpu.make_async_copy(fin, attn, sem)
    keep.start()
    keep.wait()


TURN, CROSS, BEGIN = 22, 33, 38


def kernel_hidden_ffn(n, part, x_in, gain, cot, gu_shard, down_shard,
                      attn, normed, part_two, act_hbm, dgu_hbm, down_out, gu_hbm, down_hbm,
                      red, fin, rs_send, rs_recv, bc_send, bc_recv, sem, act, dgu, down_part, gu, down, sems,
                      g_send, g_recv, g_local):
    line = Line(n, part, red, fin, (rs_send, rs_recv, bc_send, bc_recv))
    half = pl.ds(0, line.batch)
    gather = Gather((gu_shard, down_shard, gu, down, g_send, g_recv, g_local))
    keeps = [pltpu.make_async_copy(gu, gu_hbm, sems.at[0]), pltpu.make_async_copy(down, down_hbm, sems.at[1])]

    def arrive():
        gather.end()
        for keep in keeps:
            keep.start()

    begin = max(BEGIN, line.per + 2 * HOP * (n - 1))
    ffn = FeedForward((normed.at[half, :], cot.at[half, :], gu_hbm, down_hbm, act_hbm, dgu_hbm, down_out, part_two,
                       act, dgu, down_part, gu, down, sems), begin, 0, arrive)
    line.greet(gather.partners())
    gather.start()

    def finish(total, at):
        h = x_in[at, :].astype(f32) + total
        normed[at, :] = (h * norm_scale(h) * gain[0:1, :]).astype(bf16)

    def beside(step):
        @pl.when(step == TURN)
        def _():
            gather.turn()

        @pl.when(step == CROSS)
        def _():
            gather.cross()

        ffn.step(step)

    line.run(finish, beside, ffn.end)
    last = pltpu.make_async_copy(fin, attn, sem)
    last.start()
    ffn.finish()
    gather.sent()
    for keep in keeps:
        keep.wait()
    last.wait()


def kernel_dhidden(n, part, x_in, attn, cot, gain, total_out, dattn, dgain,
                   red, fin, rs_send, rs_recv, bc_send, bc_recv, sem, sums):
    line = Line(n, part, red, fin, (rs_send, rs_recv, bc_send, bc_recv))
    line.greet()

    def finish(total, at):
        h = x_in[at, :].astype(f32) + attn[at, :].astype(f32)
        dh = cot[at, :].astype(f32) + norm_back_rows(h, gain[0:1, :], total, sums, at)
        dattn[at, :] = dh.astype(bf16)

    line.run(finish)
    keep = pltpu.make_async_copy(fin, total_out, sem)
    keep.start()
    dgain[0:1, :] = jnp.sum(sums[...], axis=0, keepdims=True)
    keep.wait()


def kernel_dhidden_ffn(n, two_a, x_in, attn, cot, gain, normed_hbm, gu_hbm, down_hbm, act_in, dgu_in, down_in,
                       total_out, dattn, dgain, act_hbm, dgu_hbm, down_out,
                       red, fin, rs_send, rs_recv, bc_send, bc_recv, sem, sums,
                       part, normed, more, act, dgu, down_part, gu, down, sems):
    line = Line(n, part, red, fin, (rs_send, rs_recv, bc_send, bc_recv))
    half = line.batch
    ffn = FeedForward((normed, cot.at[pl.ds(half, half), :], gu_hbm, down_hbm, act_hbm, dgu_hbm, down_out, part,
                       act, dgu, down_part, gu, down, sems), 1, 1)
    line.gap = max(0, ffn.end - line.per)
    brought = [pltpu.make_async_copy(two_a, part.at[pl.ds(0, half), :], more.at[0]),
               pltpu.make_async_copy(normed_hbm.at[pl.ds(half, half), :], normed, more.at[1])]
    for load in brought:
        load.start()
    ffn.start()
    line.greet()
    for load in brought:
        load.wait()

    def finish(total, at):
        h = x_in[at, :].astype(f32) + attn[at, :].astype(f32)
        dh = cot[at, :].astype(f32) + norm_back_rows(h, gain[0:1, :], total, sums, at)
        dattn[at, :] = dh.astype(bf16)

    line.run(finish, ffn.step, ffn.end)
    keep = pltpu.make_async_copy(fin, total_out, sem)
    keep.start()
    dgain[0:1, :] = jnp.sum(sums[...], axis=0, keepdims=True)
    ffn.finish()
    keep.wait()


def kernel_dinput(dp, n, part, x_in, attn, cot, total_two, gain_one, gain_two, dgain_two, dgate, dinput, dgains,
                  red, fin, rs_send, rs_recv, bc_send, bc_recv, sem, sums,
                  src, dst, g_send, g_recv, gates, m_send, m_recv):
    line = Line(n, part, red, fin, (rs_send, rs_recv, bc_send, bc_recv))
    me = lax.axis_index("dp")
    rank = line.rank
    others = [lax.rem(me + i, dp) for i in range(dp)]
    ranks = [lax.rem(rank + i, n) for i in range(n)]
    line.greet(others[1:], ranks[1:])

    def mp_swap(i):
        return pltpu.make_async_remote_copy(
            dgate, gates.at[rank], m_send.at[i], m_recv.at[i], device_id={"mp": ranks[i]})

    for i in range(1, n):
        mp_swap(i).start()
    gates[rank] = dgate[...]

    def finish(total, at):
        x = x_in[at, :].astype(f32)
        h = x + attn[at, :].astype(f32)
        dh = cot[at, :].astype(f32) + norm_back_rows(h, gain_two[0:1, :], total_two[at, :].astype(f32))
        dinput[at, :] = dh + norm_back_rows(x, gain_one[0:1, :], total, sums, at)

    line.run(finish)
    for i in range(1, n):
        mp_swap(i).wait()
    gate = gates[0]
    for r in range(1, n):
        gate = gate + gates[r]
    cols, val = dgain_two.shape[1] // dp, dgate.shape[1]
    one = jnp.sum(sums[...], axis=0, keepdims=True)
    for p in range(dp):
        src[p, 0:1, :cols] = one[:, p * cols : (p + 1) * cols]
        src[p, 1:2, :cols] = dgain_two[0:1, p * cols : (p + 1) * cols]
        src[p, 2:3, :val] = gate[0:1, :]

    def swap(i):
        return pltpu.make_async_remote_copy(
            src.at[others[i]], dst.at[me], g_send.at[i], g_recv.at[i], device_id={"dp": others[i]})

    for i in range(1, dp):
        swap(i).start()
    dst[me] = src[me]
    for i in range(1, dp):
        swap(i).wait()
    total = dst[0]
    for p in range(1, dp):
        total = total + dst[p]
    dgains[...] = total


def line_call(kernel, cid, name, n, ins, outs, extra=(), away_in=(), away_out=(), aliases=None, sums=True, micros=100):
    tokens, width = outs[0].shape
    pieces = tokens // 2 // ROWS
    vmem = pl.BlockSpec(memory_space=pltpu.VMEM)
    far = pl.BlockSpec(memory_space=pl.ANY)
    return pl.pallas_call(
        partial(kernel, n),
        in_specs=[far if i in away_in else vmem for i in range(len(ins))],
        out_specs=[far if i in away_out else vmem for i in range(len(outs))],
        out_shape=outs,
        scratch_shapes=[pltpu.VMEM((2, pieces, ROWS, width), bf16), pltpu.VMEM((tokens, width), bf16)]
        + [pltpu.SemaphoreType.DMA((2, pieces))] * 4
        + [pltpu.SemaphoreType.DMA]
        + ([pltpu.VMEM((tokens // ROWS, width), f32)] if sums else [])
        + list(extra),
        input_output_aliases=aliases or {},
        compiler_params=pltpu.CompilerParams(
            collective_id=cid, has_side_effects=True, vmem_limit_bytes=VLIM),
        cost_estimate=cost(micros),
        name=name,
    )(*ins)


def from_behind(value, axis, by):
    length = lax.axis_size(axis)
    pairs = [(i, i + by) for i in range(length) if 0 <= i + by < length]
    return lax.ppermute(value, axis, pairs)


def norm_rows(values, gain):
    return values * lax.rsqrt(jnp.mean(values * values, axis=-1, keepdims=True) + 1e-06) * gain


def feed_forward(normed, cot, gu, down):
    units = down.shape[1]
    gate_up = dot(normed, gu)
    gate, up = gate_up[:, :units], gate_up[:, units:]
    sig = jax.nn.sigmoid(gate)
    act = low(gate * sig * up)
    grad = dot(cot, down)
    dgate = grad * up * sig * (1.0 + gate * (1.0 - sig))
    dgu = low(jnp.concatenate([dgate, grad * gate * sig], axis=1))
    return (act, dgu, dot(dgu, gu, NT, bf16), dot(act, down, NT, bf16))


class HalvingSum:
    def __init__(self, value, axis):
        self.value, self.axis = value, axis
        self.n, self.rank = lax.axis_size(axis), lax.axis_index(axis)
        bits = [1 << i for i in range(self.n.bit_length() - 1)]
        self.todo = [(self.halve, b) for b in bits] + [(self.double, b) for b in reversed(bits)]

    def swap(self, value, bit):
        return lax.ppermute(value, self.axis, [(i, i ^ bit) for i in range(self.n)])

    def halve(self, bit):
        half = self.value.shape[0] // 2
        up = (self.rank & bit) // bit
        kept = lax.dynamic_slice_in_dim(self.value, up * half, half)
        got = self.swap(lax.dynamic_slice_in_dim(self.value, (1 - up) * half, half), bit)
        self.value = (kept.astype(f32) + got.astype(f32)).astype(bf16)

    def double(self, bit):
        up = (self.rank & bit) != 0
        got = self.swap(self.value, bit)
        self.value = jnp.concatenate([jnp.where(up, got, self.value), jnp.where(up, self.value, got)])

    def step(self):
        if self.todo:
            act, bit = self.todo.pop(0)
            act(bit)

    def tie(self, *others):
        self.value, *others = lax.optimization_barrier((self.value, *others))
        return others


def low(x):
    return x.astype(bf16)


def dot(a, b, dims=NN, out=f32):
    return lax.dot_general(a, b, dims, preferred_element_type=out)


adam_step = 10.0


def rowwise(value):
    return with_layout_constraint(value, Layout(major_to_minor=tuple(range(value.ndim))))


def adamw(weight, grad, first, second, rate, shrink):
    grad = grad.astype(f32)
    first = 0.9 * first + 0.1 * grad
    second = 0.999 * second + 0.001 * grad * grad
    first_hat = first / (1.0 - 0.9**adam_step)
    second_hat = second / (1.0 - 0.999**adam_step)
    weight = weight - rate * (first_hat / (jnp.sqrt(second_hat) + 1e-08) + shrink * weight)
    return [weight, first, second]


def on_device(tokens_in, cotangent, segment_ids, pad_mask, *state):
    masters, firsts, seconds = state[0::3], state[1::3], state[2::3]
    (qk_proj, vg_proj, ab_proj, out_proj, gu_proj, down_proj,
     norm_gains, qk_conv, v_conv, out_gain, decay_params) = masters
    tokens = tokens_in.shape[0]
    dp = lax.axis_size("dp")
    mine = lax.axis_index("dp")
    start = mine * tokens
    rows = qk_proj.shape[0]
    heads, key, val = qk_proj.shape[2], qk_proj.shape[3], vg_proj.shape[3]
    units = gu_proj.shape[2]
    hk, hv = heads * key, heads * val
    mixer = Mixer(tokens, heads, key, val)

    small = [norm_gains, qk_conv, v_conv, out_gain]
    flat = jnp.concatenate([low(x).reshape(-1) for x in small])
    small_cols = pl.cdiv(flat.shape[0], rows)
    room = 128 - 2 * heads - small_cols
    flat = jnp.pad(flat, (0, rows * small_cols - flat.shape[0])).reshape(rows, small_cols)
    extra = jnp.concatenate(
        [low(ab_proj).reshape(rows, 2 * heads), flat, jnp.zeros((rows, room), bf16)], axis=1
    )
    vg_low = low(vg_proj)
    shard_one = jnp.concatenate(
        [low(qk_proj).reshape(rows, 2 * hk), vg_low[:, 0].reshape(rows, hv), extra], axis=1
    )
    shard_two = jnp.concatenate(
        [vg_low[:, 1].reshape(rows, hv), low(out_proj).reshape(hv, rows).T], axis=1
    )
    fused = units % BAND == 0 and dp == 8
    band = BAND if fused else units
    bands = [slice(at, at + band) for at in range(0, units, band)]
    shard_gu = jnp.concatenate([low(gu_proj[:, i, b]) for b in bands for i in (0, 1)], axis=1)
    shard_down = low(down_proj).T

    def gather(x):
        return lax.all_gather(x, "dp", axis=0, tiled=True)

    def scatter(value):
        return lax.psum_scatter(value, "dp", scatter_dimension=0, tiled=True)

    full_one = gather(shard_one)
    full_two = gather(shard_two)

    cut = 2 * hk + hv
    flats = full_one[:, cut + 2 * heads : cut + 2 * heads + small_cols].reshape(dp, rows * small_cols)
    parts, at = [], 0
    for x in small:
        size = x.size
        parts.append(flats[:, at : at + size].reshape((dp,) + x.shape).astype(f32))
        at += size
    gains = jnp.moveaxis(parts[0], 0, 1).reshape(2, -1)
    taps_qk = jnp.moveaxis(parts[1], 0, 3).reshape(2, CONV, hk)
    taps_qk = jnp.moveaxis(taps_qk, 0, 1).reshape(CONV, 2 * hk)
    taps_v = jnp.moveaxis(parts[2], 0, 2).reshape(CONV, hv)
    gain = jnp.broadcast_to(parts[3].reshape(1, val), (8, val))
    decay_low = lax.optimization_barrier(low(decay_params)).astype(f32)

    padded_ids = jnp.concatenate([jnp.full((4,), -1, jnp.int32), segment_ids])
    here_ids = lax.dynamic_slice_in_dim(padded_ids, start + 1, tokens + SPAN)
    prior_ids = lax.dynamic_slice_in_dim(padded_ids, start, tokens + SPAN)
    positions = start - SPAN + jnp.arange(tokens + SPAN, dtype=jnp.int32)
    resets_ext = ((here_ids != prior_ids) | (positions == 0)).astype(f32)
    resets_here = resets_ext[SPAN:]
    keep_ext = 1.0 - resets_ext
    valid_rows = [jnp.ones((tokens,), f32)]
    for lag in range(1, SPAN + 1):
        valid_rows.append(valid_rows[-1] * keep_ext[SPAN - lag + 1 : SPAN - lag + 1 + tokens])
    lag_valid = jnp.stack(valid_rows)
    pad = lax.dynamic_slice_in_dim(pad_mask, start, tokens).astype(f32)

    x_rim = from_behind(tokens_in[tokens - HALO :], "dp", 1)
    x = tokens_in.astype(f32)
    normed = low(norm_rows(x, gains[0]))
    normed_rim = low(norm_rows(x_rim.astype(f32), gains[0]))
    pre_qk = dot(normed, full_one[:, : 2 * hk], out=bf16)
    pre_v = dot(normed, full_one[:, 2 * hk : cut], out=bf16)
    mixed = dot(normed, full_one[:, cut:])[:, : 2 * heads].reshape(tokens, 2, heads)
    rim = low(dot(normed_rim, full_one[:, :cut])).astype(f32)
    (g, b), pull_gates = jax.vjp(lambda ab, dec: gates_of(ab, dec, pad), mixed, decay_low)
    aux, rowform = token_tables(g, b, pad, lag_valid, resets_here)

    rim_qk, rim_v = rim[:, : 2 * hk], rim[:, 2 * hk :]
    q, k, w, u, p, inv, r, r_end = mixer.forward_local(
        pre_qk, pre_v, rim_qk, rim_v, taps_qk, taps_v, aux, rowform
    )
    spot = mine.astype(jnp.int32).reshape(1)
    r_end, full_two = lax.optimization_barrier((low(r_end), full_two))
    gate_pre = dot(normed, full_two[:, :hv])
    maps = lax.all_gather(r_end, "dp")
    maps, gate_pre = lax.optimization_barrier((maps, gate_pre))
    y, st, vn, o = mixer.output(spot, maps, r, w, u, p, q, aux, gate_pre, gain)

    out_t = full_two[:, hv:]
    mp = lax.axis_size("mp")
    gain_one, gain_two = (jnp.broadcast_to(gains[i : i + 1], (8, gains.shape[1])) for i in (0, 1))
    half, width = tokens // 2, tokens_in.shape[1]
    like = sds((tokens, width), bf16)
    like_gain = sds(gain_two.shape)
    part_one = dot(y, out_t, NT, bf16)
    if fused:
        ffn_full = [sds((tokens, units), bf16), sds((tokens, 2 * units), bf16), like]
        ffn_weights = [sds((dp * rows, 2 * units), bf16), sds((dp * rows, units), bf16)]
        ffn_room = [pltpu.VMEM((half, units), bf16), pltpu.VMEM((half, 2 * units), bf16), pltpu.VMEM((half, width), bf16),
                    *[pltpu.VMEM(w.shape, bf16) for w in ffn_weights], pltpu.SemaphoreType.DMA((5,))]
        swaps = (len(Gather.KINDS), 2)
        attn, normed_two, two_a, act, dgu, down_part, full_gu, full_down = line_call(
            kernel_hidden_ffn, 0, "sum_hidden", mp,
            [part_one, tokens_in, gain_two, cotangent, shard_gu, shard_down],
            [like, like, sds((half, width), bf16)] + ffn_full + ffn_weights,
            ffn_room + [pltpu.SemaphoreType.DMA(swaps)] * 2 + [pltpu.SemaphoreType.DMA((2,))],
            away_in=(4, 5), away_out=(0, 3, 4, 5, 6, 7), sums=False, micros=120
        )
        total_two, dattn, dgain_two, act, dgu, down_part = line_call(
            kernel_dhidden_ffn, 1, "sum_dhidden", mp,
            [two_a, tokens_in, attn, cotangent, gain_two, normed_two, full_gu, full_down, act, dgu, down_part],
            [like, like, like_gain] + ffn_full,
            [pltpu.VMEM((tokens, width), bf16), pltpu.VMEM((half, width), bf16), pltpu.SemaphoreType.DMA((2,))] + ffn_room,
            away_in=(0, 5, 6, 7, 8, 9, 10), away_out=(0, 3, 4, 5), aliases={8: 3, 9: 4, 10: 5}, micros=120
        )
    else:
        full_gu, full_down = gather(shard_gu), gather(shard_down)
        attn, normed_two = line_call(
            kernel_hidden, 0, "sum_hidden", mp, [part_one, tokens_in, gain_two], [like, like],
            away_out=(0,), sums=False
        )
        act, dgu, two, down_part = feed_forward(normed_two, cotangent, full_gu, full_down)
        total_two, dattn, dgain_two = line_call(
            kernel_dhidden, 1, "sum_dhidden", mp, [two, tokens_in, attn, cotangent, gain_two],
            [like, like, like_gain], away_out=(0,)
        )
    down_sum = HalvingSum(down_part, "mp")
    (dattn,) = down_sum.tie(dattn)
    down_sum.step()
    dy = dot(dattn, out_t)
    grad_out = dot(dattn, y, TN, bf16)
    do, dgate, dgain, z, z_end = mixer.backward_local(dy, o, gate_pre, gain, aux, q, k, w, p)
    z_end, act, dgu = down_sum.tie(low(z_end), act, dgu)
    down_sum.step()
    grad_gu = dot(normed_two, dgu, TN, bf16)
    grad_down = dot(cotangent, act, TN, bf16)
    back_maps = lax.all_gather(z_end, "dp")
    grad_gate_w = dot(normed, dgate, TN, bf16)
    grad_two = jnp.concatenate([grad_gate_w, grad_out], axis=1)
    back_maps, grad_two, grad_gu, grad_down = down_sum.tie(back_maps, grad_two, grad_gu, grad_down)
    down_sum.step()
    red_gu = scatter(grad_gu)
    red_down = scatter(grad_down)
    red_two = scatter(grad_two)
    (dqk, dv, tail_qk, tail_v, head_qk, head_v, dtaps_qk, dtaps_v, dcg, dbeta) = mixer.backward(
        spot, back_maps, z, do, st, vn, q, k, w, u, p, inv, aux, rowform,
        pre_qk, pre_v, rim_qk, rim_v, taps_qk, taps_v
    )
    dqk, dv, head_qk, head_v = down_sum.tie(dqk, dv, head_qk, head_v)
    down_sum.step()
    heads_back = from_behind(jnp.concatenate([head_qk, head_v], axis=1), "dp", -1)
    dqk = lax.dynamic_update_slice(dqk, low(tail_qk + heads_back[:, : 2 * hk]), (tokens - HALO, 0))
    dv = lax.dynamic_update_slice(dv, low(tail_v + heads_back[:, 2 * hk :]), (tokens - HALO, 0))
    dmixed, ddecay = pull_gates((in_chunks(dcg, True), dbeta))
    dab = jnp.pad(low(dmixed.reshape(tokens, 2 * heads)), ((0, 0), (0, 128 - 2 * heads)))
    dpre = jnp.concatenate([dqk, dv, dab], axis=1)
    grad_one = dot(normed, dpre, TN, bf16)
    grad_small = [
        dtaps_qk.reshape(CONV, 2, heads, dp, -1).transpose(1, 0, 2, 3, 4),
        dtaps_v.reshape(CONV, heads, dp, -1),
    ]
    grad_flat = jnp.concatenate(
        [jnp.moveaxis(gs, -2, 0).reshape(dp, -1) for gs in grad_small], axis=1
    )
    high = low(ddecay).astype(f32)
    pair = jnp.stack([high, ddecay - high]).reshape(1, 1, -1)
    slots = jnp.where(jnp.arange(dp)[None, :, None] == mine, pair, 0.0)
    slots = jnp.broadcast_to(slots, (dp,) + slots.shape[1:]).reshape(dp, -1)
    used = grad_flat.shape[1]
    grad_flat = jnp.concatenate([grad_flat, slots], axis=1)
    grad_flat = jnp.pad(grad_flat, ((0, 0), (0, rows * small_cols - grad_flat.shape[1])))
    grad_flat = low(grad_flat).reshape(dp * rows, small_cols)
    grad_one = lax.dynamic_update_slice(grad_one, grad_flat, (0, cut + 2 * heads))
    grad_one, dpre = lax.optimization_barrier((grad_one, dpre))
    red_one = scatter(grad_one)
    normed_part = low(dot(dpre, full_one, NT) + dot(dgate, full_two[:, :hv], NT))
    while down_sum.todo:
        down_sum.step()
    (normed_part,) = down_sum.tie(normed_part)
    block_out = low(x + attn.astype(f32) + down_sum.value.astype(f32))
    swap = (8, max(rows, val))
    input_grad, dgains = line_call(
        partial(kernel_dinput, dp), 2, "sum_dinput", mp,
        [normed_part, tokens_in, attn, cotangent, total_two, gain_one, gain_two, dgain_two, dgain],
        [sds((tokens, width)), sds(swap)],
        [pltpu.VMEM((dp,) + swap, f32)] * 2 + [pltpu.SemaphoreType.DMA((dp,))] * 2
        + [pltpu.VMEM((mp,) + dgain.shape, f32)] + [pltpu.SemaphoreType.DMA((mp,))] * 2,
    )
    red_flat = red_one[:, cut + 2 * heads : cut + 2 * heads + small_cols].astype(f32).reshape(-1)
    red_small, at = [dgains[:2, :rows]], 0
    for s in small[1:3]:
        red_small.append(red_flat[at : at + s.size].reshape(s.shape))
        at += s.size
    red_small.append(lax.dynamic_slice_in_dim(dgains[2], mine * out_gain.size, out_gain.size))
    slots = red_flat[used : used + slots.shape[1]].reshape((dp, 2) + ddecay.shape)
    grads = [
        red_one[:, : 2 * hk].reshape(qk_proj.shape),
        jnp.stack([red_one[:, 2 * hk : cut].reshape(rows, heads, val),
                   red_two[:, :hv].reshape(rows, heads, val)], axis=1),
        red_one[:, cut : cut + 2 * heads].reshape(ab_proj.shape),
        rowwise(red_two[:, hv:].T).reshape(out_proj.shape),
        rowwise(jnp.stack([jnp.concatenate([red_gu[:, 2 * b.start + i * band :][:, :band] for b in bands], axis=1)
                           for i in (0, 1)], axis=1)),
        rowwise(red_down.T),
    ] + red_small + [jnp.sum(slots, axis=(0, 1))]
    matrix_rate = 2.5 * D ** (-0.5)
    rates = [matrix_rate] * 6 + [0.5, 1.0, 1.0, 0.5, 2.0]
    shrinks = [0.1] * 6 + [0.0] * 5
    updates = []
    for i in range(11):
        updates += adamw(masters[i], grads[i], firsts[i], seconds[i], rates[i], shrinks[i])
    copies = [low(updates[3 * i]) for i in range(6)]
    return (block_out, input_grad, *updates, *copies)


def solution(mesh):
    weights = [
        P("dp", None, "mp", None),
        P("dp", None, "mp", None),
        P("dp", None, "mp"),
        P("mp", None, "dp"),
        P("dp", None, "mp"),
        P("mp", "dp"),
        P(None, "dp"),
        P(None, None, "mp", "dp"),
        P(None, "mp", "dp"),
        P("dp"),
        P(None, "mp"),
    ]
    thrice = tuple(w for w in weights for _ in range(3))
    rowwise = P("dp", None)
    return jax.shard_map(
        on_device,
        mesh=mesh,
        in_specs=(rowwise, rowwise, P(), P()) + thrice,
        out_specs=(rowwise, rowwise) + thrice + tuple(weights[:6]),
        check_vma=False,
    )
```

```python
from functools import partial

import jax
import jax.numpy as jnp
from jax import lax
from jax.experimental import pallas as pl
from jax.experimental.layout import Layout, with_layout_constraint
from jax.experimental.pallas import tpu as pltpu
from jax.sharding import PartitionSpec as P

D = 2048
CONV = 4
SPAN = CONV - 1
CH = 128
HALO = 8
f32 = jnp.float32
bf16 = jnp.bfloat16
VLIM = 56 * 2**20

NN = (((1,), (0,)), ((), ()))
NT = (((1,), (1,)), ((), ()))
TN = (((0,), (0,)), ((), ()))

N_INV = 3
N_FWD = 1
N_SCAN = 1
N_BWD = 1


def mm(a, b, dims=NN, passes=1):
    def dot(x, y):
        return lax.dot_general(x, y, dims, preferred_element_type=f32)

    ah, bh = a.astype(bf16), b.astype(bf16)
    out = dot(ah, bh)
    if passes in (3, "right"):
        out = out + dot((a - ah.astype(f32)).astype(bf16), bh)
    if passes in (3, "left"):
        out = out + dot(ah, (b - bh.astype(f32)).astype(bf16))
    return out


def grid_iotas(n):
    return (
        lax.broadcasted_iota(jnp.int32, (n, n), 0),
        lax.broadcasted_iota(jnp.int32, (n, n), 1),
    )


def unit_lower_inverse(lowers, n):
    rows, cols = grid_iotas(n)
    eye = (rows == cols).astype(f32)
    small = lax.shift_right_logical(rows, 3) == lax.shift_right_logical(cols, 3)
    diag = [jnp.where(small, low, 0.0) for low in lowers]
    two = [mm(d, d) for d in diag]
    four = [mm(t, t, NN, N_INV) for t in two]
    inv = [eye - d for d in diag]
    inv = [x + mm(x, t, NN, "left") for x, t in zip(inv, two)]
    inv = [x + mm(x, f, NN, N_INV) for x, f in zip(inv, four)]
    bits = 3
    while (1 << bits) < n:
        wide = lax.shift_right_logical(rows, bits + 1) == lax.shift_right_logical(cols, bits + 1)
        fine = lax.shift_right_logical(rows, bits) != lax.shift_right_logical(cols, bits)
        off = [jnp.where(wide & fine, low, 0.0) for low in lowers]
        half = [mm(x, o, NN, "right") for x, o in zip(inv, off)]
        inv = [x - mm(y, x, NN, N_INV) for x, y in zip(inv, half)]
        bits += 1
    return inv


def sigmoid(x):
    return 1.0 / (1.0 + jnp.exp(-x))


def decay_matrix(aux, rows, h, heads, tri):
    cg = aux[:, 5 + h : 6 + h]
    cg_row = rows[1 + h : 2 + h, :]
    same = (aux[:, 4:5] == rows[0:1, :]) & tri
    return jnp.where(same, jnp.exp(jnp.where(same, cg - cg_row, 0.0)), 0.0)


def conv_of(ext_ref, taps_ref, aux, c0, c1):
    n = aux.shape[0]
    total = ext_ref[HALO : HALO + n, c0:c1] * taps_ref[SPAN : SPAN + 1, c0:c1]
    for lag in range(1, SPAN + 1):
        total = total + ext_ref[HALO - lag : HALO - lag + n, c0:c1] * (
            taps_ref[SPAN - lag : SPAN - lag + 1, c0:c1] * aux[:, lag - 1 : lag]
        )
    return total


def unit_of(act):
    return lax.rsqrt(jnp.sum(act * act, axis=-1, keepdims=True) + 1e-06)


def kernel_a(heads, key, val, pqk, pv, hqk, hv, tqk, tv, aux_ref, rows_ref,
             q_out, k_out, w_out, u_out, p_out, t_out, r_out, rend_out,
             xqk, xv, state):
    c = pl.program_id(0)
    n = pqk.shape[0]
    hk = heads * key

    @pl.when(c == 0)
    def _():
        xqk[0:HALO, :] = hqk[...]
        xv[0:HALO, :] = hv[...]
        r, s = (lax.broadcasted_iota(jnp.int32, (key, key + val), i) for i in (0, 1))
        for h in range(heads):
            state[h] = (r == s).astype(f32)

    xqk[HALO:, :] = pqk[...].astype(f32)
    xv[HALO:, :] = pv[...].astype(f32)
    aux = aux_ref[...]
    rows = rows_ref[0]
    ti, si = grid_iotas(n)
    tri = ti >= si
    lowers, queries, keys = [], [], []
    for h in range(heads):
        uq = conv_of(xqk, tqk, aux, h * key, (h + 1) * key)
        uk = conv_of(xqk, tqk, aux, hk + h * key, hk + (h + 1) * key)
        aq = uq * sigmoid(uq)
        ak = uk * sigmoid(uk)
        q = aq * unit_of(aq) * key ** (-0.5)
        k = ak * unit_of(ak)
        q_out[:, h * key : (h + 1) * key] = q
        k_out[:, h * key : (h + 1) * key] = k
        dec = decay_matrix(aux, rows, h, heads, tri)
        beta = aux[:, 5 + 3 * heads + h : 6 + 3 * heads + h]
        p_out[:, h * n : (h + 1) * n] = mm(q, k, NT, N_FWD) * dec
        lower = jnp.where(ti > si, mm(k, k, NT, N_FWD) * dec, 0.0) * beta
        lowers.append(lower.astype(bf16).astype(f32))
        queries.append(q)
        keys.append(k)
    invs = unit_lower_inverse(lowers, n)
    for h in range(heads):
        k = keys[h]
        beta = aux[:, 5 + 3 * heads + h : 6 + 3 * heads + h]
        fs = aux[:, 5 + heads + h : 6 + heads + h]
        lr = aux[:, 5 + 2 * heads + h : 6 + 2 * heads + h]
        uv = conv_of(xv, tv, aux, h * val, (h + 1) * val)
        v = uv * sigmoid(uv)
        t_out[:, h * n : (h + 1) * n] = invs[h]
        w = mm(invs[h], (beta * fs) * k, NN, N_FWD)
        u = mm(invs[h], beta * v, NN, N_FWD)
        w_out[:, h * key : (h + 1) * key] = w
        u_out[:, h * val : (h + 1) * val] = u
        st = state[h]
        r_out[0, h] = st
        new = jnp.concatenate([jnp.zeros((n, key), f32), u], axis=1) - mm(w, st, NN, N_SCAN)
        st = fs[n - 1 :, :] * st + mm(lr * k, new, TN, N_SCAN)
        state[h] = st
        rend_out[h] = st
    xqk[0:HALO, :] = xqk[n:, :]
    xv[0:HALO, :] = xv[n:, :]


def kernel_b(heads, key, val, mine, gath, r_in, w_in, u_in, p_in, q_in, aux_ref, gate_in, gain_ref,
             y_out, s_out, vn_out, o_out, start):
    c = pl.program_id(0)
    n = w_in.shape[0]

    @pl.when(c == 0)
    def _():
        start[...] = jnp.zeros_like(start)

        @pl.loop(0, mine[0])
        def _(d):
            for h in range(heads):
                start[h] = gath[d, h, :, key:].astype(f32) + mm(gath[d, h, :, :key], start[h], NN, N_FWD)

    aux = aux_ref[...]
    pad = aux[:, 3:4]
    for h in range(heads):
        fs = aux[:, 5 + heads + h : 6 + heads + h]
        st = r_in[0, h, :, key:] + mm(r_in[0, h, :, :key], start[h], NN, N_FWD)
        s_out[0, h] = st
        v0, v1 = h * val, (h + 1) * val
        new = u_in[:, v0:v1] - mm(w_in[:, h * key : (h + 1) * key], st, NN, N_FWD)
        vn_out[:, v0:v1] = new
        o = mm(fs * q_in[:, h * key : (h + 1) * key], st, NN, N_FWD)
        o = o + mm(p_in[:, h * n : (h + 1) * n], new, NN, N_FWD)
        o_out[:, v0:v1] = o
        scale = lax.rsqrt(jnp.mean(o * o, axis=-1, keepdims=True) + 1e-05)
        gate = gate_in[:, v0:v1]
        y = o * scale * gain_ref[0:1, :] * (gate * sigmoid(gate)) * pad
        y_out[:, v0:v1] = y.astype(bf16)


def kernel_c(heads, key, val, dy_in, o_in, gate_in, gain_ref, aux_ref, q_in, k_in, w_in, p_in,
             do_out, dgate_out, dgain_out, z_out, zend_out, carry):
    c = pl.program_id(0)
    n = dy_in.shape[0]

    @pl.when(c == 0)
    def _():
        r, s = (lax.broadcasted_iota(jnp.int32, (key, key + val), i) for i in (0, 1))
        for h in range(heads):
            carry[h] = (r == s).astype(f32)
        dgain_out[...] = jnp.zeros_like(dgain_out)

    aux = aux_ref[...]
    pad = aux[:, 3:4]
    gain = gain_ref[0:1, :]
    for h in range(heads):
        v0, v1 = h * val, (h + 1) * val
        k0, k1 = h * key, (h + 1) * key
        fs = aux[:, 5 + heads + h : 6 + heads + h]
        lr = aux[:, 5 + 2 * heads + h : 6 + 2 * heads + h]
        o = o_in[:, v0:v1]
        gate = gate_in[:, v0:v1]
        dy = dy_in[:, v0:v1] * pad
        scale = lax.rsqrt(jnp.mean(o * o, axis=-1, keepdims=True) + 1e-05)
        sig = sigmoid(gate)
        act = gate * sig
        unit = o * scale
        prod = dy * unit
        dgain_out[0:1, :] += jnp.sum(prod * act, axis=0, keepdims=True)
        dgate_out[:, v0:v1] = (prod * gain * (sig * (1.0 + gate * (1.0 - sig)))).astype(bf16)
        dn = dy * gain * act
        do = scale * (dn - unit * jnp.mean(dn * unit, axis=-1, keepdims=True))
        do_out[:, v0:v1] = do
        zst = carry[h]
        z_out[0, h] = zst
        lead = jnp.zeros((n, key), f32)
        dnew = jnp.concatenate([lead, mm(p_in[:, h * n : (h + 1) * n], do, TN, N_FWD)], axis=1)
        dnew = dnew + mm(lr * k_in[:, k0:k1], zst, NN, N_SCAN)
        own = jnp.concatenate(
            [jnp.zeros((key, key), f32), mm(fs * q_in[:, k0:k1], do, TN, N_FWD)], axis=1
        )
        zst = fs[n - 1 :, :] * zst + own - mm(w_in[:, k0:k1], dnew, TN, N_SCAN)
        carry[h] = zst
        zend_out[h] = zst


def through_act(u, grad):
    sig = sigmoid(u)
    return grad * (sig * (1.0 + u * (1.0 - sig)))


def kernel_d(heads, key, val, count, mine, gath, z_in, do_in, s_in, vn_in, q_in, k_in, w_in, u_in, p_in, t_in,
             aux_ref, rows_ref, pqk, pv, bqk, bv, hqk, hv, tqk, tv,
             dqk_out, dv_out, tailqk, tailv, headqk, headv, dtqk, dtv, dcg_out, dbeta_out,
             xqk, xv, dxqk, dxv, end):
    c = pl.program_id(0)
    steps = pl.num_programs(0)
    n = do_in.shape[0]
    hk = heads * key

    @pl.when(c == 0)
    def _():
        end[...] = jnp.zeros_like(end)

        @pl.loop(0, count - 1 - mine[0])
        def _(i):
            d = count - 1 - i
            for h in range(heads):
                end[h] = gath[d, h, :, key:].astype(f32) + mm(gath[d, h, :, :key], end[h], NN, N_FWD)

        dxqk[...] = jnp.zeros_like(dxqk)
        dxv[...] = jnp.zeros_like(dxv)
        dtqk[...] = jnp.zeros_like(dtqk)
        dtv[...] = jnp.zeros_like(dtv)

    @pl.when(c < steps - 1)
    def _():
        xqk[0:HALO, :] = bqk[...].astype(f32)[bqk.shape[0] - HALO :]
        xv[0:HALO, :] = bv[...].astype(f32)[bv.shape[0] - HALO :]

    @pl.when(c == steps - 1)
    def _():
        xqk[0:HALO, :] = hqk[...]
        xv[0:HALO, :] = hv[...]

    xqk[HALO:, :] = pqk[...].astype(f32)
    xv[HALO:, :] = pv[...].astype(f32)
    aux = aux_ref[...]
    rows = rows_ref[0]
    ti, si = grid_iotas(n)
    tri = ti >= si
    last = (lax.broadcasted_iota(jnp.int32, (n, 1), 0) == n - 1).astype(f32)
    dxqk[n:, :] = dxqk[0:HALO, :]
    dxv[n:, :] = dxv[0:HALO, :]
    dxqk[0:n, :] = jnp.zeros((n, 2 * hk), f32)
    dxv[0:n, :] = jnp.zeros((n, heads * val), f32)

    def conv_back(du, ext, dext, taps, dtaps, c0, c1):
        for lag in range(SPAN + 1):
            part = du if lag == 0 else du * aux[:, lag - 1 : lag]
            dtaps[SPAN - lag : SPAN - lag + 1, c0:c1] += jnp.sum(
                part * ext[HALO - lag : HALO - lag + n, c0:c1], axis=0, keepdims=True
            )
            spot = slice(HALO - lag, HALO - lag + n)
            dext[spot, c0:c1] += part * taps[SPAN - lag : SPAN - lag + 1, c0:c1]

    for h in range(heads):
        v0, v1 = h * val, (h + 1) * val
        k0, k1 = h * key, (h + 1) * key
        fs = aux[:, 5 + heads + h : 6 + heads + h]
        lr = aux[:, 5 + 2 * heads + h : 6 + 2 * heads + h]
        beta = aux[:, 5 + 3 * heads + h : 6 + 3 * heads + h]
        q, k = q_in[:, k0:k1], k_in[:, k0:k1]
        w, u = w_in[:, k0:k1], u_in[:, v0:v1]
        p, inv = p_in[:, h * n : (h + 1) * n], t_in[:, h * n : (h + 1) * n]
        do, new, st = do_in[:, v0:v1], vn_in[:, v0:v1], s_in[0, h]
        dst = z_in[0, h, :, key:] + mm(z_in[0, h, :, :key], end[h], NN, N_BWD)
        dec = decay_matrix(aux, rows, h, heads, tri)
        kk = mm(k, k, NT, N_BWD)
        kl = lr * k
        dnew = mm(p, do, TN, N_BWD) + mm(kl, dst, NN, N_BWD)
        dp = mm(do, new, NT, N_BWD)
        dqf = mm(do, st, NT, N_BWD)
        dkl = mm(new, dst, NT, N_BWD)
        dw = -mm(dnew, st, NT, N_BWD)
        drv = mm(inv, dnew, TN, N_BWD)
        drk = mm(inv, dw, TN, N_BWD)
        dlow = -(mm(drv, u, NT, N_BWD) + mm(drk, w, NT, N_BWD))
        dlow = jnp.where(ti > si, dlow, 0.0) * dec
        dkk = dlow * beta
        hh = dp * dec
        pairs = dkk * kk + dp * p
        dq = fs * dqf + mm(hh, k, NN, N_BWD)
        dk = mm(hh, q, TN, N_BWD) + mm(dkk, k, NN, N_BWD) + mm(dkk, k, TN, N_BWD)
        dk = dk + lr * dkl + (beta * fs) * drk
        uv = conv_of(xv, tv, aux, v0, v1)
        v = uv * sigmoid(uv)
        kd = jnp.sum(k * drk, axis=-1, keepdims=True) * fs
        dbeta = jnp.sum(dlow * kk, axis=-1, keepdims=True) + kd
        dbeta = dbeta + jnp.sum(v * drv, axis=-1, keepdims=True)
        leave = lr * jnp.sum(k * dkl, axis=-1, keepdims=True)
        dcg = jnp.sum(pairs, axis=-1, keepdims=True) + beta * kd - leave
        dcg = dcg + fs * jnp.sum(q * dqf, axis=-1, keepdims=True)
        ones = jnp.ones((n, 8), f32)
        dcg = dcg - mm(pairs, ones, TN, 3)[:, 0:1]
        tail = jnp.sum(leave, axis=0, keepdims=True) + fs[n - 1 :, :] * jnp.sum(
            jnp.sum(st * dst, axis=-1, keepdims=True), axis=0, keepdims=True
        )
        dcg_out[:, h : h + 1] = dcg + last * tail
        dbeta_out[:, h : h + 1] = dbeta
        conv_back(through_act(uv, beta * drv), xv, dxv, tv, dtv, v0, v1)
        for off, grad, size in ((0, dq, key ** (-0.5)), (hk, dk, 1.0)):
            uu = conv_of(xqk, tqk, aux, off + k0, off + k1)
            act = uu * sigmoid(uu)
            rs = unit_of(act)
            da = (rs * size) * (grad - act * (rs * rs) * jnp.sum(act * grad, axis=-1, keepdims=True))
            conv_back(through_act(uu, da), xqk, dxqk, tqk, dtqk, off + k0, off + k1)
    dqk_out[...] = dxqk[HALO:, :].astype(bf16)
    dv_out[...] = dxv[HALO:, :].astype(bf16)

    @pl.when(c == 0)
    def _():
        tailqk[...] = dxqk[n:, :]
        tailv[...] = dxv[n:, :]

    headqk[...] = dxqk[0:HALO, :]
    headv[...] = dxv[0:HALO, :]


def cost(microseconds):
    return pl.CostEstimate(
        flops=int(microseconds * 1e9), bytes_accessed=int(microseconds * 3.3e6), transcendentals=0)


def params(**kw):
    return pltpu.CompilerParams(vmem_limit_bytes=VLIM, dimension_semantics=("arbitrary",), **kw)


def sds(shape, dtype=f32):
    return jax.ShapeDtypeStruct(shape, dtype)


class Mixer:
    def __init__(self, tokens, heads, key, val):
        self.sizes = (heads, key, val)
        self.tokens, self.n, self.steps = tokens, CH, tokens // CH

    def rows(self, width, back=False):
        m = self.steps - 1
        return pl.BlockSpec((self.n, width), (lambda c: (m - c, 0)) if back else (lambda c: (c, 0)))

    def lead(self, shape, back=False):
        m, rest = self.steps - 1, (0,) * len(shape)
        return pl.BlockSpec((1,) + shape, (lambda c: (m - c,) + rest) if back else (lambda c: (c,) + rest))

    def whole(self, shape):
        rest = (0,) * len(shape)
        return pl.BlockSpec(shape, lambda c: rest)

    def forward_local(self, pqk, pv, hqk, hv, tqk, tv, aux, rows):
        heads, key, val = self.sizes
        t, n, s = self.tokens, self.n, self.steps
        hk, hv_ = heads * key, heads * val
        wide = key + val
        return pl.pallas_call(
            partial(kernel_a, heads, key, val),
            grid=(s,),
            in_specs=[self.rows(2 * hk), self.rows(hv_), self.whole(hqk.shape), self.whole(hv.shape),
                      self.whole(tqk.shape), self.whole(tv.shape), self.rows(aux.shape[1]), self.lead(rows.shape[1:])],
            out_specs=[self.rows(hk), self.rows(hk), self.rows(hk), self.rows(hv_), self.rows(heads * n), self.rows(heads * n),
                       self.lead((heads, key, wide)), self.whole((heads, key, wide))],
            out_shape=[sds((t, hk)), sds((t, hk)), sds((t, hk)), sds((t, hv_)), sds((t, heads * n)), sds((t, heads * n)),
                       sds((s, heads, key, wide)), sds((heads, key, wide))],
            scratch_shapes=[pltpu.VMEM((HALO + n, 2 * hk), f32), pltpu.VMEM((HALO + n, hv_), f32),
                            pltpu.VMEM((heads, key, wide), f32)],
            compiler_params=params(),
            cost_estimate=cost(39),
            name="mixer_local",
        )(pqk, pv, hqk, hv, tqk, tv, aux, rows)

    def output(self, mine, gath, r, w, u, p, q, aux, gate, gain):
        heads, key, val = self.sizes
        t, n, s = self.tokens, self.n, self.steps
        hk, hv_ = heads * key, heads * val
        return pl.pallas_call(
            partial(kernel_b, heads, key, val),
            grid=(s,),
            in_specs=[pl.BlockSpec(memory_space=pltpu.SMEM), self.whole(gath.shape), self.lead((heads, key, key + val)),
                      self.rows(hk), self.rows(hv_), self.rows(heads * n), self.rows(hk), self.rows(aux.shape[1]),
                      self.rows(hv_), self.whole(gain.shape)],
            out_specs=[self.rows(hv_), self.lead((heads, key, val)), self.rows(hv_), self.rows(hv_)],
            out_shape=[sds((t, hv_), bf16), sds((s, heads, key, val)), sds((t, hv_)), sds((t, hv_))],
            scratch_shapes=[pltpu.VMEM((heads, key, val), f32)],
            compiler_params=params(),
            cost_estimate=cost(18),
            name="mixer_output",
        )(mine, gath, r, w, u, p, q, aux, gate, gain)

    def backward_local(self, dy, o, gate, gain, aux, q, k, w, p):
        heads, key, val = self.sizes
        t, n, s = self.tokens, self.n, self.steps
        hk, hv_ = heads * key, heads * val
        wide = key + val
        back = partial(self.rows, back=True)
        return pl.pallas_call(
            partial(kernel_c, heads, key, val),
            grid=(s,),
            in_specs=[back(hv_), back(hv_), back(hv_), self.whole(gain.shape), back(aux.shape[1]),
                      back(hk), back(hk), back(hk), back(heads * n)],
            out_specs=[back(hv_), back(hv_), self.whole((8, val)), self.lead((heads, key, wide), True),
                       self.whole((heads, key, wide))],
            out_shape=[sds((t, hv_)), sds((t, hv_), bf16), sds((8, val)), sds((s, heads, key, wide)),
                       sds((heads, key, wide))],
            scratch_shapes=[pltpu.VMEM((heads, key, wide), f32)],
            compiler_params=params(),
            cost_estimate=cost(17),
            name="mixer_back_local",
        )(dy, o, gate, gain, aux, q, k, w, p)

    def backward(self, mine, gath, z, do, st, vn, q, k, w, u, p, inv, aux, rows, pqk, pv, hqk, hv, tqk, tv):
        heads, key, val = self.sizes
        t, n, s = self.tokens, self.n, self.steps
        hk, hv_ = heads * key, heads * val
        back = partial(self.rows, back=True)
        ratio = n // 16
        m = s - 1

        def before(width):
            return pl.BlockSpec((16, width), lambda c: (jnp.maximum((m - c) * ratio - 1, 0), 0))

        return pl.pallas_call(
            partial(kernel_d, heads, key, val, gath.shape[0]),
            grid=(s,),
            in_specs=[pl.BlockSpec(memory_space=pltpu.SMEM), self.whole(gath.shape), self.lead((heads, key, key + val), True),
                      back(hv_), self.lead((heads, key, val), True), back(hv_), back(hk), back(hk), back(hk), back(hv_),
                      back(heads * n), back(heads * n), back(aux.shape[1]), self.lead(rows.shape[1:], True),
                      back(2 * hk), back(hv_), before(2 * hk), before(hv_), self.whole(hqk.shape), self.whole(hv.shape),
                      self.whole(tqk.shape), self.whole(tv.shape)],
            out_specs=[back(2 * hk), back(hv_), self.whole((HALO, 2 * hk)), self.whole((HALO, hv_)),
                       self.whole((HALO, 2 * hk)), self.whole((HALO, hv_)), self.whole((CONV, 2 * hk)), self.whole((CONV, hv_)),
                       back(heads), back(heads)],
            out_shape=[sds((t, 2 * hk), bf16), sds((t, hv_), bf16), sds((HALO, 2 * hk)), sds((HALO, hv_)),
                       sds((HALO, 2 * hk)), sds((HALO, hv_)), sds((CONV, 2 * hk)), sds((CONV, hv_)),
                       sds((t, heads)), sds((t, heads))],
            scratch_shapes=[pltpu.VMEM((HALO + n, 2 * hk), f32), pltpu.VMEM((HALO + n, hv_), f32),
                            pltpu.VMEM((HALO + n, 2 * hk), f32), pltpu.VMEM((HALO + n, hv_), f32),
                            pltpu.VMEM((heads, key, val), f32)],
            compiler_params=params(),
            cost_estimate=cost(50),
            name="mixer_back",
        )(mine, gath, z, do, st, vn, q, k, w, u, p, inv, aux, rows, pqk, pv, pqk, pv, hqk, hv, tqk, tv)


def gates_of(mixed_ab, decay, pad):
    g = -jnp.exp(decay[0]) * jax.nn.softplus(mixed_ab[:, 0] + decay[1]) * pad[:, None]
    b = jax.nn.sigmoid(mixed_ab[:, 1]) * pad[:, None]
    return (g, b)


def in_chunks(values, upper):
    tri = jnp.tril(jnp.ones((CH, CH), f32))
    tri = tri.T if upper else tri
    parts = values.reshape(-1, CH, values.shape[1])
    return jnp.einsum("ts,csh->cth", tri, parts, precision=lax.Precision.HIGHEST).reshape(values.shape)


def token_tables(g, b, pad, lag_valid, resets):
    t, heads = g.shape
    sums = in_chunks(jnp.concatenate([g, resets[:, None]], axis=1), False)
    cg, count = sums[:, :heads], sums[:, heads:]
    ends = sums.reshape(-1, CH, heads + 1)[:, -1:]
    ends = jnp.broadcast_to(ends, (ends.shape[0], CH, heads + 1)).reshape(t, heads + 1)
    fs = jnp.where(count == 0, jnp.exp(cg), 0.0)
    to_end = count == ends[:, heads:]
    lr = jnp.where(to_end, jnp.exp(jnp.where(to_end, ends[:, :heads] - cg, 0.0)), 0.0)
    aux = jnp.concatenate([lag_valid[1:].T, pad[:, None], count, cg, fs, lr, b], axis=1)
    rows = jnp.concatenate([count, cg], axis=1).reshape(-1, CH, heads + 1).transpose(0, 2, 1)
    return (aux, rows)


ROWS = 16
HOP = 3
BAND = 128


class Line:
    def __init__(self, n, part, red, fin, sems, gap=0):
        self.n, self.part, self.red, self.fin, self.gap = n, part, red, fin, gap
        self.rs_send, self.rs_recv, self.bc_send, self.bc_recv = sems
        self.batch = part.shape[0] // 2
        self.pieces = self.batch // ROWS
        self.per = self.pieces // 2
        self.rank = lax.axis_index("mp")

    def pos(self, side):
        return self.rank if side == 0 else self.n - 1 - self.rank

    def fwd(self, side):
        return {"mp": self.rank + 1 if side == 0 else self.rank - 1}

    def bwd(self, side):
        return {"mp": self.rank - 1 if side == 0 else self.rank + 1}

    def rows(self, side, j):
        row = lax.div(j, self.per) * self.batch + side * (self.batch // 2) + lax.rem(j, self.per) * ROWS
        return pl.ds(pl.multiple_of(row, ROWS), ROWS)

    def turn(self, step, delay):
        raw = step - delay
        late = raw >= self.per + self.gap
        live = ((raw >= 0) & (raw < self.per)) | (late & (raw < self.pieces + self.gap))
        return jnp.where(late, raw - self.gap, raw), live

    def first(self, side, j):
        return pltpu.make_async_remote_copy(
            self.part.at[self.rows(side, j), :], self.red.at[side, j],
            self.rs_send.at[side, j], self.rs_recv.at[side, j], device_id=self.fwd(side))

    def onward(self, side, j):
        return pltpu.make_async_remote_copy(
            self.red.at[side, j], self.red.at[side, j],
            self.rs_send.at[side, j], self.rs_recv.at[side, j], device_id=self.fwd(side))

    def back(self, side, j):
        at = self.rows(side, j)
        return pltpu.make_async_remote_copy(
            self.fin.at[at, :], self.fin.at[at, :],
            self.bc_send.at[side, j], self.bc_recv.at[side, j], device_id=self.bwd(side))

    def greet(self, dp_others=(), mp_others=()):
        barrier = pltpu.get_barrier_semaphore()
        more = len(dp_others) + len(mp_others)
        for other in dp_others:
            pl.semaphore_signal(barrier, inc=1, device_id={"dp": other})
        for other in mp_others:
            pl.semaphore_signal(barrier, inc=1, device_id={"mp": other})
        if mp_others:
            pl.semaphore_wait(barrier, more)
            return

        @pl.when(self.rank > 0)
        def _():
            pl.semaphore_signal(barrier, inc=1, device_id={"mp": self.rank - 1})

        @pl.when(self.rank < self.n - 1)
        def _():
            pl.semaphore_signal(barrier, inc=1, device_id={"mp": self.rank + 1})

        @pl.when((self.rank > 0) & (self.rank < self.n - 1))
        def _():
            pl.semaphore_wait(barrier, 2 + more)

        @pl.when((self.rank == 0) | (self.rank == self.n - 1))
        def _():
            pl.semaphore_wait(barrier, 1 + more)

    def total(self, side, j):
        own = self.part[self.rows(side, j), :]
        return (self.red[side, j].astype(f32) + own.astype(f32)).astype(bf16)

    def run(self, finish, beside=None, least=0):
        n = self.n

        def done(side, j):
            at = self.rows(side, j)
            finish(self.fin[at, :].astype(f32), at)

        @pl.loop(0, max(self.pieces + self.gap + 2 * HOP * (n - 1), least))
        def _(step):
            for side in (0, 1):
                pos = self.pos(side)
                j, live = self.turn(step, HOP * pos)

                @pl.when(live)
                def _(side=side, pos=pos, j=j):
                    @pl.when(pos == 0)
                    def _():
                        self.first(side, j).start()

                    @pl.when(pos > 0)
                    def _():
                        self.onward(side, j).wait_recv()

                    @pl.when((pos > 0) & (pos < n - 1))
                    def _():
                        self.red[side, j] = self.total(side, j)
                        self.onward(side, j).start()

                    @pl.when(pos == n - 1)
                    def _():
                        self.fin[self.rows(side, j), :] = self.total(side, j)
                        self.back(side, j).start()
                        done(side, j)

            for side in (0, 1):
                pos = self.pos(side)
                j, live = self.turn(step, HOP * (n - 1) + HOP * (n - 1 - pos))

                @pl.when(live & (pos < n - 1))
                def _(side=side, pos=pos, j=j):
                    self.back(side, j).wait_recv()

                    @pl.when(pos > 0)
                    def _():
                        self.back(side, j).start()

                    done(side, j)

            if beside is not None:
                beside(step)

        @pl.loop(0, self.pieces)
        def _(j):
            for side in (0, 1):
                pos = self.pos(side)

                @pl.when(pos < n - 1)
                def _(side=side):
                    self.onward(side, j).wait_send()

                @pl.when(pos > 0)
                def _(side=side):
                    self.back(side, j).wait_send()


def norm_scale(values):
    return lax.rsqrt(jnp.mean(values * values, axis=-1, keepdims=True) + 1e-06)


def norm_back_rows(u, gain, grad, sums=None, at=None):
    scale = norm_scale(u)
    unit = u * scale
    if sums is not None:
        sums[pl.ds(lax.div(at.start, ROWS), 1), :] = jnp.sum(grad * unit, axis=0, keepdims=True)
    scaled = grad * gain
    return scale * (scaled - unit * jnp.mean(scaled * unit, axis=-1, keepdims=True))


class FeedForward:
    def __init__(self, refs, begin, batch, arrive=None):
        self.arrive = arrive or self.wait_loads
        (self.normed, self.cot, self.gu_hbm, self.down_hbm, self.act_hbm, self.dgu_hbm, self.down_out, self.part_two,
         self.act, self.dgu, self.down_part, self.gu, self.down, self.sems) = refs
        self.begin, self.batch = begin, batch
        self.count = self.act.shape[0]
        self.bands = self.down.shape[1] // BAND
        self.units = self.bands + self.gu.shape[0] // (2 * BAND)
        self.end = begin + self.units

    def loads(self):
        return [pltpu.make_async_copy(self.gu_hbm, self.gu, self.sems.at[0]),
                pltpu.make_async_copy(self.down_hbm, self.down, self.sems.at[1])]

    def stores(self):
        at = pl.ds(self.batch * self.count, self.count)
        return [pltpu.make_async_copy(self.act, self.act_hbm.at[at, :], self.sems.at[2]),
                pltpu.make_async_copy(self.dgu, self.dgu_hbm.at[at, :], self.sems.at[3]),
                pltpu.make_async_copy(self.down_part, self.down_out.at[at, :], self.sems.at[4])]

    def start(self):
        for load in self.loads():
            load.start()

    def wait_loads(self):
        for load in self.loads():
            load.wait()

    def finish(self):
        for store in self.stores():
            store.start()
        for store in self.stores():
            store.wait()

    def step(self, step):
        at = step - self.begin
        mine = pl.ds(self.batch * self.count, self.count)

        @pl.when(at == 0)
        def _():
            self.arrive()

        @pl.when((at >= 0) & (at < self.bands))
        def _():
            two = pl.ds(pl.multiple_of(at * 2 * BAND, 2 * BAND), 2 * BAND)
            one = pl.ds(pl.multiple_of(at * BAND, BAND), BAND)
            gate_up = lax.dot_general(self.normed[...], self.gu[:, two], NN, preferred_element_type=f32)
            grad = lax.dot_general(self.cot[...], self.down[:, one], NN, preferred_element_type=f32)
            gate, up = gate_up[:, :BAND], gate_up[:, BAND:]
            sig = sigmoid(gate)
            swish = gate * sig
            self.act[:, one] = (swish * up).astype(bf16)
            dgate = grad * up * sig * (1.0 + gate * (1.0 - sig))
            self.dgu[:, two] = jnp.concatenate([dgate, grad * swish], axis=1).astype(bf16)

        @pl.when((at >= self.bands) & (at < self.units))
        def _():
            out = pl.ds(pl.multiple_of((at - self.bands) * 2 * BAND, 2 * BAND), 2 * BAND)
            self.part_two[mine, out] = lax.dot_general(
                self.dgu[...], self.gu[out, :], NT, preferred_element_type=f32).astype(bf16)
            self.down_part[:, out] = lax.dot_general(
                self.act[...], self.down[out, :], NT, preferred_element_type=f32).astype(bf16)


class Gather:
    KINDS = ("own1", "own2", "own0", "one0", "one2", "two0", "two1", "both0a", "both0b")

    def __init__(self, refs):
        arrays = (len(refs) - 3) // 2
        self.shards, self.full = refs[:arrays], refs[arrays : 2 * arrays]
        self.send, self.recv, self.local = refs[2 * arrays :]
        self.arrays = range(arrays)
        self.me = lax.axis_index("dp")
        self.count = self.shards[0].shape[0]

    def flip(self, device, bit):
        size = 1 << bit
        return device + size - 2 * size * lax.rem(lax.div(device, size), 2)

    def plan(self, kind, sender):
        one, two = self.flip(sender, 1), self.flip(sender, 2)
        both = self.flip(one, 2)
        return {"own1": (1, sender, 2), "own2": (2, sender, 2), "own0": (0, sender, 2),
                "one0": (0, one, 2), "one2": (2, one, 0), "two0": (0, two, 2), "two1": (1, two, 1),
                "both0a": (0, both, 0), "both0b": (0, both, 1)}[kind]

    def copy(self, kind, array, sending):
        k = self.KINDS.index(kind)
        bit = self.plan(kind, self.me)[0]
        other = self.flip(self.me, bit)
        _, owner, half = self.plan(kind, self.me if sending else other)
        size = self.count if half == 2 else self.count // 2
        start = owner * self.count + (size if half == 1 else 0)
        spot = self.full[array].at[pl.ds(pl.multiple_of(start, size), size), :]
        source = self.shards[array] if sending and kind.startswith("own") else spot
        return pltpu.make_async_remote_copy(
            source, spot, self.send.at[k, array], self.recv.at[k, array], device_id={"dp": other})

    def own(self, array):
        spot = pl.ds(pl.multiple_of(self.me * self.count, self.count), self.count)
        return pltpu.make_async_copy(self.shards[array], self.full[array].at[spot, :], self.local.at[array])

    def partners(self):
        return [self.flip(self.me, bit) for bit in (0, 1, 2)]

    def go(self, *kinds):
        for kind in kinds:
            for array in self.arrays:
                self.copy(kind, array, True).start()

    def come(self, *kinds):
        for kind in kinds:
            for array in self.arrays:
                self.copy(kind, array, False).wait_recv()

    def start(self):
        for array in self.arrays:
            self.own(array).start()
        self.go("own1", "own2", "own0")

    def turn(self):
        self.come("own1", "own2")
        self.go("one2", "two1", "one0", "two0")

    def cross(self):
        self.come("one2", "two1")
        self.go("both0a", "both0b")

    def end(self):
        self.come("own0", "one0", "two0", "both0a", "both0b")
        for array in self.arrays:
            self.own(array).wait()

    def sent(self):
        for kind in self.KINDS:
            for array in self.arrays:
                self.copy(kind, array, True).wait_send()


def kernel_hidden(n, part, x_in, gain, attn, normed, red, fin, rs_send, rs_recv, bc_send, bc_recv, sem):
    line = Line(n, part, red, fin, (rs_send, rs_recv, bc_send, bc_recv))
    line.greet()

    def finish(total, at):
        h = x_in[at, :].astype(f32) + total
        normed[at, :] = (h * norm_scale(h) * gain[0:1, :]).astype(bf16)

    line.run(finish)
    keep = pltpu.make_async_copy(fin, attn, sem)
    keep.start()
    keep.wait()


def kernel_gather(shard, full, send, recv, local):
    gather = Gather((shard, full, send, recv, local))
    barrier = pltpu.get_barrier_semaphore()
    partners = gather.partners()
    for other in partners:
        pl.semaphore_signal(barrier, inc=1, device_id={"dp": other})
    pl.semaphore_wait(barrier, len(partners))
    gather.start()
    gather.turn()
    gather.cross()
    gather.end()
    gather.sent()


def gather_call(cid, name, shard):
    swaps = pltpu.SemaphoreType.DMA((len(Gather.KINDS), 1))
    far = pl.BlockSpec(memory_space=pl.ANY)
    return pl.pallas_call(
        kernel_gather,
        in_specs=[far],
        out_specs=far,
        out_shape=sds((8 * shard.shape[0], shard.shape[1]), shard.dtype),
        scratch_shapes=[swaps, swaps, pltpu.SemaphoreType.DMA((1,))],
        compiler_params=pltpu.CompilerParams(collective_id=cid, has_side_effects=True, vmem_limit_bytes=VLIM),
        cost_estimate=cost(45),
        name=name,
    )(shard)


TURN, CROSS, BEGIN = 22, 33, 38


def kernel_hidden_ffn(n, part, x_in, gain, cot, gu_shard, down_shard,
                      attn, normed, part_two, act_hbm, dgu_hbm, down_out, gu_hbm, down_hbm,
                      red, fin, rs_send, rs_recv, bc_send, bc_recv, sem, act, dgu, down_part, gu, down, sems,
                      g_send, g_recv, g_local):
    line = Line(n, part, red, fin, (rs_send, rs_recv, bc_send, bc_recv))
    half = pl.ds(0, line.batch)
    gather = Gather((gu_shard, down_shard, gu, down, g_send, g_recv, g_local))
    keeps = [pltpu.make_async_copy(gu, gu_hbm, sems.at[0]), pltpu.make_async_copy(down, down_hbm, sems.at[1])]

    def arrive():
        gather.end()
        for keep in keeps:
            keep.start()

    begin = max(BEGIN, line.per + 2 * HOP * (n - 1))
    ffn = FeedForward((normed.at[half, :], cot.at[half, :], gu_hbm, down_hbm, act_hbm, dgu_hbm, down_out, part_two,
                       act, dgu, down_part, gu, down, sems), begin, 0, arrive)
    line.greet(gather.partners())
    gather.start()

    def finish(total, at):
        h = x_in[at, :].astype(f32) + total
        normed[at, :] = (h * norm_scale(h) * gain[0:1, :]).astype(bf16)

    def beside(step):
        @pl.when(step == TURN)
        def _():
            gather.turn()

        @pl.when(step == CROSS)
        def _():
            gather.cross()

        ffn.step(step)

    line.run(finish, beside, ffn.end)
    last = pltpu.make_async_copy(fin, attn, sem)
    last.start()
    ffn.finish()
    gather.sent()
    for keep in keeps:
        keep.wait()
    last.wait()


def kernel_dhidden(n, part, x_in, attn, cot, gain, total_out, dattn, dgain,
                   red, fin, rs_send, rs_recv, bc_send, bc_recv, sem, sums):
    line = Line(n, part, red, fin, (rs_send, rs_recv, bc_send, bc_recv))
    line.greet()

    def finish(total, at):
        h = x_in[at, :].astype(f32) + attn[at, :].astype(f32)
        dh = cot[at, :].astype(f32) + norm_back_rows(h, gain[0:1, :], total, sums, at)
        dattn[at, :] = dh.astype(bf16)

    line.run(finish)
    keep = pltpu.make_async_copy(fin, total_out, sem)
    keep.start()
    dgain[0:1, :] = jnp.sum(sums[...], axis=0, keepdims=True)
    keep.wait()


def kernel_dhidden_ffn(n, two_a, x_in, attn, cot, gain, normed_hbm, gu_hbm, down_hbm, act_in, dgu_in, down_in,
                       total_out, dattn, dgain, act_hbm, dgu_hbm, down_out,
                       red, fin, rs_send, rs_recv, bc_send, bc_recv, sem, sums,
                       part, normed, more, act, dgu, down_part, gu, down, sems):
    line = Line(n, part, red, fin, (rs_send, rs_recv, bc_send, bc_recv))
    half = line.batch
    ffn = FeedForward((normed, cot.at[pl.ds(half, half), :], gu_hbm, down_hbm, act_hbm, dgu_hbm, down_out, part,
                       act, dgu, down_part, gu, down, sems), 1, 1)
    line.gap = max(0, ffn.end - line.per)
    brought = [pltpu.make_async_copy(two_a, part.at[pl.ds(0, half), :], more.at[0]),
               pltpu.make_async_copy(normed_hbm.at[pl.ds(half, half), :], normed, more.at[1])]
    for load in brought:
        load.start()
    ffn.start()
    line.greet()
    for load in brought:
        load.wait()

    def finish(total, at):
        h = x_in[at, :].astype(f32) + attn[at, :].astype(f32)
        dh = cot[at, :].astype(f32) + norm_back_rows(h, gain[0:1, :], total, sums, at)
        dattn[at, :] = dh.astype(bf16)

    line.run(finish, ffn.step, ffn.end)
    keep = pltpu.make_async_copy(fin, total_out, sem)
    keep.start()
    dgain[0:1, :] = jnp.sum(sums[...], axis=0, keepdims=True)
    ffn.finish()
    keep.wait()


def kernel_dinput(dp, n, part, x_in, attn, cot, total_two, gain_one, gain_two, dgain_two, dgate, dinput, dgains,
                  red, fin, rs_send, rs_recv, bc_send, bc_recv, sem, sums,
                  src, dst, g_send, g_recv, gates, m_send, m_recv):
    line = Line(n, part, red, fin, (rs_send, rs_recv, bc_send, bc_recv))
    me = lax.axis_index("dp")
    rank = line.rank
    others = [lax.rem(me + i, dp) for i in range(dp)]
    ranks = [lax.rem(rank + i, n) for i in range(n)]
    line.greet(others[1:], ranks[1:])

    def mp_swap(i):
        return pltpu.make_async_remote_copy(
            dgate, gates.at[rank], m_send.at[i], m_recv.at[i], device_id={"mp": ranks[i]})

    for i in range(1, n):
        mp_swap(i).start()
    gates[rank] = dgate[...]

    def finish(total, at):
        x = x_in[at, :].astype(f32)
        h = x + attn[at, :].astype(f32)
        dh = cot[at, :].astype(f32) + norm_back_rows(h, gain_two[0:1, :], total_two[at, :].astype(f32))
        dinput[at, :] = dh + norm_back_rows(x, gain_one[0:1, :], total, sums, at)

    line.run(finish)
    for i in range(1, n):
        mp_swap(i).wait()
    gate = gates[0]
    for r in range(1, n):
        gate = gate + gates[r]
    cols, val = dgain_two.shape[1] // dp, dgate.shape[1]
    one = jnp.sum(sums[...], axis=0, keepdims=True)
    for p in range(dp):
        src[p, 0:1, :cols] = one[:, p * cols : (p + 1) * cols]
        src[p, 1:2, :cols] = dgain_two[0:1, p * cols : (p + 1) * cols]
        src[p, 2:3, :val] = gate[0:1, :]

    def swap(i):
        return pltpu.make_async_remote_copy(
            src.at[others[i]], dst.at[me], g_send.at[i], g_recv.at[i], device_id={"dp": others[i]})

    for i in range(1, dp):
        swap(i).start()
    dst[me] = src[me]
    for i in range(1, dp):
        swap(i).wait()
    total = dst[0]
    for p in range(1, dp):
        total = total + dst[p]
    dgains[...] = total


def line_call(kernel, cid, name, n, ins, outs, extra=(), away_in=(), away_out=(), aliases=None, sums=True, micros=100):
    tokens, width = outs[0].shape
    pieces = tokens // 2 // ROWS
    vmem = pl.BlockSpec(memory_space=pltpu.VMEM)
    far = pl.BlockSpec(memory_space=pl.ANY)
    return pl.pallas_call(
        partial(kernel, n),
        in_specs=[far if i in away_in else vmem for i in range(len(ins))],
        out_specs=[far if i in away_out else vmem for i in range(len(outs))],
        out_shape=outs,
        scratch_shapes=[pltpu.VMEM((2, pieces, ROWS, width), bf16), pltpu.VMEM((tokens, width), bf16)]
        + [pltpu.SemaphoreType.DMA((2, pieces))] * 4
        + [pltpu.SemaphoreType.DMA]
        + ([pltpu.VMEM((tokens // ROWS, width), f32)] if sums else [])
        + list(extra),
        input_output_aliases=aliases or {},
        compiler_params=pltpu.CompilerParams(
            collective_id=cid, has_side_effects=True, vmem_limit_bytes=VLIM),
        cost_estimate=cost(micros),
        name=name,
    )(*ins)


def from_behind(value, axis, by):
    length = lax.axis_size(axis)
    pairs = [(i, i + by) for i in range(length) if 0 <= i + by < length]
    return lax.ppermute(value, axis, pairs)


def norm_rows(values, gain):
    return values * lax.rsqrt(jnp.mean(values * values, axis=-1, keepdims=True) + 1e-06) * gain


def feed_forward(normed, cot, gu, down):
    units = down.shape[1]
    gate_up = dot(normed, gu)
    gate, up = gate_up[:, :units], gate_up[:, units:]
    sig = jax.nn.sigmoid(gate)
    act = low(gate * sig * up)
    grad = dot(cot, down)
    dgate = grad * up * sig * (1.0 + gate * (1.0 - sig))
    dgu = low(jnp.concatenate([dgate, grad * gate * sig], axis=1))
    return (act, dgu, dot(dgu, gu, NT, bf16), dot(act, down, NT, bf16))


class HalvingSum:
    def __init__(self, value, axis):
        self.value, self.axis = value, axis
        self.n, self.rank = lax.axis_size(axis), lax.axis_index(axis)
        bits = [1 << i for i in range(self.n.bit_length() - 1)]
        self.todo = [(self.halve, b) for b in bits] + [(self.double, b) for b in reversed(bits)]

    def swap(self, value, bit):
        return lax.ppermute(value, self.axis, [(i, i ^ bit) for i in range(self.n)])

    def halve(self, bit):
        half = self.value.shape[0] // 2
        up = (self.rank & bit) // bit
        kept = lax.dynamic_slice_in_dim(self.value, up * half, half)
        got = self.swap(lax.dynamic_slice_in_dim(self.value, (1 - up) * half, half), bit)
        self.value = (kept.astype(f32) + got.astype(f32)).astype(bf16)

    def double(self, bit):
        up = (self.rank & bit) != 0
        got = self.swap(self.value, bit)
        self.value = jnp.concatenate([jnp.where(up, got, self.value), jnp.where(up, self.value, got)])

    def step(self):
        if self.todo:
            act, bit = self.todo.pop(0)
            act(bit)

    def tie(self, *others):
        self.value, *others = lax.optimization_barrier((self.value, *others))
        return others


def low(x):
    return x.astype(bf16)


def dot(a, b, dims=NN, out=f32):
    return lax.dot_general(a, b, dims, preferred_element_type=out)


adam_step = 10.0


def rowwise(value):
    return with_layout_constraint(value, Layout(major_to_minor=tuple(range(value.ndim))))


def adamw(weight, grad, first, second, rate, shrink):
    grad = grad.astype(f32)
    first = 0.9 * first + 0.1 * grad
    second = 0.999 * second + 0.001 * grad * grad
    first_hat = first / (1.0 - 0.9**adam_step)
    second_hat = second / (1.0 - 0.999**adam_step)
    weight = weight - rate * (first_hat / (jnp.sqrt(second_hat) + 1e-08) + shrink * weight)
    return [weight, first, second]


def on_device(tokens_in, cotangent, segment_ids, pad_mask, *state):
    masters, firsts, seconds = state[0::3], state[1::3], state[2::3]
    (qk_proj, vg_proj, ab_proj, out_proj, gu_proj, down_proj,
     norm_gains, qk_conv, v_conv, out_gain, decay_params) = masters
    matrix_rate = 2.5 * D ** (-0.5)
    tokens = tokens_in.shape[0]
    dp = lax.axis_size("dp")
    mine = lax.axis_index("dp")
    start = mine * tokens
    rows = qk_proj.shape[0]
    heads, key, val = qk_proj.shape[2], qk_proj.shape[3], vg_proj.shape[3]
    units = gu_proj.shape[2]
    hk, hv = heads * key, heads * val
    mixer = Mixer(tokens, heads, key, val)

    small = [norm_gains, qk_conv, v_conv, out_gain]
    flat = jnp.concatenate([low(x).reshape(-1) for x in small])
    small_cols = pl.cdiv(flat.shape[0], rows)
    room = 128 - 2 * heads - small_cols
    flat = jnp.pad(flat, (0, rows * small_cols - flat.shape[0])).reshape(rows, small_cols)
    extra = jnp.concatenate(
        [low(ab_proj).reshape(rows, 2 * heads), flat, jnp.zeros((rows, room), bf16)], axis=1
    )
    vg_low = low(vg_proj)
    shard_one = jnp.concatenate(
        [low(qk_proj).reshape(rows, 2 * hk), vg_low[:, 0].reshape(rows, hv), extra], axis=1
    )
    shard_two = jnp.concatenate(
        [vg_low[:, 1].reshape(rows, hv), low(out_proj).reshape(hv, rows).T], axis=1
    )
    fused = units % BAND == 0 and dp == 8
    band = BAND if fused else units
    bands = [slice(at, at + band) for at in range(0, units, band)]
    shard_gu = jnp.concatenate([low(gu_proj[:, i, b]) for b in bands for i in (0, 1)], axis=1)
    shard_down = low(down_proj).T

    def gather(x):
        return lax.all_gather(x, "dp", axis=0, tiled=True)

    def scatter(value):
        return lax.psum_scatter(value, "dp", scatter_dimension=0, tiled=True)

    full_one = gather_call(3, "gather_one", shard_one) if dp == 8 else gather(shard_one)
    full_one, shard_two = lax.optimization_barrier((full_one, shard_two))
    full_two = gather(shard_two)

    cut = 2 * hk + hv
    flats = full_one[:, cut + 2 * heads : cut + 2 * heads + small_cols].reshape(dp, rows * small_cols)
    parts, at = [], 0
    for x in small:
        size = x.size
        parts.append(flats[:, at : at + size].reshape((dp,) + x.shape).astype(f32))
        at += size
    gains = jnp.moveaxis(parts[0], 0, 1).reshape(2, -1)
    taps_qk = jnp.moveaxis(parts[1], 0, 3).reshape(2, CONV, hk)
    taps_qk = jnp.moveaxis(taps_qk, 0, 1).reshape(CONV, 2 * hk)
    taps_v = jnp.moveaxis(parts[2], 0, 2).reshape(CONV, hv)
    gain = jnp.broadcast_to(parts[3].reshape(1, val), (8, val))
    decay_low = lax.optimization_barrier(low(decay_params)).astype(f32)

    padded_ids = jnp.concatenate([jnp.full((4,), -1, jnp.int32), segment_ids])
    here_ids = lax.dynamic_slice_in_dim(padded_ids, start + 1, tokens + SPAN)
    prior_ids = lax.dynamic_slice_in_dim(padded_ids, start, tokens + SPAN)
    positions = start - SPAN + jnp.arange(tokens + SPAN, dtype=jnp.int32)
    resets_ext = ((here_ids != prior_ids) | (positions == 0)).astype(f32)
    resets_here = resets_ext[SPAN:]
    keep_ext = 1.0 - resets_ext
    valid_rows = [jnp.ones((tokens,), f32)]
    for lag in range(1, SPAN + 1):
        valid_rows.append(valid_rows[-1] * keep_ext[SPAN - lag + 1 : SPAN - lag + 1 + tokens])
    lag_valid = jnp.stack(valid_rows)
    pad = lax.dynamic_slice_in_dim(pad_mask, start, tokens).astype(f32)

    x_rim = from_behind(tokens_in[tokens - HALO :], "dp", 1)
    x = tokens_in.astype(f32)
    normed = low(norm_rows(x, gains[0]))
    normed_rim = low(norm_rows(x_rim.astype(f32), gains[0]))
    pre_qk = dot(normed, full_one[:, : 2 * hk], out=bf16)
    pre_v = dot(normed, full_one[:, 2 * hk : cut], out=bf16)
    mixed = dot(normed, full_one[:, cut:])[:, : 2 * heads].reshape(tokens, 2, heads)
    rim = low(dot(normed_rim, full_one[:, :cut])).astype(f32)
    (g, b), pull_gates = jax.vjp(lambda ab, dec: gates_of(ab, dec, pad), mixed, decay_low)
    aux, rowform = token_tables(g, b, pad, lag_valid, resets_here)

    rim_qk, rim_v = rim[:, : 2 * hk], rim[:, 2 * hk :]
    q, k, w, u, p, inv, r, r_end = mixer.forward_local(
        pre_qk, pre_v, rim_qk, rim_v, taps_qk, taps_v, aux, rowform
    )
    spot = mine.astype(jnp.int32).reshape(1)
    r_end, full_two = lax.optimization_barrier((low(r_end), full_two))
    gate_pre = dot(normed, full_two[:, :hv])
    maps = lax.all_gather(r_end, "dp")
    maps, gate_pre = lax.optimization_barrier((maps, gate_pre))
    y, st, vn, o = mixer.output(spot, maps, r, w, u, p, q, aux, gate_pre, gain)

    out_t = full_two[:, hv:]
    mp = lax.axis_size("mp")
    gain_one, gain_two = (jnp.broadcast_to(gains[i : i + 1], (8, gains.shape[1])) for i in (0, 1))
    half, width = tokens // 2, tokens_in.shape[1]
    like = sds((tokens, width), bf16)
    like_gain = sds(gain_two.shape)
    part_one = dot(y, out_t, NT, bf16)
    if fused:
        ffn_full = [sds((tokens, units), bf16), sds((tokens, 2 * units), bf16), like]
        ffn_weights = [sds((dp * rows, 2 * units), bf16), sds((dp * rows, units), bf16)]
        ffn_room = [pltpu.VMEM((half, units), bf16), pltpu.VMEM((half, 2 * units), bf16), pltpu.VMEM((half, width), bf16),
                    *[pltpu.VMEM(w.shape, bf16) for w in ffn_weights], pltpu.SemaphoreType.DMA((5,))]
        swaps = (len(Gather.KINDS), 2)
        attn, normed_two, two_a, act, dgu, down_part, full_gu, full_down = line_call(
            kernel_hidden_ffn, 0, "sum_hidden", mp,
            [part_one, tokens_in, gain_two, cotangent, shard_gu, shard_down],
            [like, like, sds((half, width), bf16)] + ffn_full + ffn_weights,
            ffn_room + [pltpu.SemaphoreType.DMA(swaps)] * 2 + [pltpu.SemaphoreType.DMA((2,))],
            away_in=(4, 5), away_out=(0, 3, 4, 5, 6, 7), sums=False, micros=120
        )
        total_two, dattn, dgain_two, act, dgu, down_part = line_call(
            kernel_dhidden_ffn, 1, "sum_dhidden", mp,
            [two_a, tokens_in, attn, cotangent, gain_two, normed_two, full_gu, full_down, act, dgu, down_part],
            [like, like, like_gain] + ffn_full,
            [pltpu.VMEM((tokens, width), bf16), pltpu.VMEM((half, width), bf16), pltpu.SemaphoreType.DMA((2,))] + ffn_room,
            away_in=(0, 5, 6, 7, 8, 9, 10), away_out=(0, 3, 4, 5), aliases={8: 3, 9: 4, 10: 5}, micros=120
        )
    else:
        full_gu, full_down = gather(shard_gu), gather(shard_down)
        attn, normed_two = line_call(
            kernel_hidden, 0, "sum_hidden", mp, [part_one, tokens_in, gain_two], [like, like],
            away_out=(0,), sums=False
        )
        act, dgu, two, down_part = feed_forward(normed_two, cotangent, full_gu, full_down)
        total_two, dattn, dgain_two = line_call(
            kernel_dhidden, 1, "sum_dhidden", mp, [two, tokens_in, attn, cotangent, gain_two],
            [like, like, like_gain], away_out=(0,)
        )
    down_sum = HalvingSum(down_part, "mp")
    (dattn,) = down_sum.tie(dattn)
    down_sum.step()
    dy = dot(dattn, out_t)
    grad_out = dot(dattn, y, TN, bf16)
    do, dgate, dgain, z, z_end = mixer.backward_local(dy, o, gate_pre, gain, aux, q, k, w, p)
    z_end, act, dgu = down_sum.tie(low(z_end), act, dgu)
    down_sum.step()
    grad_gu = dot(normed_two, dgu, TN, bf16)
    grad_down = dot(cotangent, act, TN, bf16)
    back_maps = lax.all_gather(z_end, "dp")
    grad_gate_w = dot(normed, dgate, TN, bf16)
    grad_two = jnp.concatenate([grad_gate_w, grad_out], axis=1)
    back_maps, grad_two, grad_gu, grad_down = down_sum.tie(back_maps, grad_two, grad_gu, grad_down)
    down_sum.step()
    red_gu = scatter(grad_gu)
    red_down = scatter(grad_down)
    red_two = scatter(grad_two)
    (dqk, dv, tail_qk, tail_v, head_qk, head_v, dtaps_qk, dtaps_v, dcg, dbeta) = mixer.backward(
        spot, back_maps, z, do, st, vn, q, k, w, u, p, inv, aux, rowform,
        pre_qk, pre_v, rim_qk, rim_v, taps_qk, taps_v
    )
    dqk, dv, head_qk, head_v = down_sum.tie(dqk, dv, head_qk, head_v)
    down_sum.step()
    heads_back = from_behind(jnp.concatenate([head_qk, head_v], axis=1), "dp", -1)
    dqk = lax.dynamic_update_slice(dqk, low(tail_qk + heads_back[:, : 2 * hk]), (tokens - HALO, 0))
    dv = lax.dynamic_update_slice(dv, low(tail_v + heads_back[:, 2 * hk :]), (tokens - HALO, 0))
    dmixed, ddecay = pull_gates((in_chunks(dcg, True), dbeta))
    dab = jnp.pad(low(dmixed.reshape(tokens, 2 * heads)), ((0, 0), (0, 128 - 2 * heads)))
    dpre = jnp.concatenate([dqk, dv, dab], axis=1)
    grad_one = dot(normed, dpre, TN, bf16)
    grad_small = [
        dtaps_qk.reshape(CONV, 2, heads, dp, -1).transpose(1, 0, 2, 3, 4),
        dtaps_v.reshape(CONV, heads, dp, -1),
    ]
    grad_flat = jnp.concatenate(
        [jnp.moveaxis(gs, -2, 0).reshape(dp, -1) for gs in grad_small], axis=1
    )
    high = low(ddecay).astype(f32)
    pair = jnp.stack([high, ddecay - high]).reshape(1, 1, -1)
    slots = jnp.where(jnp.arange(dp)[None, :, None] == mine, pair, 0.0)
    slots = jnp.broadcast_to(slots, (dp,) + slots.shape[1:]).reshape(dp, -1)
    used = grad_flat.shape[1]
    grad_flat = jnp.concatenate([grad_flat, slots], axis=1)
    grad_flat = jnp.pad(grad_flat, ((0, 0), (0, rows * small_cols - grad_flat.shape[1])))
    grad_flat = low(grad_flat).reshape(dp * rows, small_cols)
    grad_one = lax.dynamic_update_slice(grad_one, grad_flat, (0, cut + 2 * heads))
    grad_one, dpre = lax.optimization_barrier((grad_one, dpre))
    red_one = scatter(grad_one)
    normed_part = low(dot(dpre, full_one, NT) + dot(dgate, full_two[:, :hv], NT))
    while down_sum.todo:
        down_sum.step()
    (normed_part,) = down_sum.tie(normed_part)
    block_out = low(x + attn.astype(f32) + down_sum.value.astype(f32))
    swap = (8, max(rows, val))
    input_grad, dgains = line_call(
        partial(kernel_dinput, dp), 2, "sum_dinput", mp,
        [normed_part, tokens_in, attn, cotangent, total_two, gain_one, gain_two, dgain_two, dgain],
        [sds((tokens, width)), sds(swap)],
        [pltpu.VMEM((dp,) + swap, f32)] * 2 + [pltpu.SemaphoreType.DMA((dp,))] * 2
        + [pltpu.VMEM((mp,) + dgain.shape, f32)] + [pltpu.SemaphoreType.DMA((mp,))] * 2,
    )
    red_flat = red_one[:, cut + 2 * heads : cut + 2 * heads + small_cols].astype(f32).reshape(-1)
    red_small, at = [dgains[:2, :rows]], 0
    for s in small[1:3]:
        red_small.append(red_flat[at : at + s.size].reshape(s.shape))
        at += s.size
    red_small.append(lax.dynamic_slice_in_dim(dgains[2], mine * out_gain.size, out_gain.size))
    slots = red_flat[used : used + slots.shape[1]].reshape((dp, 2) + ddecay.shape)
    grads = [
        red_one[:, : 2 * hk].reshape(qk_proj.shape),
        jnp.stack([red_one[:, 2 * hk : cut].reshape(rows, heads, val),
                   red_two[:, :hv].reshape(rows, heads, val)], axis=1),
        red_one[:, cut : cut + 2 * heads].reshape(ab_proj.shape),
        rowwise(red_two[:, hv:].T).reshape(out_proj.shape),
        rowwise(red_gu.reshape(rows, len(bands), 2, band).transpose(0, 2, 1, 3).reshape(gu_proj.shape)),
        rowwise(red_down.T),
    ] + red_small + [jnp.sum(slots, axis=(0, 1))]
    rates = [matrix_rate] * 6 + [0.5, 1.0, 1.0, 0.5, 2.0]
    shrinks = [0.1] * 6 + [0.0] * 5
    updates = []
    for i in range(11):
        updates += adamw(masters[i], grads[i], firsts[i], seconds[i], rates[i], shrinks[i])
    copies = [low(updates[3 * i]) for i in range(6)]
    return (block_out, input_grad, *updates, *copies)


def solution(mesh):
    weights = [
        P("dp", None, "mp", None),
        P("dp", None, "mp", None),
        P("dp", None, "mp"),
        P("mp", None, "dp"),
        P("dp", None, "mp"),
        P("mp", "dp"),
        P(None, "dp"),
        P(None, None, "mp", "dp"),
        P(None, "mp", "dp"),
        P("dp"),
        P(None, "mp"),
    ]
    thrice = tuple(w for w in weights for _ in range(3))
    rowwise = P("dp", None)
    return jax.shard_map(
        on_device,
        mesh=mesh,
        in_specs=(rowwise, rowwise, P(), P()) + thrice,
        out_specs=(rowwise, rowwise) + thrice + tuple(weights[:6]),
        check_vma=False,
    )
```

```python
from functools import partial

import jax
import jax.numpy as jnp
from jax import lax
from jax.experimental import pallas as pl
from jax.experimental.layout import Layout, with_layout_constraint
from jax.experimental.pallas import tpu as pltpu
from jax.sharding import PartitionSpec as P

D = 2048
CONV = 4
SPAN = CONV - 1
CH = 128
HALO = 8
f32 = jnp.float32
bf16 = jnp.bfloat16
VLIM = 60 * 2**20

NN = (((1,), (0,)), ((), ()))
NT = (((1,), (1,)), ((), ()))
TN = (((0,), (0,)), ((), ()))

N_INV = 3
N_FWD = 1
N_SCAN = 1
N_BWD = 1


def mm(a, b, dims=NN, passes=1):
    def dot(x, y):
        return lax.dot_general(x, y, dims, preferred_element_type=f32)

    ah, bh = a.astype(bf16), b.astype(bf16)
    out = dot(ah, bh)
    if passes in (3, "right"):
        out = out + dot((a - ah.astype(f32)).astype(bf16), bh)
    if passes in (3, "left"):
        out = out + dot(ah, (b - bh.astype(f32)).astype(bf16))
    return out


def grid_iotas(n):
    return (
        lax.broadcasted_iota(jnp.int32, (n, n), 0),
        lax.broadcasted_iota(jnp.int32, (n, n), 1),
    )


def unit_lower_inverse(lowers, n):
    rows, cols = grid_iotas(n)
    eye = (rows == cols).astype(f32)
    small = lax.shift_right_logical(rows, 3) == lax.shift_right_logical(cols, 3)
    diag = [jnp.where(small, low, 0.0) for low in lowers]
    two = [mm(d, d) for d in diag]
    four = [mm(t, t, NN, N_INV) for t in two]
    inv = [eye - d for d in diag]
    inv = [x + mm(x, t, NN, "left") for x, t in zip(inv, two)]
    inv = [x + mm(x, f, NN, N_INV) for x, f in zip(inv, four)]
    bits = 3
    while (1 << bits) < n:
        wide = lax.shift_right_logical(rows, bits + 1) == lax.shift_right_logical(cols, bits + 1)
        fine = lax.shift_right_logical(rows, bits) != lax.shift_right_logical(cols, bits)
        off = [jnp.where(wide & fine, low, 0.0) for low in lowers]
        half = [mm(x, o, NN, "right") for x, o in zip(inv, off)]
        inv = [x - mm(y, x, NN, N_INV) for x, y in zip(inv, half)]
        bits += 1
    return inv


def sigmoid(x):
    return 1.0 / (1.0 + jnp.exp(-x))


def decay_matrix(aux, rows, h, heads, tri):
    cg = aux[:, 5 + h : 6 + h]
    cg_row = rows[1 + h : 2 + h, :]
    same = (aux[:, 4:5] == rows[0:1, :]) & tri
    return jnp.where(same, jnp.exp(jnp.where(same, cg - cg_row, 0.0)), 0.0)


def conv_of(ext_ref, taps_ref, aux, c0, c1):
    n = aux.shape[0]
    total = ext_ref[HALO : HALO + n, c0:c1] * taps_ref[SPAN : SPAN + 1, c0:c1]
    for lag in range(1, SPAN + 1):
        total = total + ext_ref[HALO - lag : HALO - lag + n, c0:c1] * (
            taps_ref[SPAN - lag : SPAN - lag + 1, c0:c1] * aux[:, lag - 1 : lag]
        )
    return total


def unit_of(act):
    return lax.rsqrt(jnp.sum(act * act, axis=-1, keepdims=True) + 1e-06)


def kernel_a(heads, key, val, pqk, pv, hqk, hv, tqk, tv, aux_ref, rows_ref,
             q_out, k_out, w_out, u_out, p_out, t_out, r_out, rend_out,
             xqk, xv, state):
    c = pl.program_id(0)
    n = pqk.shape[0]
    hk = heads * key

    @pl.when(c == 0)
    def _():
        xqk[0:HALO, :] = hqk[...]
        xv[0:HALO, :] = hv[...]
        r, s = (lax.broadcasted_iota(jnp.int32, (key, key + val), i) for i in (0, 1))
        for h in range(heads):
            state[h] = (r == s).astype(f32)

    xqk[HALO:, :] = pqk[...].astype(f32)
    xv[HALO:, :] = pv[...].astype(f32)
    aux = aux_ref[...]
    rows = rows_ref[0]
    ti, si = grid_iotas(n)
    tri = ti >= si
    lowers, queries, keys = [], [], []
    for h in range(heads):
        uq = conv_of(xqk, tqk, aux, h * key, (h + 1) * key)
        uk = conv_of(xqk, tqk, aux, hk + h * key, hk + (h + 1) * key)
        aq = uq * sigmoid(uq)
        ak = uk * sigmoid(uk)
        q = aq * unit_of(aq) * key ** (-0.5)
        k = ak * unit_of(ak)
        q_out[:, h * key : (h + 1) * key] = q
        k_out[:, h * key : (h + 1) * key] = k
        dec = decay_matrix(aux, rows, h, heads, tri)
        beta = aux[:, 5 + 3 * heads + h : 6 + 3 * heads + h]
        p_out[:, h * n : (h + 1) * n] = mm(q, k, NT, N_FWD) * dec
        lower = jnp.where(ti > si, mm(k, k, NT, N_FWD) * dec, 0.0) * beta
        lowers.append(lower.astype(bf16).astype(f32))
        queries.append(q)
        keys.append(k)
    invs = unit_lower_inverse(lowers, n)
    for h in range(heads):
        k = keys[h]
        beta = aux[:, 5 + 3 * heads + h : 6 + 3 * heads + h]
        fs = aux[:, 5 + heads + h : 6 + heads + h]
        lr = aux[:, 5 + 2 * heads + h : 6 + 2 * heads + h]
        uv = conv_of(xv, tv, aux, h * val, (h + 1) * val)
        v = uv * sigmoid(uv)
        t_out[:, h * n : (h + 1) * n] = invs[h]
        w = mm(invs[h], (beta * fs) * k, NN, N_FWD)
        u = mm(invs[h], beta * v, NN, N_FWD)
        w_out[:, h * key : (h + 1) * key] = w
        u_out[:, h * val : (h + 1) * val] = u
        st = state[h]
        r_out[0, h] = st
        new = jnp.concatenate([jnp.zeros((n, key), f32), u], axis=1) - mm(w, st, NN, N_SCAN)
        st = fs[n - 1 :, :] * st + mm(lr * k, new, TN, N_SCAN)
        state[h] = st
        rend_out[h] = st
    xqk[0:HALO, :] = xqk[n:, :]
    xv[0:HALO, :] = xv[n:, :]


def kernel_b(heads, key, val, mine, gath, r_in, w_in, u_in, p_in, q_in, aux_ref, gate_in, gain_ref,
             y_out, s_out, vn_out, o_out, start):
    c = pl.program_id(0)
    n = w_in.shape[0]

    @pl.when(c == 0)
    def _():
        start[...] = jnp.zeros_like(start)

        @pl.loop(0, mine[0])
        def _(d):
            for h in range(heads):
                start[h] = gath[d, h, :, key:].astype(f32) + mm(gath[d, h, :, :key], start[h], NN, N_FWD)

    aux = aux_ref[...]
    pad = aux[:, 3:4]
    for h in range(heads):
        fs = aux[:, 5 + heads + h : 6 + heads + h]
        st = r_in[0, h, :, key:] + mm(r_in[0, h, :, :key], start[h], NN, N_FWD)
        s_out[0, h] = st
        v0, v1 = h * val, (h + 1) * val
        new = u_in[:, v0:v1] - mm(w_in[:, h * key : (h + 1) * key], st, NN, N_FWD)
        vn_out[:, v0:v1] = new
        o = mm(fs * q_in[:, h * key : (h + 1) * key], st, NN, N_FWD)
        o = o + mm(p_in[:, h * n : (h + 1) * n], new, NN, N_FWD)
        o_out[:, v0:v1] = o
        scale = lax.rsqrt(jnp.mean(o * o, axis=-1, keepdims=True) + 1e-05)
        gate = gate_in[:, v0:v1]
        y = o * scale * gain_ref[0:1, :] * (gate * sigmoid(gate)) * pad
        y_out[:, v0:v1] = y.astype(bf16)


def kernel_c(heads, key, val, dy_in, o_in, gate_in, gain_ref, aux_ref, q_in, k_in, w_in, p_in,
             do_out, dgate_out, dgain_out, z_out, zend_out, carry):
    c = pl.program_id(0)
    n = dy_in.shape[0]

    @pl.when(c == 0)
    def _():
        r, s = (lax.broadcasted_iota(jnp.int32, (key, key + val), i) for i in (0, 1))
        for h in range(heads):
            carry[h] = (r == s).astype(f32)
        dgain_out[...] = jnp.zeros_like(dgain_out)

    aux = aux_ref[...]
    pad = aux[:, 3:4]
    gain = gain_ref[0:1, :]
    for h in range(heads):
        v0, v1 = h * val, (h + 1) * val
        k0, k1 = h * key, (h + 1) * key
        fs = aux[:, 5 + heads + h : 6 + heads + h]
        lr = aux[:, 5 + 2 * heads + h : 6 + 2 * heads + h]
        o = o_in[:, v0:v1]
        gate = gate_in[:, v0:v1]
        dy = dy_in[:, v0:v1] * pad
        scale = lax.rsqrt(jnp.mean(o * o, axis=-1, keepdims=True) + 1e-05)
        sig = sigmoid(gate)
        act = gate * sig
        unit = o * scale
        prod = dy * unit
        dgain_out[0:1, :] += jnp.sum(prod * act, axis=0, keepdims=True)
        dgate_out[:, v0:v1] = (prod * gain * (sig * (1.0 + gate * (1.0 - sig)))).astype(bf16)
        dn = dy * gain * act
        do = scale * (dn - unit * jnp.mean(dn * unit, axis=-1, keepdims=True))
        do_out[:, v0:v1] = do
        zst = carry[h]
        z_out[0, h] = zst
        lead = jnp.zeros((n, key), f32)
        dnew = jnp.concatenate([lead, mm(p_in[:, h * n : (h + 1) * n], do, TN, N_FWD)], axis=1)
        dnew = dnew + mm(lr * k_in[:, k0:k1], zst, NN, N_SCAN)
        own = jnp.concatenate(
            [jnp.zeros((key, key), f32), mm(fs * q_in[:, k0:k1], do, TN, N_FWD)], axis=1
        )
        zst = fs[n - 1 :, :] * zst + own - mm(w_in[:, k0:k1], dnew, TN, N_SCAN)
        carry[h] = zst
        zend_out[h] = zst


def through_act(u, grad):
    sig = sigmoid(u)
    return grad * (sig * (1.0 + u * (1.0 - sig)))


def kernel_d(heads, key, val, count, mine, gath, z_in, do_in, s_in, vn_in, q_in, k_in, w_in, u_in, p_in, t_in,
             aux_ref, rows_ref, pqk, pv, bqk, bv, hqk, hv, tqk, tv,
             dqk_out, dv_out, tailqk, tailv, headqk, headv, dtqk, dtv, dcg_out, dbeta_out,
             xqk, xv, dxqk, dxv, end):
    c = pl.program_id(0)
    steps = pl.num_programs(0)
    n = do_in.shape[0]
    hk = heads * key

    @pl.when(c == 0)
    def _():
        end[...] = jnp.zeros_like(end)

        @pl.loop(0, count - 1 - mine[0])
        def _(i):
            d = count - 1 - i
            for h in range(heads):
                end[h] = gath[d, h, :, key:].astype(f32) + mm(gath[d, h, :, :key], end[h], NN, N_FWD)

        dxqk[...] = jnp.zeros_like(dxqk)
        dxv[...] = jnp.zeros_like(dxv)
        dtqk[...] = jnp.zeros_like(dtqk)
        dtv[...] = jnp.zeros_like(dtv)

    @pl.when(c < steps - 1)
    def _():
        xqk[0:HALO, :] = bqk[...].astype(f32)[bqk.shape[0] - HALO :]
        xv[0:HALO, :] = bv[...].astype(f32)[bv.shape[0] - HALO :]

    @pl.when(c == steps - 1)
    def _():
        xqk[0:HALO, :] = hqk[...]
        xv[0:HALO, :] = hv[...]

    xqk[HALO:, :] = pqk[...].astype(f32)
    xv[HALO:, :] = pv[...].astype(f32)
    aux = aux_ref[...]
    rows = rows_ref[0]
    ti, si = grid_iotas(n)
    tri = ti >= si
    last = (lax.broadcasted_iota(jnp.int32, (n, 1), 0) == n - 1).astype(f32)
    dxqk[n:, :] = dxqk[0:HALO, :]
    dxv[n:, :] = dxv[0:HALO, :]
    dxqk[0:n, :] = jnp.zeros((n, 2 * hk), f32)
    dxv[0:n, :] = jnp.zeros((n, heads * val), f32)

    def conv_back(du, ext, dext, taps, dtaps, c0, c1):
        for lag in range(SPAN + 1):
            part = du if lag == 0 else du * aux[:, lag - 1 : lag]
            dtaps[SPAN - lag : SPAN - lag + 1, c0:c1] += jnp.sum(
                part * ext[HALO - lag : HALO - lag + n, c0:c1], axis=0, keepdims=True
            )
            spot = slice(HALO - lag, HALO - lag + n)
            dext[spot, c0:c1] += part * taps[SPAN - lag : SPAN - lag + 1, c0:c1]

    for h in range(heads):
        v0, v1 = h * val, (h + 1) * val
        k0, k1 = h * key, (h + 1) * key
        fs = aux[:, 5 + heads + h : 6 + heads + h]
        lr = aux[:, 5 + 2 * heads + h : 6 + 2 * heads + h]
        beta = aux[:, 5 + 3 * heads + h : 6 + 3 * heads + h]
        q, k = q_in[:, k0:k1], k_in[:, k0:k1]
        w, u = w_in[:, k0:k1], u_in[:, v0:v1]
        p, inv = p_in[:, h * n : (h + 1) * n], t_in[:, h * n : (h + 1) * n]
        do, new, st = do_in[:, v0:v1], vn_in[:, v0:v1], s_in[0, h]
        dst = z_in[0, h, :, key:] + mm(z_in[0, h, :, :key], end[h], NN, N_BWD)
        dec = decay_matrix(aux, rows, h, heads, tri)
        kk = mm(k, k, NT, N_BWD)
        kl = lr * k
        dnew = mm(p, do, TN, N_BWD) + mm(kl, dst, NN, N_BWD)
        dp = mm(do, new, NT, N_BWD)
        dqf = mm(do, st, NT, N_BWD)
        dkl = mm(new, dst, NT, N_BWD)
        dw = -mm(dnew, st, NT, N_BWD)
        drv = mm(inv, dnew, TN, N_BWD)
        drk = mm(inv, dw, TN, N_BWD)
        dlow = -(mm(drv, u, NT, N_BWD) + mm(drk, w, NT, N_BWD))
        dlow = jnp.where(ti > si, dlow, 0.0) * dec
        dkk = dlow * beta
        hh = dp * dec
        pairs = dkk * kk + dp * p
        dq = fs * dqf + mm(hh, k, NN, N_BWD)
        dk = mm(hh, q, TN, N_BWD) + mm(dkk, k, NN, N_BWD) + mm(dkk, k, TN, N_BWD)
        dk = dk + lr * dkl + (beta * fs) * drk
        uv = conv_of(xv, tv, aux, v0, v1)
        v = uv * sigmoid(uv)
        kd = jnp.sum(k * drk, axis=-1, keepdims=True) * fs
        dbeta = jnp.sum(dlow * kk, axis=-1, keepdims=True) + kd
        dbeta = dbeta + jnp.sum(v * drv, axis=-1, keepdims=True)
        leave = lr * jnp.sum(k * dkl, axis=-1, keepdims=True)
        dcg = jnp.sum(pairs, axis=-1, keepdims=True) + beta * kd - leave
        dcg = dcg + fs * jnp.sum(q * dqf, axis=-1, keepdims=True)
        ones = jnp.ones((n, 8), f32)
        dcg = dcg - mm(pairs, ones, TN, 3)[:, 0:1]
        tail = jnp.sum(leave, axis=0, keepdims=True) + fs[n - 1 :, :] * jnp.sum(
            jnp.sum(st * dst, axis=-1, keepdims=True), axis=0, keepdims=True
        )
        dcg_out[:, h : h + 1] = dcg + last * tail
        dbeta_out[:, h : h + 1] = dbeta
        conv_back(through_act(uv, beta * drv), xv, dxv, tv, dtv, v0, v1)
        for off, grad, size in ((0, dq, key ** (-0.5)), (hk, dk, 1.0)):
            uu = conv_of(xqk, tqk, aux, off + k0, off + k1)
            act = uu * sigmoid(uu)
            rs = unit_of(act)
            da = (rs * size) * (grad - act * (rs * rs) * jnp.sum(act * grad, axis=-1, keepdims=True))
            conv_back(through_act(uu, da), xqk, dxqk, tqk, dtqk, off + k0, off + k1)
    dqk_out[...] = dxqk[HALO:, :].astype(bf16)
    dv_out[...] = dxv[HALO:, :].astype(bf16)

    @pl.when(c == 0)
    def _():
        tailqk[...] = dxqk[n:, :]
        tailv[...] = dxv[n:, :]

    headqk[...] = dxqk[0:HALO, :]
    headv[...] = dxv[0:HALO, :]


def cost(microseconds):
    return pl.CostEstimate(
        flops=int(microseconds * 1e9), bytes_accessed=int(microseconds * 3.3e6), transcendentals=0)


def params(**kw):
    return pltpu.CompilerParams(vmem_limit_bytes=VLIM, dimension_semantics=("arbitrary",), **kw)


def sds(shape, dtype=f32):
    return jax.ShapeDtypeStruct(shape, dtype)


class Mixer:
    def __init__(self, tokens, heads, key, val):
        self.sizes = (heads, key, val)
        self.tokens, self.n, self.steps = tokens, CH, tokens // CH

    def rows(self, width, back=False):
        m = self.steps - 1
        return pl.BlockSpec((self.n, width), (lambda c: (m - c, 0)) if back else (lambda c: (c, 0)))

    def lead(self, shape, back=False):
        m, rest = self.steps - 1, (0,) * len(shape)
        return pl.BlockSpec((1,) + shape, (lambda c: (m - c,) + rest) if back else (lambda c: (c,) + rest))

    def whole(self, shape):
        rest = (0,) * len(shape)
        return pl.BlockSpec(shape, lambda c: rest)

    def forward_local(self, pqk, pv, hqk, hv, tqk, tv, aux, rows):
        heads, key, val = self.sizes
        t, n, s = self.tokens, self.n, self.steps
        hk, hv_ = heads * key, heads * val
        wide = key + val
        return pl.pallas_call(
            partial(kernel_a, heads, key, val),
            grid=(s,),
            in_specs=[self.rows(2 * hk), self.rows(hv_), self.whole(hqk.shape), self.whole(hv.shape),
                      self.whole(tqk.shape), self.whole(tv.shape), self.rows(aux.shape[1]), self.lead(rows.shape[1:])],
            out_specs=[self.rows(hk), self.rows(hk), self.rows(hk), self.rows(hv_), self.rows(heads * n), self.rows(heads * n),
                       self.lead((heads, key, wide)), self.whole((heads, key, wide))],
            out_shape=[sds((t, hk)), sds((t, hk)), sds((t, hk)), sds((t, hv_)), sds((t, heads * n)), sds((t, heads * n)),
                       sds((s, heads, key, wide)), sds((heads, key, wide))],
            scratch_shapes=[pltpu.VMEM((HALO + n, 2 * hk), f32), pltpu.VMEM((HALO + n, hv_), f32),
                            pltpu.VMEM((heads, key, wide), f32)],
            compiler_params=params(),
            cost_estimate=cost(39),
            name="mixer_local",
        )(pqk, pv, hqk, hv, tqk, tv, aux, rows)

    def output(self, mine, gath, r, w, u, p, q, aux, gate, gain):
        heads, key, val = self.sizes
        t, n, s = self.tokens, self.n, self.steps
        hk, hv_ = heads * key, heads * val
        return pl.pallas_call(
            partial(kernel_b, heads, key, val),
            grid=(s,),
            in_specs=[pl.BlockSpec(memory_space=pltpu.SMEM), self.whole(gath.shape), self.lead((heads, key, key + val)),
                      self.rows(hk), self.rows(hv_), self.rows(heads * n), self.rows(hk), self.rows(aux.shape[1]),
                      self.rows(hv_), self.whole(gain.shape)],
            out_specs=[self.rows(hv_), self.lead((heads, key, val)), self.rows(hv_), self.rows(hv_)],
            out_shape=[sds((t, hv_), bf16), sds((s, heads, key, val)), sds((t, hv_)), sds((t, hv_))],
            scratch_shapes=[pltpu.VMEM((heads, key, val), f32)],
            compiler_params=params(),
            cost_estimate=cost(18),
            name="mixer_output",
        )(mine, gath, r, w, u, p, q, aux, gate, gain)

    def backward_local(self, dy, o, gate, gain, aux, q, k, w, p):
        heads, key, val = self.sizes
        t, n, s = self.tokens, self.n, self.steps
        hk, hv_ = heads * key, heads * val
        wide = key + val
        back = partial(self.rows, back=True)
        return pl.pallas_call(
            partial(kernel_c, heads, key, val),
            grid=(s,),
            in_specs=[back(hv_), back(hv_), back(hv_), self.whole(gain.shape), back(aux.shape[1]),
                      back(hk), back(hk), back(hk), back(heads * n)],
            out_specs=[back(hv_), back(hv_), self.whole((8, val)), self.lead((heads, key, wide), True),
                       self.whole((heads, key, wide))],
            out_shape=[sds((t, hv_)), sds((t, hv_), bf16), sds((8, val)), sds((s, heads, key, wide)),
                       sds((heads, key, wide))],
            scratch_shapes=[pltpu.VMEM((heads, key, wide), f32)],
            compiler_params=params(),
            cost_estimate=cost(17),
            name="mixer_back_local",
        )(dy, o, gate, gain, aux, q, k, w, p)

    def backward(self, mine, gath, z, do, st, vn, q, k, w, u, p, inv, aux, rows, pqk, pv, hqk, hv, tqk, tv):
        heads, key, val = self.sizes
        t, n, s = self.tokens, self.n, self.steps
        hk, hv_ = heads * key, heads * val
        back = partial(self.rows, back=True)
        ratio = n // 16
        m = s - 1

        def before(width):
            return pl.BlockSpec((16, width), lambda c: (jnp.maximum((m - c) * ratio - 1, 0), 0))

        return pl.pallas_call(
            partial(kernel_d, heads, key, val, gath.shape[0]),
            grid=(s,),
            in_specs=[pl.BlockSpec(memory_space=pltpu.SMEM), self.whole(gath.shape), self.lead((heads, key, key + val), True),
                      back(hv_), self.lead((heads, key, val), True), back(hv_), back(hk), back(hk), back(hk), back(hv_),
                      back(heads * n), back(heads * n), back(aux.shape[1]), self.lead(rows.shape[1:], True),
                      back(2 * hk), back(hv_), before(2 * hk), before(hv_), self.whole(hqk.shape), self.whole(hv.shape),
                      self.whole(tqk.shape), self.whole(tv.shape)],
            out_specs=[back(2 * hk), back(hv_), self.whole((HALO, 2 * hk)), self.whole((HALO, hv_)),
                       self.whole((HALO, 2 * hk)), self.whole((HALO, hv_)), self.whole((CONV, 2 * hk)), self.whole((CONV, hv_)),
                       back(heads), back(heads)],
            out_shape=[sds((t, 2 * hk), bf16), sds((t, hv_), bf16), sds((HALO, 2 * hk)), sds((HALO, hv_)),
                       sds((HALO, 2 * hk)), sds((HALO, hv_)), sds((CONV, 2 * hk)), sds((CONV, hv_)),
                       sds((t, heads)), sds((t, heads))],
            scratch_shapes=[pltpu.VMEM((HALO + n, 2 * hk), f32), pltpu.VMEM((HALO + n, hv_), f32),
                            pltpu.VMEM((HALO + n, 2 * hk), f32), pltpu.VMEM((HALO + n, hv_), f32),
                            pltpu.VMEM((heads, key, val), f32)],
            compiler_params=params(),
            cost_estimate=cost(50),
            name="mixer_back",
        )(mine, gath, z, do, st, vn, q, k, w, u, p, inv, aux, rows, pqk, pv, pqk, pv, hqk, hv, tqk, tv)


def gates_of(mixed_ab, decay, pad):
    g = -jnp.exp(decay[0]) * jax.nn.softplus(mixed_ab[:, 0] + decay[1]) * pad[:, None]
    b = jax.nn.sigmoid(mixed_ab[:, 1]) * pad[:, None]
    return (g, b)


def in_chunks(values, upper):
    tri = jnp.tril(jnp.ones((CH, CH), f32))
    tri = tri.T if upper else tri
    parts = values.reshape(-1, CH, values.shape[1])
    return jnp.einsum("ts,csh->cth", tri, parts, precision=lax.Precision.HIGHEST).reshape(values.shape)


def token_tables(g, b, pad, lag_valid, resets):
    t, heads = g.shape
    sums = in_chunks(jnp.concatenate([g, resets[:, None]], axis=1), False)
    cg, count = sums[:, :heads], sums[:, heads:]
    ends = sums.reshape(-1, CH, heads + 1)[:, -1:]
    ends = jnp.broadcast_to(ends, (ends.shape[0], CH, heads + 1)).reshape(t, heads + 1)
    fs = jnp.where(count == 0, jnp.exp(cg), 0.0)
    to_end = count == ends[:, heads:]
    lr = jnp.where(to_end, jnp.exp(jnp.where(to_end, ends[:, :heads] - cg, 0.0)), 0.0)
    aux = jnp.concatenate([lag_valid[1:].T, pad[:, None], count, cg, fs, lr, b], axis=1)
    rows = jnp.concatenate([count, cg], axis=1).reshape(-1, CH, heads + 1).transpose(0, 2, 1)
    return (aux, rows)


ROWS = 16
HOP = 3
BAND = 256
LANES = 128


class Line:
    def __init__(self, n, part, red, fin, sems, gap=0):
        self.n, self.part, self.red, self.fin, self.gap = n, part, red, fin, gap
        self.rs_send, self.rs_recv, self.bc_send, self.bc_recv = sems
        self.batch = part.shape[0] // 2
        self.pieces = self.batch // ROWS
        self.per = self.pieces // 2
        self.rank = lax.axis_index("mp")

    def pos(self, side):
        return self.rank if side == 0 else self.n - 1 - self.rank

    def fwd(self, side):
        return {"mp": self.rank + 1 if side == 0 else self.rank - 1}

    def bwd(self, side):
        return {"mp": self.rank - 1 if side == 0 else self.rank + 1}

    def rows(self, side, j):
        row = lax.div(j, self.per) * self.batch + side * (self.batch // 2) + lax.rem(j, self.per) * ROWS
        return pl.ds(pl.multiple_of(row, ROWS), ROWS)

    def turn(self, step, delay):
        raw = step - delay
        late = raw >= self.per + self.gap
        live = ((raw >= 0) & (raw < self.per)) | (late & (raw < self.pieces + self.gap))
        return jnp.where(late, raw - self.gap, raw), live

    def first(self, side, j):
        return pltpu.make_async_remote_copy(
            self.part.at[self.rows(side, j), :], self.red.at[side, j],
            self.rs_send.at[side, j], self.rs_recv.at[side, j], device_id=self.fwd(side))

    def onward(self, side, j):
        return pltpu.make_async_remote_copy(
            self.red.at[side, j], self.red.at[side, j],
            self.rs_send.at[side, j], self.rs_recv.at[side, j], device_id=self.fwd(side))

    def back(self, side, j):
        at = self.rows(side, j)
        return pltpu.make_async_remote_copy(
            self.fin.at[at, :], self.fin.at[at, :],
            self.bc_send.at[side, j], self.bc_recv.at[side, j], device_id=self.bwd(side))

    def greet(self, dp_others=(), mp_others=()):
        barrier = pltpu.get_barrier_semaphore()
        more = len(dp_others) + len(mp_others)
        for other in dp_others:
            pl.semaphore_signal(barrier, inc=1, device_id={"dp": other})
        for other in mp_others:
            pl.semaphore_signal(barrier, inc=1, device_id={"mp": other})
        if mp_others:
            pl.semaphore_wait(barrier, more)
            return

        @pl.when(self.rank > 0)
        def _():
            pl.semaphore_signal(barrier, inc=1, device_id={"mp": self.rank - 1})

        @pl.when(self.rank < self.n - 1)
        def _():
            pl.semaphore_signal(barrier, inc=1, device_id={"mp": self.rank + 1})

        @pl.when((self.rank > 0) & (self.rank < self.n - 1))
        def _():
            pl.semaphore_wait(barrier, 2 + more)

        @pl.when((self.rank == 0) | (self.rank == self.n - 1))
        def _():
            pl.semaphore_wait(barrier, 1 + more)

    def total(self, side, j):
        own = self.part[self.rows(side, j), :]
        return (self.red[side, j].astype(f32) + own.astype(f32)).astype(bf16)

    def run(self, finish, beside=None, least=0, ready=None):
        n = self.n

        def done(side, j):
            at = self.rows(side, j)
            finish(self.fin[at, :].astype(f32), at)

        @pl.loop(0, max(self.pieces + self.gap + 2 * HOP * (n - 1), least))
        def _(step):
            for side in (0, 1):
                pos = self.pos(side)
                j, live = self.turn(step, HOP * pos)

                @pl.when(live)
                def _(side=side, pos=pos, j=j):
                    @pl.when(pos == 0)
                    def _():
                        self.first(side, j).start()

                    @pl.when(pos > 0)
                    def _():
                        self.onward(side, j).wait_recv()

                    @pl.when((pos > 0) & (pos < n - 1))
                    def _():
                        self.red[side, j] = self.total(side, j)
                        self.onward(side, j).start()

                    @pl.when(pos == n - 1)
                    def _():
                        self.fin[self.rows(side, j), :] = self.total(side, j)
                        self.back(side, j).start()
                        done(side, j)

            for side in (0, 1):
                pos = self.pos(side)
                j, live = self.turn(step, HOP * (n - 1) + HOP * (n - 1 - pos))

                @pl.when(live & (pos < n - 1))
                def _(side=side, pos=pos, j=j):
                    self.back(side, j).wait_recv()

                    @pl.when(pos > 0)
                    def _():
                        self.back(side, j).start()

                    done(side, j)

            if ready is not None:
                @pl.when(step == max(0, HOP * (n - 1) - 2))
                def _():
                    ready()

            if beside is not None:
                beside(step)

        @pl.loop(0, self.pieces)
        def _(j):
            for side in (0, 1):
                pos = self.pos(side)

                @pl.when(pos < n - 1)
                def _(side=side):
                    self.onward(side, j).wait_send()

                @pl.when(pos > 0)
                def _(side=side):
                    self.back(side, j).wait_send()


def norm_scale(values):
    return lax.rsqrt(jnp.mean(values * values, axis=-1, keepdims=True) + 1e-06)


def norm_back_rows(u, gain, grad, sums=None, at=None):
    scale = norm_scale(u)
    unit = u * scale
    if sums is not None:
        sums[pl.ds(lax.div(at.start, ROWS), 1), :] = jnp.sum(grad * unit, axis=0, keepdims=True)
    scaled = grad * gain
    return scale * (scaled - unit * jnp.mean(scaled * unit, axis=-1, keepdims=True))


class FeedForward:
    def __init__(self, refs, begin, batch, arrive=None):
        self.arrive = arrive or self.wait_loads
        (self.normed, self.cot, self.gu_hbm, self.down_hbm, self.act_hbm, self.dgu_hbm, self.down_out, self.part_two,
         self.act, self.dgu, self.down_part, self.gu, self.down, self.sems) = refs
        self.begin, self.batch = begin, batch
        self.count = self.act.shape[0]
        self.hidden = self.down.shape[1]
        self.full, self.rest = divmod(self.hidden, BAND)
        self.bands = self.full + (self.rest > 0)
        self.units = self.bands + self.gu.shape[0] // BAND
        self.end = begin + self.units

    def loads(self):
        return [pltpu.make_async_copy(self.gu_hbm, self.gu, self.sems.at[0]),
                pltpu.make_async_copy(self.down_hbm, self.down, self.sems.at[1])]

    def stores(self):
        at = pl.ds(self.batch * self.count, self.count)
        return [pltpu.make_async_copy(self.act, self.act_hbm.at[at, :], self.sems.at[2]),
                pltpu.make_async_copy(self.dgu, self.dgu_hbm.at[at, :], self.sems.at[3]),
                pltpu.make_async_copy(self.down_part, self.down_out.at[at, :], self.sems.at[4])]

    def start(self):
        for load in self.loads():
            load.start()

    def wait_loads(self):
        for load in self.loads():
            load.wait()

    def finish(self):
        for store in self.stores():
            store.start()
        for store in self.stores():
            store.wait()

    def band(self, start, size):
        one = pl.ds(pl.multiple_of(start, LANES), size)
        two = pl.ds(pl.multiple_of(self.hidden + start, LANES), size)
        gate = lax.dot_general(self.normed[...], self.gu[:, one], NN, preferred_element_type=f32)
        up = lax.dot_general(self.normed[...], self.gu[:, two], NN, preferred_element_type=f32)
        grad = lax.dot_general(self.cot[...], self.down[:, one], NN, preferred_element_type=f32)
        sig = sigmoid(gate)
        swish = gate * sig
        self.act[:, one] = (swish * up).astype(bf16)
        self.dgu[:, one] = (grad * up * sig * (1.0 + gate * (1.0 - sig))).astype(bf16)
        self.dgu[:, two] = (grad * swish).astype(bf16)

    def step(self, step):
        at = step - self.begin
        mine = pl.ds(self.batch * self.count, self.count)

        @pl.when(at == 0)
        def _():
            self.arrive()

        @pl.when((at >= 0) & (at < self.full))
        def _():
            self.band(at * BAND, BAND)

        if self.rest:
            @pl.when(at == self.full)
            def _():
                self.band(self.full * BAND, self.rest)

        @pl.when((at >= self.bands) & (at < self.units))
        def _():
            out = pl.ds(pl.multiple_of((at - self.bands) * BAND, BAND), BAND)
            self.part_two[mine, out] = lax.dot_general(
                self.dgu[...], self.gu[out, :], NT, preferred_element_type=f32).astype(bf16)
            self.down_part[:, out] = lax.dot_general(
                self.act[...], self.down[out, :], NT, preferred_element_type=f32).astype(bf16)


class Gather:
    KINDS = ("own1", "own2", "own0", "one0", "one2", "two0", "two1", "both0a", "both0b")

    def __init__(self, refs):
        self.shards, self.full, self.send, self.recv, self.local = refs[:2], refs[2:4], *refs[4:]
        self.me = lax.axis_index("dp")
        self.count = self.shards[0].shape[0]

    def flip(self, device, bit):
        size = 1 << bit
        return device + size - 2 * size * lax.rem(lax.div(device, size), 2)

    def plan(self, kind, sender):
        one, two = self.flip(sender, 1), self.flip(sender, 2)
        both = self.flip(one, 2)
        return {"own1": (1, sender, 2), "own2": (2, sender, 2), "own0": (0, sender, 2),
                "one0": (0, one, 2), "one2": (2, one, 0), "two0": (0, two, 2), "two1": (1, two, 1),
                "both0a": (0, both, 0), "both0b": (0, both, 1)}[kind]

    def copy(self, kind, array, sending):
        k = self.KINDS.index(kind)
        bit = self.plan(kind, self.me)[0]
        other = self.flip(self.me, bit)
        _, owner, half = self.plan(kind, self.me if sending else other)
        size = self.count if half == 2 else self.count // 2
        start = owner * self.count + (size if half == 1 else 0)
        spot = self.full[array].at[pl.ds(pl.multiple_of(start, size), size), :]
        source = self.shards[array] if sending and kind.startswith("own") else spot
        return pltpu.make_async_remote_copy(
            source, spot, self.send.at[k, array], self.recv.at[k, array], device_id={"dp": other})

    def own(self, array):
        spot = pl.ds(pl.multiple_of(self.me * self.count, self.count), self.count)
        return pltpu.make_async_copy(self.shards[array], self.full[array].at[spot, :], self.local.at[array])

    def partners(self):
        return [self.flip(self.me, bit) for bit in (0, 1, 2)]

    def go(self, *kinds):
        for kind in kinds:
            for array in (0, 1):
                self.copy(kind, array, True).start()

    def come(self, *kinds):
        for kind in kinds:
            for array in (0, 1):
                self.copy(kind, array, False).wait_recv()

    def start(self):
        for array in (0, 1):
            self.own(array).start()
        self.go("own1", "own2", "own0")

    def turn(self):
        self.come("own1", "own2")
        self.go("one2", "two1", "one0", "two0")

    def cross(self):
        self.come("one2", "two1")
        self.go("both0a", "both0b")

    def end(self):
        self.come("own0", "one0", "two0", "both0a", "both0b")
        for array in (0, 1):
            self.own(array).wait()

    def sent(self):
        for kind in self.KINDS:
            for array in (0, 1):
                self.copy(kind, array, True).wait_send()


def kernel_hidden(n, part, x_in, gain, attn, normed, red, fin, rs_send, rs_recv, bc_send, bc_recv, sem, ready=None):
    line = Line(n, part, red, fin, (rs_send, rs_recv, bc_send, bc_recv))
    line.greet()

    def finish(total, at):
        h = x_in[at, :].astype(f32) + total
        normed[at, :] = (h * norm_scale(h) * gain[0:1, :]).astype(bf16)

    line.run(finish, ready=ready)
    keep = pltpu.make_async_copy(fin, attn, sem)
    keep.start()
    keep.wait()


TURN, CROSS, BEGIN = 22, 33, 38


def kernel_hidden_ffn(n, part, x_in, gain, cot, gu_shard, down_shard,
                      attn, normed, part_two, act_hbm, dgu_hbm, down_out, gu_hbm, down_hbm,
                      red, fin, rs_send, rs_recv, bc_send, bc_recv, sem, act, dgu, down_part, gu, down, sems,
                      g_send, g_recv, g_local, ready=None):
    line = Line(n, part, red, fin, (rs_send, rs_recv, bc_send, bc_recv))
    half = pl.ds(0, line.batch)
    gather = Gather((gu_shard, down_shard, gu, down, g_send, g_recv, g_local))
    keeps = [pltpu.make_async_copy(gu, gu_hbm, sems.at[0]), pltpu.make_async_copy(down, down_hbm, sems.at[1])]

    def arrive():
        gather.end()
        for keep in keeps:
            keep.start()

    begin = max(BEGIN, line.per + 2 * HOP * (n - 1))
    ffn = FeedForward((normed.at[half, :], cot.at[half, :], gu_hbm, down_hbm, act_hbm, dgu_hbm, down_out, part_two,
                       act, dgu, down_part, gu, down, sems), begin, 0, arrive)
    line.greet(gather.partners())
    gather.start()

    def finish(total, at):
        h = x_in[at, :].astype(f32) + total
        normed[at, :] = (h * norm_scale(h) * gain[0:1, :]).astype(bf16)

    def beside(step):
        @pl.when(step == TURN)
        def _():
            gather.turn()

        @pl.when(step == CROSS)
        def _():
            gather.cross()

        ffn.step(step)

    line.run(finish, beside, ffn.end, ready)
    last = pltpu.make_async_copy(fin, attn, sem)
    last.start()
    ffn.finish()
    gather.sent()
    for keep in keeps:
        keep.wait()
    last.wait()


def kernel_dhidden(n, part, x_in, attn, cot, gain, total_out, dattn, dgain,
                   red, fin, rs_send, rs_recv, bc_send, bc_recv, sem, sums, ready=None):
    line = Line(n, part, red, fin, (rs_send, rs_recv, bc_send, bc_recv))
    line.greet()

    def finish(total, at):
        h = x_in[at, :].astype(f32) + attn[at, :].astype(f32)
        dh = cot[at, :].astype(f32) + norm_back_rows(h, gain[0:1, :], total, sums, at)
        dattn[at, :] = dh.astype(bf16)

    line.run(finish, ready=ready)
    keep = pltpu.make_async_copy(fin, total_out, sem)
    keep.start()
    dgain[0:1, :] = jnp.sum(sums[...], axis=0, keepdims=True)
    keep.wait()


def kernel_dhidden_ffn(n, two_a, x_in, attn, cot, gain, normed_hbm, gu_hbm, down_hbm, act_in, dgu_in, down_in,
                       total_out, dattn, dgain, act_hbm, dgu_hbm, down_out,
                       red, fin, rs_send, rs_recv, bc_send, bc_recv, sem, sums,
                       part, normed, more, act, dgu, down_part, gu, down, sems, ready=None):
    line = Line(n, part, red, fin, (rs_send, rs_recv, bc_send, bc_recv))
    half = line.batch
    ffn = FeedForward((normed, cot.at[pl.ds(half, half), :], gu_hbm, down_hbm, act_hbm, dgu_hbm, down_out, part,
                       act, dgu, down_part, gu, down, sems), 1, 1)
    line.gap = max(0, ffn.end - line.per)
    brought = [pltpu.make_async_copy(two_a, part.at[pl.ds(0, half), :], more.at[0]),
               pltpu.make_async_copy(normed_hbm.at[pl.ds(half, half), :], normed, more.at[1])]
    for load in brought:
        load.start()
    ffn.start()
    line.greet()
    for load in brought:
        load.wait()

    def finish(total, at):
        h = x_in[at, :].astype(f32) + attn[at, :].astype(f32)
        dh = cot[at, :].astype(f32) + norm_back_rows(h, gain[0:1, :], total, sums, at)
        dattn[at, :] = dh.astype(bf16)

    line.run(finish, ffn.step, ffn.end, ready)
    keep = pltpu.make_async_copy(fin, total_out, sem)
    keep.start()
    dgain[0:1, :] = jnp.sum(sums[...], axis=0, keepdims=True)
    ffn.finish()
    keep.wait()


def kernel_dinput(dp, n, part, x_in, attn, cot, total_two, gain_one, gain_two, dgain_two, dgate, dinput, dgains,
                  red, fin, rs_send, rs_recv, bc_send, bc_recv, sem, sums,
                  src, dst, g_send, g_recv, gates, m_send, m_recv, ready=None):
    line = Line(n, part, red, fin, (rs_send, rs_recv, bc_send, bc_recv))
    me = lax.axis_index("dp")
    rank = line.rank
    others = [lax.rem(me + i, dp) for i in range(dp)]
    ranks = [lax.rem(rank + i, n) for i in range(n)]
    line.greet(others[1:], ranks[1:])

    def mp_swap(i):
        return pltpu.make_async_remote_copy(
            dgate, gates.at[rank], m_send.at[i], m_recv.at[i], device_id={"mp": ranks[i]})

    for i in range(1, n):
        mp_swap(i).start()
    gates[rank] = dgate[...]

    def finish(total, at):
        x = x_in[at, :].astype(f32)
        h = x + attn[at, :].astype(f32)
        dh = cot[at, :].astype(f32) + norm_back_rows(h, gain_two[0:1, :], total_two[at, :].astype(f32))
        dinput[at, :] = dh + norm_back_rows(x, gain_one[0:1, :], total, sums, at)

    line.run(finish, ready=ready)
    for i in range(1, n):
        mp_swap(i).wait()
    gate = gates[0]
    for r in range(1, n):
        gate = gate + gates[r]
    cols, val = dgain_two.shape[1] // dp, dgate.shape[1]
    one = jnp.sum(sums[...], axis=0, keepdims=True)
    for p in range(dp):
        src[p, 0:1, :cols] = one[:, p * cols : (p + 1) * cols]
        src[p, 1:2, :cols] = dgain_two[0:1, p * cols : (p + 1) * cols]
        src[p, 2:3, :val] = gate[0:1, :]

    def swap(i):
        return pltpu.make_async_remote_copy(
            src.at[others[i]], dst.at[me], g_send.at[i], g_recv.at[i], device_id={"dp": others[i]})

    for i in range(1, dp):
        swap(i).start()
    dst[me] = src[me]
    for i in range(1, dp):
        swap(i).wait()
    total = dst[0]
    for p in range(1, dp):
        total = total + dst[p]
    dgains[...] = total


def with_late(kernel, late, n, *refs):
    refs, count = list(refs), len(late)
    spaces, sems = refs[-1 - count : -1], refs[-1]
    refs = refs[: -1 - count]
    loads = [pltpu.make_async_copy(refs[at], space, sems.at[i]) for i, (at, space) in enumerate(zip(late, spaces))]
    for at, space in zip(late, spaces):
        refs[at] = space
    for load in loads:
        load.start()

    def ready():
        for load in loads:
            load.wait()

    kernel(n, *refs, ready=ready)


def line_call(kernel, cid, name, n, ins, outs, extra=(), away_in=(), away_out=(), aliases=None, sums=True, micros=100, late=()):
    tokens, width = outs[0].shape
    pieces = tokens // 2 // ROWS
    vmem = pl.BlockSpec(memory_space=pltpu.VMEM)
    far = pl.BlockSpec(memory_space=pl.ANY)
    if late:
        kernel = partial(with_late, kernel, late)
        extra = list(extra) + [pltpu.VMEM(ins[i].shape, ins[i].dtype) for i in late]
        extra.append(pltpu.SemaphoreType.DMA((len(late),)))
    return pl.pallas_call(
        partial(kernel, n),
        in_specs=[far if i in away_in or i in late else vmem for i in range(len(ins))],
        out_specs=[far if i in away_out else vmem for i in range(len(outs))],
        out_shape=outs,
        scratch_shapes=[pltpu.VMEM((2, pieces, ROWS, width), bf16), pltpu.VMEM((tokens, width), bf16)]
        + [pltpu.SemaphoreType.DMA((2, pieces))] * 4
        + [pltpu.SemaphoreType.DMA]
        + ([pltpu.VMEM((tokens // ROWS, width), f32)] if sums else [])
        + list(extra),
        input_output_aliases=aliases or {},
        compiler_params=pltpu.CompilerParams(
            collective_id=cid, has_side_effects=True, vmem_limit_bytes=VLIM),
        cost_estimate=cost(micros),
        name=name,
    )(*ins)


def from_behind(value, axis, by):
    length = lax.axis_size(axis)
    pairs = [(i, i + by) for i in range(length) if 0 <= i + by < length]
    return lax.ppermute(value, axis, pairs)


def norm_rows(values, gain):
    return values * lax.rsqrt(jnp.mean(values * values, axis=-1, keepdims=True) + 1e-06) * gain


def feed_forward(normed, cot, gu, down):
    units = down.shape[1]
    gate_up = dot(normed, gu)
    gate, up = gate_up[:, :units], gate_up[:, units:]
    sig = jax.nn.sigmoid(gate)
    act = low(gate * sig * up)
    grad = dot(cot, down)
    dgate = grad * up * sig * (1.0 + gate * (1.0 - sig))
    dgu = low(jnp.concatenate([dgate, grad * gate * sig], axis=1))
    return (act, dgu, dot(dgu, gu, NT, bf16), dot(act, down, NT, bf16))


class HalvingSum:
    def __init__(self, value, axis):
        self.value, self.axis = value, axis
        self.n, self.rank = lax.axis_size(axis), lax.axis_index(axis)
        bits = [1 << i for i in range(self.n.bit_length() - 1)]
        self.todo = [(self.halve, b) for b in bits] + [(self.double, b) for b in reversed(bits)]

    def swap(self, value, bit):
        return lax.ppermute(value, self.axis, [(i, i ^ bit) for i in range(self.n)])

    def halve(self, bit):
        half = self.value.shape[0] // 2
        up = (self.rank & bit) // bit
        kept = lax.dynamic_slice_in_dim(self.value, up * half, half)
        got = self.swap(lax.dynamic_slice_in_dim(self.value, (1 - up) * half, half), bit)
        self.value = (kept.astype(f32) + got.astype(f32)).astype(bf16)

    def double(self, bit):
        up = (self.rank & bit) != 0
        got = self.swap(self.value, bit)
        self.value = jnp.concatenate([jnp.where(up, got, self.value), jnp.where(up, self.value, got)])

    def step(self):
        if self.todo:
            act, bit = self.todo.pop(0)
            act(bit)

    def tie(self, *others):
        self.value, *others = lax.optimization_barrier((self.value, *others))
        return others


def low(x):
    return x.astype(bf16)


def dot(a, b, dims=NN, out=f32):
    return lax.dot_general(a, b, dims, preferred_element_type=out)


adam_step = 10.0


def rowwise(value):
    return with_layout_constraint(value, Layout(major_to_minor=tuple(range(value.ndim))))


def adamw(weight, grad, first, second, rate, shrink):
    grad = grad.astype(f32)
    first = 0.9 * first + 0.1 * grad
    second = 0.999 * second + 0.001 * grad * grad
    first_hat = first / (1.0 - 0.9**adam_step)
    second_hat = second / (1.0 - 0.999**adam_step)
    weight = weight - rate * (first_hat / (jnp.sqrt(second_hat) + 1e-08) + shrink * weight)
    return [weight, first, second]


def on_device(tokens_in, cotangent, segment_ids, pad_mask, *state):
    masters, firsts, seconds = state[0::3], state[1::3], state[2::3]
    (qk_proj, vg_proj, ab_proj, out_proj, gu_proj, down_proj,
     norm_gains, qk_conv, v_conv, out_gain, decay_params) = masters
    tokens = tokens_in.shape[0]
    dp = lax.axis_size("dp")
    mine = lax.axis_index("dp")
    start = mine * tokens
    rows = qk_proj.shape[0]
    heads, key, val = qk_proj.shape[2], qk_proj.shape[3], vg_proj.shape[3]
    units = gu_proj.shape[2]
    hk, hv = heads * key, heads * val
    mixer = Mixer(tokens, heads, key, val)

    small = [norm_gains, qk_conv, v_conv, out_gain]
    flat = jnp.concatenate([low(x).reshape(-1) for x in small])
    small_cols = pl.cdiv(flat.shape[0], rows)
    room = 128 - 2 * heads - small_cols
    flat = jnp.pad(flat, (0, rows * small_cols - flat.shape[0])).reshape(rows, small_cols)
    extra = jnp.concatenate(
        [low(ab_proj).reshape(rows, 2 * heads), flat, jnp.zeros((rows, room), bf16)], axis=1
    )
    vg_low = low(vg_proj)
    shard_one = jnp.concatenate(
        [low(qk_proj).reshape(rows, 2 * hk), vg_low[:, 0].reshape(rows, hv), extra], axis=1
    )
    shard_two = jnp.concatenate(
        [vg_low[:, 1].reshape(rows, hv), low(out_proj).reshape(hv, rows).T], axis=1
    )
    fused = units % LANES == 0 and dp == 8
    shard_gu = low(gu_proj).reshape(rows, 2 * units)
    shard_down = low(down_proj).T

    def gather(x):
        return lax.all_gather(x, "dp", axis=0, tiled=True)

    def scatter(value):
        return lax.psum_scatter(value, "dp", scatter_dimension=0, tiled=True)

    full_one = gather(shard_one)
    full_two = gather(shard_two)

    cut = 2 * hk + hv
    flats = full_one[:, cut + 2 * heads : cut + 2 * heads + small_cols].reshape(dp, rows * small_cols)
    parts, at = [], 0
    for x in small:
        size = x.size
        parts.append(flats[:, at : at + size].reshape((dp,) + x.shape).astype(f32))
        at += size
    gains = jnp.moveaxis(parts[0], 0, 1).reshape(2, -1)
    taps_qk = jnp.moveaxis(parts[1], 0, 3).reshape(2, CONV, hk)
    taps_qk = jnp.moveaxis(taps_qk, 0, 1).reshape(CONV, 2 * hk)
    taps_v = jnp.moveaxis(parts[2], 0, 2).reshape(CONV, hv)
    gain = jnp.broadcast_to(parts[3].reshape(1, val), (8, val))
    decay_low = lax.optimization_barrier(low(decay_params)).astype(f32)

    padded_ids = jnp.concatenate([jnp.full((4,), -1, jnp.int32), segment_ids])
    here_ids = lax.dynamic_slice_in_dim(padded_ids, start + 1, tokens + SPAN)
    prior_ids = lax.dynamic_slice_in_dim(padded_ids, start, tokens + SPAN)
    positions = start - SPAN + jnp.arange(tokens + SPAN, dtype=jnp.int32)
    resets_ext = ((here_ids != prior_ids) | (positions == 0)).astype(f32)
    resets_here = resets_ext[SPAN:]
    keep_ext = 1.0 - resets_ext
    valid_rows = [jnp.ones((tokens,), f32)]
    for lag in range(1, SPAN + 1):
        valid_rows.append(valid_rows[-1] * keep_ext[SPAN - lag + 1 : SPAN - lag + 1 + tokens])
    lag_valid = jnp.stack(valid_rows)
    pad = lax.dynamic_slice_in_dim(pad_mask, start, tokens).astype(f32)

    x_rim = from_behind(tokens_in[tokens - HALO :], "dp", 1)
    x = tokens_in.astype(f32)
    normed = low(norm_rows(x, gains[0]))
    normed_rim = low(norm_rows(x_rim.astype(f32), gains[0]))
    pre_qk = dot(normed, full_one[:, : 2 * hk], out=bf16)
    pre_v = dot(normed, full_one[:, 2 * hk : cut], out=bf16)
    mixed = dot(normed, full_one[:, cut:])[:, : 2 * heads].reshape(tokens, 2, heads)
    rim = low(dot(normed_rim, full_one[:, :cut])).astype(f32)
    (g, b), pull_gates = jax.vjp(lambda ab, dec: gates_of(ab, dec, pad), mixed, decay_low)
    aux, rowform = token_tables(g, b, pad, lag_valid, resets_here)

    rim_qk, rim_v = rim[:, : 2 * hk], rim[:, 2 * hk :]
    q, k, w, u, p, inv, r, r_end = mixer.forward_local(
        pre_qk, pre_v, rim_qk, rim_v, taps_qk, taps_v, aux, rowform
    )
    spot = mine.astype(jnp.int32).reshape(1)
    r_end, full_two = lax.optimization_barrier((low(r_end), full_two))
    gate_pre = dot(normed, full_two[:, :hv])
    maps = lax.all_gather(r_end, "dp")
    maps, gate_pre = lax.optimization_barrier((maps, gate_pre))
    y, st, vn, o = mixer.output(spot, maps, r, w, u, p, q, aux, gate_pre, gain)

    out_t = full_two[:, hv:]
    mp = lax.axis_size("mp")
    gain_one, gain_two = (jnp.broadcast_to(gains[i : i + 1], (8, gains.shape[1])) for i in (0, 1))
    half, width = tokens // 2, tokens_in.shape[1]
    like = sds((tokens, width), bf16)
    like_gain = sds(gain_two.shape)
    part_one = dot(y, out_t, NT, bf16)
    if fused:
        ffn_full = [sds((tokens, units), bf16), sds((tokens, 2 * units), bf16), like]
        ffn_weights = [sds((dp * rows, 2 * units), bf16), sds((dp * rows, units), bf16)]
        ffn_room = [pltpu.VMEM((half, units), bf16), pltpu.VMEM((half, 2 * units), bf16), pltpu.VMEM((half, width), bf16),
                    *[pltpu.VMEM(w.shape, bf16) for w in ffn_weights], pltpu.SemaphoreType.DMA((5,))]
        swaps = (len(Gather.KINDS), 2)
        attn, normed_two, two_a, act, dgu, down_part, full_gu, full_down = line_call(
            kernel_hidden_ffn, 0, "sum_hidden", mp,
            [part_one, tokens_in, gain_two, cotangent, shard_gu, shard_down],
            [like, like, sds((half, width), bf16)] + ffn_full + ffn_weights,
            ffn_room + [pltpu.SemaphoreType.DMA(swaps)] * 2 + [pltpu.SemaphoreType.DMA((2,))],
            away_in=(4, 5), away_out=(0, 3, 4, 5, 6, 7), sums=False, micros=120, late=(1, 3)
        )
        total_two, dattn, dgain_two, act, dgu, down_part = line_call(
            kernel_dhidden_ffn, 1, "sum_dhidden", mp,
            [two_a, tokens_in, attn, cotangent, gain_two, normed_two, full_gu, full_down, act, dgu, down_part],
            [like, like, like_gain] + ffn_full,
            [pltpu.VMEM((tokens, width), bf16), pltpu.VMEM((half, width), bf16), pltpu.SemaphoreType.DMA((2,))] + ffn_room,
            away_in=(0, 5, 6, 7, 8, 9, 10), away_out=(0, 3, 4, 5), aliases={8: 3, 9: 4, 10: 5}, micros=120, late=(1, 2)
        )
    else:
        full_gu, full_down = gather(shard_gu), gather(shard_down)
        attn, normed_two = line_call(
            kernel_hidden, 0, "sum_hidden", mp, [part_one, tokens_in, gain_two], [like, like],
            away_out=(0,), sums=False
        )
        act, dgu, two, down_part = feed_forward(normed_two, cotangent, full_gu, full_down)
        total_two, dattn, dgain_two = line_call(
            kernel_dhidden, 1, "sum_dhidden", mp, [two, tokens_in, attn, cotangent, gain_two],
            [like, like, like_gain], away_out=(0,)
        )
    down_sum = HalvingSum(down_part, "mp")
    (dattn,) = down_sum.tie(dattn)
    down_sum.step()
    dy = dot(dattn, out_t)
    grad_out = dot(dattn, y, TN, bf16)
    do, dgate, dgain, z, z_end = mixer.backward_local(dy, o, gate_pre, gain, aux, q, k, w, p)
    z_end, act, dgu = down_sum.tie(low(z_end), act, dgu)
    down_sum.step()
    grad_gu = dot(normed_two, dgu, TN, bf16)
    grad_down = dot(cotangent, act, TN, bf16)
    back_maps = lax.all_gather(z_end, "dp")
    grad_gate_w = dot(normed, dgate, TN, bf16)
    grad_two = jnp.concatenate([grad_gate_w, grad_out], axis=1)
    back_maps, grad_two, grad_gu, grad_down = down_sum.tie(back_maps, grad_two, grad_gu, grad_down)
    down_sum.step()
    red_gu = scatter(grad_gu)
    red_down = scatter(grad_down)
    red_two = scatter(grad_two)
    (dqk, dv, tail_qk, tail_v, head_qk, head_v, dtaps_qk, dtaps_v, dcg, dbeta) = mixer.backward(
        spot, back_maps, z, do, st, vn, q, k, w, u, p, inv, aux, rowform,
        pre_qk, pre_v, rim_qk, rim_v, taps_qk, taps_v
    )
    dqk, dv, head_qk, head_v = down_sum.tie(dqk, dv, head_qk, head_v)
    down_sum.step()
    heads_back = from_behind(jnp.concatenate([head_qk, head_v], axis=1), "dp", -1)
    dqk = lax.dynamic_update_slice(dqk, low(tail_qk + heads_back[:, : 2 * hk]), (tokens - HALO, 0))
    dv = lax.dynamic_update_slice(dv, low(tail_v + heads_back[:, 2 * hk :]), (tokens - HALO, 0))
    dmixed, ddecay = pull_gates((in_chunks(dcg, True), dbeta))
    dab = jnp.pad(low(dmixed.reshape(tokens, 2 * heads)), ((0, 0), (0, 128 - 2 * heads)))
    dpre = jnp.concatenate([dqk, dv, dab], axis=1)
    grad_one = dot(normed, dpre, TN, bf16)
    grad_small = [
        dtaps_qk.reshape(CONV, 2, heads, dp, -1).transpose(1, 0, 2, 3, 4),
        dtaps_v.reshape(CONV, heads, dp, -1),
    ]
    grad_flat = jnp.concatenate(
        [jnp.moveaxis(gs, -2, 0).reshape(dp, -1) for gs in grad_small], axis=1
    )
    high = low(ddecay).astype(f32)
    pair = jnp.stack([high, ddecay - high]).reshape(1, 1, -1)
    slots = jnp.where(jnp.arange(dp)[None, :, None] == mine, pair, 0.0)
    slots = jnp.broadcast_to(slots, (dp,) + slots.shape[1:]).reshape(dp, -1)
    used = grad_flat.shape[1]
    grad_flat = jnp.concatenate([grad_flat, slots], axis=1)
    grad_flat = jnp.pad(grad_flat, ((0, 0), (0, rows * small_cols - grad_flat.shape[1])))
    grad_flat = low(grad_flat).reshape(dp * rows, small_cols)
    grad_one = lax.dynamic_update_slice(grad_one, grad_flat, (0, cut + 2 * heads))
    grad_one, dpre = lax.optimization_barrier((grad_one, dpre))
    red_one = scatter(grad_one)
    normed_part = low(dot(dpre, full_one, NT) + dot(dgate, full_two[:, :hv], NT))
    while down_sum.todo:
        down_sum.step()
    (normed_part,) = down_sum.tie(normed_part)
    block_out = low(x + attn.astype(f32) + down_sum.value.astype(f32))
    swap = (8, max(rows, val))
    input_grad, dgains = line_call(
        partial(kernel_dinput, dp), 2, "sum_dinput", mp,
        [normed_part, tokens_in, attn, cotangent, total_two, gain_one, gain_two, dgain_two, dgain],
        [sds((tokens, width)), sds(swap)],
        [pltpu.VMEM((dp,) + swap, f32)] * 2 + [pltpu.SemaphoreType.DMA((dp,))] * 2
        + [pltpu.VMEM((mp,) + dgain.shape, f32)] + [pltpu.SemaphoreType.DMA((mp,))] * 2, late=(1, 2, 3, 4),
    )
    red_flat = red_one[:, cut + 2 * heads : cut + 2 * heads + small_cols].astype(f32).reshape(-1)
    red_small, at = [dgains[:2, :rows]], 0
    for s in small[1:3]:
        red_small.append(red_flat[at : at + s.size].reshape(s.shape))
        at += s.size
    red_small.append(lax.dynamic_slice_in_dim(dgains[2], mine * out_gain.size, out_gain.size))
    slots = red_flat[used : used + slots.shape[1]].reshape((dp, 2) + ddecay.shape)
    grads = [
        red_one[:, : 2 * hk].reshape(qk_proj.shape),
        jnp.stack([red_one[:, 2 * hk : cut].reshape(rows, heads, val),
                   red_two[:, :hv].reshape(rows, heads, val)], axis=1),
        red_one[:, cut : cut + 2 * heads].reshape(ab_proj.shape),
        rowwise(red_two[:, hv:].T).reshape(out_proj.shape),
        rowwise(red_gu.reshape(gu_proj.shape)),
        rowwise(red_down.T),
    ] + red_small + [jnp.sum(slots, axis=(0, 1))]
    matrix_rate = 2.5 * D ** (-0.5)
    rates = [matrix_rate] * 6 + [0.5, 1.0, 1.0, 0.5, 2.0]
    shrinks = [0.1] * 6 + [0.0] * 5
    updates = []
    for i in range(11):
        updates += adamw(masters[i], grads[i], firsts[i], seconds[i], rates[i], shrinks[i])
    copies = [low(updates[3 * i]) for i in range(6)]
    return (block_out, input_grad, *updates, *copies)


def solution(mesh):
    weights = [
        P("dp", None, "mp", None),
        P("dp", None, "mp", None),
        P("dp", None, "mp"),
        P("mp", None, "dp"),
        P("dp", None, "mp"),
        P("mp", "dp"),
        P(None, "dp"),
        P(None, None, "mp", "dp"),
        P(None, "mp", "dp"),
        P("dp"),
        P(None, "mp"),
    ]
    thrice = tuple(w for w in weights for _ in range(3))
    rowwise = P("dp", None)
    return jax.shard_map(
        on_device,
        mesh=mesh,
        in_specs=(rowwise, rowwise, P(), P()) + thrice,
        out_specs=(rowwise, rowwise) + thrice + tuple(weights[:6]),
        check_vma=False,
    )
```
